512 devices in a mesh: slab: 32 (over x, y), pencil: 16 (over z, core).
Axes of the slice: x: 4, y: 8, z: 8, core: 2. Of those that a mesh axis runs over, the one named last changes fastest.
Arguments:
- surface_eta: float32 [2048, 4096], P('pencil', 'slab'), may hold values from -1.2 to 1.2
- surface_potential: float32 [2048, 4096], P('pencil', 'slab'), may hold values from -1.8 to 1.8
- velocity: float32 [3, 512, 256, 128], P(None, 'slab', 'pencil'), may hold values from -3 to 3
- send_point: int32 [32, 16, 32, 256], P('slab', 'pencil'), may hold values from 0 to 16383
- send_count: int32 [32, 16, 32], P('slab', 'pencil'), may hold values from 1 to 256, as said below
- stencil: int32 [4, 512, 256], P(None, 'slab', 'pencil'), may hold values from 0 to 8191, as said below
- interp_weight: float32 [4, 512, 256], P(None, 'slab', 'pencil'), may hold values from 0.2 to 1
Outputs:
- surface_vertical: float32 [2048, 4096], P('pencil', 'slab')
- velocity_next: float32 [3, 512, 256, 128], P(None, 'slab', 'pencil')
The draws below stay inside these ranges and needn't reach their ends.
Inputs may be any that keep to these rules, and one draw needn't show every extreme that they name: `send_count`: equals 256 toward the first and the last 2 slabs d, at most 64 toward the others. stencil[q, x, y] = r * 256 + j with j < send_count[r, y // 16, x // 16].
All inputs are finite; a program needn't handle non-finite values.
Results may differ from the reference program's by a relative error of at most 0.00015.
Values sent between devices are 32-bit elements; how exact they have to be, the bound alone decides.
No kernel may reach another device: no remote copies, remote signals or barrier semaphores. Data moves between devices by JAX's collectives and lax.ppermute only.
A program may use at most 128 MiB of HBM per device.

```python
import math
import jax
import jax.numpy as jnp
from jax import lax

NXW = 4096
NYW = 2048
CX = 16
CY = 16
CZ = 128
STEPS = 2
CAP = 256
Q = 4
NX = 512
NY = 256
TX = 128
TY = 128
ZONE = 2
N_SLAB = 32
N_PENCIL = 16


def count_table(key):
    count_key = jax.random.fold_in(key, 11)
    small_count = jax.random.randint(count_key, (N_SLAB, N_PENCIL, N_SLAB), 1, CAP // 4 + 1)
    target_slab = jnp.arange(N_SLAB, dtype=jnp.int32)
    in_zone = (target_slab < ZONE) | (target_slab >= N_SLAB - ZONE)
    return jnp.where(in_zone[None, None, :], CAP, small_count).astype(jnp.int32)


def draw_send_count(key, part):
    return count_table(key)


def draw_stencil(key, part):
    counts = count_table(key)
    source = jax.random.randint(jax.random.fold_in(key, 21), (Q, NX, NY), 0, N_SLAB)
    slab_of = (jnp.arange(NX, dtype=jnp.int32) // CX)[None, :, None]
    pencil_of = (jnp.arange(NY, dtype=jnp.int32) // CY)[None, None, :]
    slot_limit = counts[source, pencil_of, slab_of]
    slot_index = jax.random.randint(jax.random.fold_in(key, 22), (Q, NX, NY), 0, slot_limit)
    flat_index = source * CAP + slot_index
    flat_index = flat_index.at[0, 0, 0].set(N_SLAB * CAP - 1).at[1, 0, 0].set(0)
    return flat_index.astype(jnp.int32)


def plant(result, own_key, low, high):
    longest = result.shape.index(max(result.shape))
    spots = []
    for shift in (0, 1):
        where = [jax.random.randint(jax.random.fold_in(own_key, axis), (), 0, length) for axis, length in enumerate(result.shape)]
        where[longest] = (where[longest] + shift) % result.shape[longest]
        spots.append(tuple(where))
    return result.at[spots[0]].set(low).at[spots[1]].set(high)


def level_of(own_key, extent, cuts, smallest, largest):
    def one(position, shards_of):
        heights = jax.random.uniform(jax.random.fold_in(jax.random.fold_in(own_key, 6), position), (shards_of,), jnp.float32, smallest / len(cuts), largest / len(cuts))
        return jnp.repeat(jnp.exp(heights), extent[position] // shards_of).reshape((-1,) + (1,) * (len(extent) - position - 1))

    factor_of = one(*cuts[0])
    for cut in cuts[1:]:
        factor_of = factor_of * one(*cut)
    return factor_of


def gaussian(own_key, extent, spread, most, cuts=(), kind=jnp.bfloat16):
    array = spread * jax.random.normal(own_key, extent, jnp.float32)
    if cuts:
        array = array * level_of(own_key, extent, cuts, -0.22, 0.18)
    return jnp.clip(array, -most, most).astype(kind)


def setup_inputs(seed: int = 0) -> dict:
    key_list = jax.random.split(jax.random.key(seed), 8)
    return {
        "surface_eta": gaussian(key_list[0], (NYW, NXW), 0.2, 1.2, ((0, 16), (1, 32)), jnp.float32),
        "surface_potential": gaussian(key_list[1], (NYW, NXW), 0.3, 1.8, ((0, 16), (1, 32)), jnp.float32),
        "velocity": gaussian(key_list[2], (3, NX, NY, CZ), 0.5, 3.0, ((1, 32), (2, 16)), jnp.float32),
        "send_point": plant(jax.random.randint(key_list[3], (N_SLAB, N_PENCIL, N_SLAB, CAP), 0, TX * TY), jax.random.fold_in(key_list[3], 1), 0, (TX * TY) - 1).astype(jnp.int32),
        "send_count": draw_send_count(jax.random.fold_in(key_list[7], 71), 0),
        "stencil": draw_stencil(jax.random.fold_in(key_list[7], 71), 0),
        "interp_weight": jnp.clip(0.2 + 0.8 * jax.random.uniform(key_list[6], (Q, NX, NY), jnp.float32) ** level_of(key_list[6], (Q, NX, NY), ((1, 32), (2, 16)), -0.2, 0.2), 0.2, 1.0),
    }


TIME_STEP = 0.2
VISCOSITY = 0.6
DEPTH_RATE = 3.0

def hartley(values, axis):
    spectrum = jnp.fft.fft(values, axis=axis)
    return (spectrum.real - spectrum.imag).astype(jnp.float32)

def transform(values):
    return hartley(hartley(values, 1), 0)

def wavenumber(index, length):
    folded = jnp.minimum(index, length - index)
    return 2.0 * math.pi / length * folded.astype(jnp.float32)

def ramp_weight(distance, reach_len):
    ratio = jnp.clip(1.0 - distance / reach_len, 0.0, 1.0)
    return ratio * ratio

def blend_weight(pos_x, pos_y, total_x, total_y, reach_x, reach_y):
    along_x = jnp.maximum(ramp_weight(pos_x, reach_x), ramp_weight(total_x - 1.0 - pos_x, reach_x))
    across = jnp.maximum(ramp_weight(pos_y, reach_y), ramp_weight(total_y - 1.0 - pos_y, reach_y))
    return jnp.maximum(along_x[:, None], across[None, :])[:, :, None]

def advance(velocity, padded, relax_weight, target):
    shifted = jnp.pad(padded, ((0, 0), (0, 0), (0, 0), (1, 1)))
    components = []
    for component in range(3):
        current = shifted[component]
        plus_x = current[2:, 1:-1, 1:-1]
        minus_x = current[:-2, 1:-1, 1:-1]
        plus_y = current[1:-1, 2:, 1:-1]
        minus_y = current[1:-1, :-2, 1:-1]
        plus_z = current[1:-1, 1:-1, 2:]
        minus_z = current[1:-1, 1:-1, :-2]
        laplace = plus_x + minus_x + (plus_y + minus_y) + (plus_z + minus_z) - 6.0 * velocity[component]
        advect = velocity[0] * (plus_x - minus_x) + velocity[1] * (plus_y - minus_y) + velocity[2] * (plus_z - minus_z)
        predicted = velocity[component] + TIME_STEP * (VISCOSITY * laplace - 0.5 * advect)
        components.append((1.0 - relax_weight) * predicted + relax_weight * target[component])
    return jnp.stack(components)

def tile_view(field):
    return field.reshape(N_PENCIL, TY, N_SLAB, TX).transpose(2, 0, 1, 3).reshape(N_SLAB, N_PENCIL, TY * TX)

def reference(surface_eta, surface_potential, velocity, send_point, send_count, stencil, interp_weight):
    wave_y = wavenumber(jnp.arange(NYW, dtype=jnp.int32), NYW)[:, None]
    wave_x = wavenumber(jnp.arange(NXW, dtype=jnp.int32), NXW)[None, :]
    magnitude = jnp.sqrt(wave_x * wave_x + wave_y * wave_y)
    norm_scale = 1.0 / (NXW * NYW)
    first_mult = magnitude * norm_scale
    second_mult = magnitude * magnitude * norm_scale
    third_mult = magnitude * magnitude * magnitude * norm_scale
    height = surface_eta
    spectrum = transform(surface_potential)
    slope_one = transform(spectrum * first_mult)
    curve_one = transform(spectrum * second_mult)
    cubic_one = transform(spectrum * third_mult)
    potential_two = -height * slope_one
    spectrum = transform(potential_two)
    slope_two = transform(spectrum * first_mult)
    curve_two = transform(spectrum * second_mult)
    potential_three = -height * slope_two - 0.5 * height * height * curve_one
    spectrum = transform(potential_three)
    slope_three = transform(spectrum * first_mult)
    vertical = slope_one + slope_two + height * curve_one + slope_three + height * curve_two + 0.5 * height * height * cubic_one
    both_tiles = jnp.stack([tile_view(surface_eta), tile_view(vertical)])
    point_lists = send_point.reshape(N_SLAB, N_PENCIL, N_SLAB * CAP)
    sent = jnp.take_along_axis(both_tiles, point_lists[None], axis=3).reshape(2, N_SLAB, N_PENCIL, N_SLAB, CAP)
    live_mask = jnp.arange(CAP, dtype=jnp.int32)[None, None, None, :] < send_count[..., None]
    sent = jnp.where(live_mask[None], sent, 0.0)
    arrived = sent.transpose(0, 3, 2, 1, 4).reshape(2, N_SLAB * N_PENCIL * N_SLAB * CAP)
    slab_of = jnp.arange(NX, dtype=jnp.int32) // CX
    pencil_of = jnp.arange(NY, dtype=jnp.int32) // CY
    base_index = (slab_of[:, None] * N_PENCIL + pencil_of[None, :]) * (N_SLAB * CAP)
    sampled = arrived[:, base_index[None] + stencil]
    shares = interp_weight / lax.optimization_barrier(jnp.sum(interp_weight, axis=0))
    surface_at = lax.optimization_barrier(jnp.sum(sampled * shares[None], axis=1))
    pos_x = jnp.arange(NX, dtype=jnp.float32)
    pos_y = jnp.arange(NY, dtype=jnp.float32)
    relax_weight = blend_weight(pos_x, pos_y, float(NX), float(NY), float(ZONE * CX), float(CY))
    levels = jnp.arange(CZ, dtype=jnp.float32)
    depth_decay = jnp.exp(-DEPTH_RATE * (CZ - 1.0 - levels) / CZ)
    target = jnp.stack([surface_at[0][:, :, None] * depth_decay, jnp.zeros((NX, NY, CZ), jnp.float32), surface_at[1][:, :, None] * depth_decay])
    for substep in range(STEPS):
        padded = jnp.pad(velocity, ((0, 0), (1, 1), (1, 1), (0, 0)))
        velocity = advance(velocity, padded, relax_weight, target)
    return (vertical, velocity)
```

```python
import math

import jax
import jax.numpy as jnp
import numpy as np
from jax import lax
from jax.experimental import pallas as pl
from jax.experimental.pallas import tpu as pltpu
from jax.sharding import PartitionSpec as P

NXW = 4096
NYW = 2048
STEPS = 2
LANES = 128

TIME_STEP = 0.2
VISCOSITY = 0.6
DEPTH_RATE = 3.0


def stage_tables(peers):
    copies = LANES // peers
    length = peers * LANES
    outer = np.arange(peers)
    inner = np.arange(LANES)
    eye = np.eye(copies)
    angle_a = 2.0 * np.pi / peers * (outer[:, None] * outer[None, :] % peers)
    angle_t = 2.0 * np.pi / length * (outer[:, None] * inner[None, :] % length)
    angle_b = 2.0 * np.pi / LANES * (inner[:, None] * inner[None, :] % LANES)
    cos_a, sin_a = np.kron(np.cos(angle_a), eye), np.kron(np.sin(angle_a), eye)
    cos_b, sin_b = np.cos(angle_b), np.sin(angle_b)
    tables = {
        "fa": np.concatenate([cos_a, -sin_a], axis=0),
        "cos_t": np.repeat(np.cos(angle_t), copies, axis=0),
        "sin_t": np.repeat(np.sin(angle_t), copies, axis=0),
        "fb": np.concatenate([cos_b + sin_b, sin_b - cos_b], axis=0),
        "ib": np.concatenate([cos_b, -sin_b], axis=1),
        "ia": np.concatenate([cos_a + sin_a, sin_a - cos_a], axis=1),
    }
    return tables


TAB_Y = stage_tables(16)
TAB_X = stage_tables(32)


def pair_inverse_b(ib):
    rows = ib.reshape(32, 4, 2 * LANES)
    big = np.zeros((32, 2, 4, 2, 2 * LANES))
    for field in range(2):
        big[:, field, :, field, :] = rows
    return big.reshape(2 * LANES, 4 * LANES)


def pair_inverse_a(ia):
    rows = ia.reshape(32, 4, 2 * LANES)
    big = np.zeros((32, 2, 4, 2, 2 * LANES))
    for field in range(2):
        big[:, field, :, field, :] = rows
    return big.reshape(2 * LANES, 4 * LANES)


Y_IB_PAIR = pair_inverse_b(TAB_Y["ib"])
X_IA_PAIR = pair_inverse_a(TAB_X["ia"])


def f32(array):
    return jnp.asarray(np.asarray(array, np.float32))


def mm(left, right):
    return jnp.dot(
        left, right, precision=lax.Precision.HIGHEST, preferred_element_type=jnp.float32
    )


def twiddle(real, imag, cos_t, sin_t):
    return real * cos_t + imag * sin_t, imag * cos_t - real * sin_t


def forward(block, fa, cos_t, sin_t, fb):
    outer = mm(fa, block)
    real, imag = twiddle(outer[:LANES], outer[LANES:], cos_t, sin_t)
    return mm(jnp.concatenate([real, imag], axis=1), fb)


def run(body, outs, *args):
    shapes = [jax.ShapeDtypeStruct(shape, jnp.float32) for shape in outs]

    def kernel(*refs):
        results = body(*[ref[...] for ref in refs[: len(args)]])
        for ref, result in zip(refs[len(args) :], results, strict=True):
            ref[...] = result.reshape(ref.shape)

    return pl.pallas_call(kernel, out_shape=shapes)(*args)


def turn_inputs(eta, potential):
    eta_t = eta.T.reshape(16, 8, LANES)
    potential_t = potential.T.reshape(16, 8, LANES)
    return (jnp.concatenate([eta_t, potential_t], axis=1),)


def turn(block):
    return (block.reshape(-1, LANES).T,)


def first_y(both, fa, cos_t, sin_t, fb):
    eta = both[:, :8].reshape(LANES, LANES)
    potential = both[:, 8:].reshape(LANES, LANES)
    return forward(potential, fa, cos_t, sin_t, fb), eta


def x_stage(powers):
    def multiply(spec, kappa, power):
        factor = kappa
        for _ in range(power - 1):
            factor = factor * kappa
        return spec * (factor * (1.0 / (NXW * NYW)))

    def body(block, kappa, fa, cos_t, sin_t, fb, ib, ia_pair, *older):
        spec = forward(block.reshape(LANES, LANES), fa, cos_t, sin_t, fb)
        other = older[0] if older else spec
        pair = jnp.concatenate(
            [multiply(spec, kappa, powers[0]), multiply(other, kappa, powers[1])], axis=0
        )
        inner = mm(pair, ib)
        parts = []
        for field in range(2):
            rows = inner[field * LANES : (field + 1) * LANES]
            parts += twiddle(rows[:, :LANES], rows[:, LANES:], cos_t, sin_t)
        return mm(ia_pair, jnp.concatenate(parts, axis=0)), spec

    return body


def back_y(block, cos_t, sin_t, ib_pair, ia):
    inner = mm(block.reshape(LANES, 2 * LANES), ib_pair)
    reals, imags = [], []
    for field in range(2):
        part = inner[:, 2 * field * LANES : 2 * (field + 1) * LANES]
        real, imag = twiddle(part[:, :LANES], part[:, LANES:], cos_t, sin_t)
        reals.append(real)
        imags.append(imag)
    stacked = jnp.concatenate(
        [jnp.concatenate(reals, axis=1), jnp.concatenate(imags, axis=1)], axis=0
    )
    fields = mm(ia, stacked)
    return fields[:, :LANES], fields[:, LANES:]


def second_y(block, eta, fa, cos_t, sin_t, fb, ib_pair, ia):
    slope_one, cubic_one = back_y(block, cos_t, sin_t, ib_pair, ia)
    spectrum = forward(-eta * slope_one, fa, cos_t, sin_t, fb)
    return spectrum, slope_one, cubic_one


def third_y(block, eta, fa, cos_t, sin_t, fb, ib_pair, ia):
    slope_two, curve_one = back_y(block, cos_t, sin_t, ib_pair, ia)
    potential_three = -eta * slope_two - 0.5 * eta * eta * curve_one
    return forward(potential_three, fa, cos_t, sin_t, fb), slope_two, curve_one


def last_y(block, eta, slope_one, cubic_one, slope_two, curve_one, cos_t, sin_t, ib_pair, ia):
    slope_three, curve_two = back_y(block, cos_t, sin_t, ib_pair, ia)
    vertical = (
        slope_one
        + slope_two
        + eta * curve_one
        + slope_three
        + eta * curve_two
        + 0.5 * eta * eta * cubic_one
    )
    return (vertical,)


def swap(values, axis):
    return lax.all_to_all(values, axis, 0, 0, tiled=True)


def wave_surface(surface_eta, surface_potential):
    slab_index = lax.axis_index("slab")
    pencil_index = lax.axis_index("pencil")
    fwd_y = [f32(TAB_Y[key]) for key in ("fa", "cos_t", "sin_t", "fb")]
    both_y = fwd_y + [f32(Y_IB_PAIR), f32(TAB_Y["ia"])]
    inv_y = [f32(TAB_Y["cos_t"]), f32(TAB_Y["sin_t"]), f32(Y_IB_PAIR), f32(TAB_Y["ia"])]
    tab_x = [f32(TAB_X[key]) for key in ("fa", "cos_t", "sin_t", "fb", "ib")] + [f32(X_IA_PAIR)]
    square = (LANES, LANES)

    row = lax.broadcasted_iota(jnp.int32, square, 0)
    lane = lax.broadcasted_iota(jnp.int32, square, 1)
    index_x = row // 4 + 32 * lane
    index_y = pencil_index + 16 * (slab_index * 4 + row % 4)
    wave_x = wavenumber(index_x, NXW)
    wave_y = wavenumber(index_y, NYW)
    kappa = jnp.sqrt(wave_x * wave_x + wave_y * wave_y)

    def outward(block):
        (turned,) = run(turn, [square], swap(block.reshape(16, 8, LANES), "pencil"))
        return swap(turned.reshape(32, 4, LANES), "slab").reshape(square)

    def homeward(block):
        (turned,) = run(turn, [(LANES, 2 * LANES)], swap(block, "slab"))
        return swap(turned.reshape(16, 8, 2 * LANES), "pencil")

    pair = (32, 8, LANES)
    (turned,) = run(turn_inputs, [(16, 16, LANES)], surface_eta, surface_potential)
    spectrum, eta = run(first_y, [square, square], swap(turned, "pencil"), *fwd_y)
    block, spec_one = run(x_stage((1, 3)), [pair, square], outward(spectrum), kappa, *tab_x)
    spectrum, slope_one, cubic_one = run(second_y, [square] * 3, homeward(block), eta, *both_y)
    block, spec_two = run(
        x_stage((1, 2)), [pair, square], outward(spectrum), kappa, *tab_x, spec_one
    )
    spectrum, slope_two, curve_one = run(third_y, [square] * 3, homeward(block), eta, *both_y)
    block, _ = run(x_stage((1, 2)), [pair, square], outward(spectrum), kappa, *tab_x, spec_two)
    (vertical,) = run(
        last_y,
        [(16, 8, LANES)],
        homeward(block),
        eta,
        slope_one,
        cubic_one,
        slope_two,
        curve_one,
        *inv_y,
    )
    (tile,) = run(turn, [square], swap(vertical, "pencil"))
    return tile


def wavenumber(index, length):
    folded = jnp.minimum(index, length - index)
    return 2.0 * math.pi / length * folded.astype(jnp.float32)


def padded_2(shard, sides, width):
    for axis, dim in sides:
        size, length = (lax.axis_size(axis), shard.shape[dim])
        up = [(i, (i + 1) % size) for i in range(size - 1)]
        down = [(j, i) for i, j in up]
        last = lax.slice_in_dim(shard, length - width, length, axis=dim)
        leading = lax.slice_in_dim(shard, 0, width, axis=dim)
        before = lax.ppermute(last, axis, up)
        after = lax.ppermute(leading, axis, down)
        shard = jnp.concatenate([before, shard, after], axis=dim)
    return shard


def ramp_weight(distance, reach_len):
    ratio = jnp.clip(1.0 - distance / reach_len, 0.0, 1.0)
    return ratio * ratio


def blend_weight(pos_x, pos_y, total_x, total_y, reach_x, reach_y):
    along_x = jnp.maximum(ramp_weight(pos_x, reach_x), ramp_weight(total_x - 1.0 - pos_x, reach_x))
    across = jnp.maximum(ramp_weight(pos_y, reach_y), ramp_weight(total_y - 1.0 - pos_y, reach_y))
    return jnp.maximum(along_x[:, None], across[None, :])[:, :, None]


def advance(velocity, padded, relax_weight, target):
    shifted = jnp.pad(padded, ((0, 0), (0, 0), (0, 0), (1, 1)))
    components = []
    for component in range(3):
        current = shifted[component]
        plus_x = current[2:, 1:-1, 1:-1]
        minus_x = current[:-2, 1:-1, 1:-1]
        plus_y = current[1:-1, 2:, 1:-1]
        minus_y = current[1:-1, :-2, 1:-1]
        plus_z = current[1:-1, 1:-1, 2:]
        minus_z = current[1:-1, 1:-1, :-2]
        laplace = (
            plus_x + minus_x + (plus_y + minus_y) + (plus_z + minus_z) - 6.0 * velocity[component]
        )
        advect = (
            velocity[0] * (plus_x - minus_x)
            + velocity[1] * (plus_y - minus_y)
            + velocity[2] * (plus_z - minus_z)
        )
        predicted = velocity[component] + TIME_STEP * (VISCOSITY * laplace - 0.5 * advect)
        components.append((1.0 - relax_weight) * predicted + relax_weight * target[component])
    return jnp.stack(components)


def on_device(
    surface_eta, surface_potential, velocity, send_point, send_count, stencil, interp_weight
):
    slab_count = lax.axis_size("slab")
    pencil_count = lax.axis_size("pencil")
    slab_index = lax.axis_index("slab")
    pencil_index = lax.axis_index("pencil")
    tile_rows, tile_cols = surface_eta.shape
    vertical = wave_surface(surface_eta, surface_potential)
    point_lists = send_point[0, 0]
    counts = send_count[0, 0]
    capacity = point_lists.shape[1]
    values = jnp.stack([surface_eta, vertical]).reshape(2, tile_rows * tile_cols)
    picked = values[:, point_lists]
    live_mask = jnp.arange(capacity, dtype=jnp.int32)[None, :] < counts[:, None]
    picked = jnp.where(live_mask[None], picked, 0.0)
    arrived = lax.all_to_all(picked, "slab", split_axis=1, concat_axis=1, tiled=True).reshape(
        2, slab_count * capacity
    )
    sampled = arrived[:, stencil]
    shares = interp_weight / jnp.sum(interp_weight, axis=0)
    surface_at = jnp.sum(sampled * shares[None], axis=1)
    block_x = velocity.shape[1]
    block_y = velocity.shape[2]
    depth_cells = velocity.shape[3]
    zone_slabs = max(1, slab_count // 16)
    pos_x = (slab_index * block_x + jnp.arange(block_x, dtype=jnp.int32)).astype(jnp.float32)
    pos_y = (pencil_index * block_y + jnp.arange(block_y, dtype=jnp.int32)).astype(jnp.float32)
    relax_weight = blend_weight(
        pos_x,
        pos_y,
        float(block_x * slab_count),
        float(block_y * pencil_count),
        float(zone_slabs * block_x),
        float(block_y),
    )
    levels = jnp.arange(depth_cells, dtype=jnp.float32)
    depth_decay = jnp.exp(-DEPTH_RATE * (depth_cells - 1.0 - levels) / depth_cells)
    target = jnp.stack(
        [
            surface_at[0][:, :, None] * depth_decay,
            jnp.zeros((block_x, block_y, depth_cells), jnp.float32),
            surface_at[1][:, :, None] * depth_decay,
        ]
    )
    for substep in range(STEPS):
        padded = padded_2(velocity, (("slab", 1), ("pencil", 2)), 1)
        velocity = advance(velocity, padded, relax_weight, target)
    return (vertical, velocity)


def solution(mesh):
    in_specs = (
        P("pencil", "slab"),
        P("pencil", "slab"),
        P(None, "slab", "pencil", None),
        P("slab", "pencil", None, None),
        P("slab", "pencil", None),
        P(None, "slab", "pencil"),
        P(None, "slab", "pencil"),
    )
    out_specs = (P("pencil", "slab"), P(None, "slab", "pencil", None))
    return jax.shard_map(
        on_device, mesh=mesh, in_specs=in_specs, out_specs=out_specs, check_vma=False
    )
```

```python
import math

import jax
import jax.numpy as jnp
import numpy as np
from jax import lax
from jax.experimental import pallas as pl
from jax.experimental.pallas import tpu as pltpu
from jax.sharding import PartitionSpec as P

NXW = 4096
NYW = 2048
LANES = 128
CX = 16
CY = 16
CZ = 128
NX = 512
NY = 256
ZONE = 2

TIME_STEP = 0.2
VISCOSITY = 0.6
DEPTH_RATE = 3.0


def stage_tables(peers):
    copies = LANES // peers
    length = peers * LANES
    outer = np.arange(peers)
    inner = np.arange(LANES)
    eye = np.eye(copies)
    angle_a = 2.0 * np.pi / peers * (outer[:, None] * outer[None, :] % peers)
    angle_t = 2.0 * np.pi / length * (outer[:, None] * inner[None, :] % length)
    angle_b = 2.0 * np.pi / LANES * (inner[:, None] * inner[None, :] % LANES)
    cos_a, sin_a = np.kron(np.cos(angle_a), eye), np.kron(np.sin(angle_a), eye)
    cos_b, sin_b = np.cos(angle_b), np.sin(angle_b)
    tables = {
        "fa": np.concatenate([cos_a, -sin_a], axis=0),
        "cos_t": np.repeat(np.cos(angle_t), copies, axis=0),
        "sin_t": np.repeat(np.sin(angle_t), copies, axis=0),
        "fb": np.concatenate([cos_b + sin_b, sin_b - cos_b], axis=0),
        "ib": np.concatenate([cos_b, -sin_b], axis=1),
        "ia": np.concatenate([cos_a + sin_a, sin_a - cos_a], axis=1),
    }
    return tables


TAB_Y = stage_tables(16)
TAB_X = stage_tables(32)


def pair_inverse_b(ib):
    rows = ib.reshape(32, 4, 2 * LANES)
    big = np.zeros((32, 2, 4, 2, 2 * LANES))
    for field in range(2):
        big[:, field, :, field, :] = rows
    return big.reshape(2 * LANES, 4 * LANES)


def pair_inverse_a(ia):
    rows = ia.reshape(32, 4, 2 * LANES)
    big = np.zeros((32, 2, 4, 2, 2 * LANES))
    for field in range(2):
        big[:, field, :, field, :] = rows
    return big.reshape(2 * LANES, 4 * LANES)


Y_IB_PAIR = pair_inverse_b(TAB_Y["ib"])
X_IA_PAIR = pair_inverse_a(TAB_X["ia"])


def f32(array):
    return jnp.asarray(np.asarray(array, np.float32))


def mm(left, right):
    return jnp.dot(
        left, right, precision=lax.Precision.HIGHEST, preferred_element_type=jnp.float32
    )


def twiddle(real, imag, cos_t, sin_t):
    return real * cos_t + imag * sin_t, imag * cos_t - real * sin_t


def forward(block, fa, cos_t, sin_t, fb):
    outer = mm(fa, block)
    real, imag = twiddle(outer[:LANES], outer[LANES:], cos_t, sin_t)
    return mm(jnp.concatenate([real, imag], axis=1), fb)


def run(body, outs, *args):
    shapes = [jax.ShapeDtypeStruct(shape, jnp.float32) for shape in outs]

    def kernel(*refs):
        results = body(*refs[: len(args)])
        for ref, result in zip(refs[len(args) :], results, strict=True):
            for index, piece in result if isinstance(result, list) else [(..., result)]:
                ref[index] = piece.reshape(ref.shape) if index is ... else piece

    params = pltpu.CompilerParams(vmem_limit_bytes=8 << 20)
    return pl.pallas_call(kernel, out_shape=shapes, compiler_params=params)(*args)


def loaded(body):
    return lambda *refs: body(*[ref[...] for ref in refs])


def turn_inputs(eta, potential):
    eta_t = eta.T.reshape(16, 8, LANES)
    potential_t = potential.T.reshape(16, 8, LANES)
    return (jnp.concatenate([eta_t, potential_t], axis=1),)


def turn(block):
    return (block.reshape(-1, LANES).T,)


def first_y(both, fa, cos_t, sin_t, fb):
    eta = both[:, :8].reshape(LANES, LANES)
    potential = both[:, 8:].reshape(LANES, LANES)
    return forward(potential, fa, cos_t, sin_t, fb), eta


def x_stage(powers):
    def multiply(spec, kappa, power):
        factor = kappa
        for _ in range(power - 1):
            factor = factor * kappa
        return spec * (factor * (1.0 / (NXW * NYW)))

    def body(block, kappa, fa, cos_t, sin_t, fb, ib, ia_pair, *older):
        spec = forward(block.reshape(LANES, LANES), fa, cos_t, sin_t, fb)
        other = older[0] if older else spec
        pair = jnp.concatenate(
            [multiply(spec, kappa, powers[0]), multiply(other, kappa, powers[1])], axis=0
        )
        inner = mm(pair, ib)
        parts = []
        for field in range(2):
            rows = inner[field * LANES : (field + 1) * LANES]
            parts += twiddle(rows[:, :LANES], rows[:, LANES:], cos_t, sin_t)
        return mm(ia_pair, jnp.concatenate(parts, axis=0)), spec

    return body


def back_y(block, cos_t, sin_t, ib_pair, ia):
    inner = mm(block.reshape(LANES, 2 * LANES), ib_pair)
    reals, imags = [], []
    for field in range(2):
        part = inner[:, 2 * field * LANES : 2 * (field + 1) * LANES]
        real, imag = twiddle(part[:, :LANES], part[:, LANES:], cos_t, sin_t)
        reals.append(real)
        imags.append(imag)
    stacked = jnp.concatenate(
        [jnp.concatenate(reals, axis=1), jnp.concatenate(imags, axis=1)], axis=0
    )
    fields = mm(ia, stacked)
    return fields[:, :LANES], fields[:, LANES:]


def second_y(block, eta, fa, cos_t, sin_t, fb, ib_pair, ia):
    slope_one, cubic_one = back_y(block, cos_t, sin_t, ib_pair, ia)
    spectrum = forward(-eta * slope_one, fa, cos_t, sin_t, fb)
    return spectrum, slope_one, cubic_one


def third_y(block, eta, fa, cos_t, sin_t, fb, ib_pair, ia):
    slope_two, curve_one = back_y(block, cos_t, sin_t, ib_pair, ia)
    potential_three = -eta * slope_two - 0.5 * eta * eta * curve_one
    return forward(potential_three, fa, cos_t, sin_t, fb), slope_two, curve_one


def last_y(block, eta, slope_one, cubic_one, slope_two, curve_one, cos_t, sin_t, ib_pair, ia):
    slope_three, curve_two = back_y(block, cos_t, sin_t, ib_pair, ia)
    vertical = (
        slope_one
        + slope_two
        + eta * curve_one
        + slope_three
        + eta * curve_two
        + 0.5 * eta * eta * cubic_one
    )
    return (vertical,)


def swap(values, axis):
    return lax.all_to_all(values, axis, 0, 0, tiled=True)


def wave_surface(surface_eta, surface_potential):
    slab_index = lax.axis_index("slab")
    pencil_index = lax.axis_index("pencil")
    fwd_y = [f32(TAB_Y[key]) for key in ("fa", "cos_t", "sin_t", "fb")]
    both_y = fwd_y + [f32(Y_IB_PAIR), f32(TAB_Y["ia"])]
    inv_y = [f32(TAB_Y["cos_t"]), f32(TAB_Y["sin_t"]), f32(Y_IB_PAIR), f32(TAB_Y["ia"])]
    tab_x = [f32(TAB_X[key]) for key in ("fa", "cos_t", "sin_t", "fb", "ib")] + [f32(X_IA_PAIR)]
    square = (LANES, LANES)

    row = lax.broadcasted_iota(jnp.int32, square, 0)
    lane = lax.broadcasted_iota(jnp.int32, square, 1)
    index_x = row // 4 + 32 * lane
    index_y = pencil_index + 16 * (slab_index * 4 + row % 4)
    wave_x = wavenumber(index_x, NXW)
    wave_y = wavenumber(index_y, NYW)
    kappa = jnp.sqrt(wave_x * wave_x + wave_y * wave_y)

    def outward(block):
        (turned,) = run(loaded(turn), [square], swap(block.reshape(16, 8, LANES), "pencil"))
        return swap(turned.reshape(32, 4, LANES), "slab").reshape(square)

    def homeward(block):
        (turned,) = run(loaded(turn), [(LANES, 2 * LANES)], swap(block, "slab"))
        return swap(turned.reshape(16, 8, 2 * LANES), "pencil")

    pair = (32, 8, LANES)
    (turned,) = run(loaded(turn_inputs), [(16, 16, LANES)], surface_eta, surface_potential)
    spectrum, eta = run(loaded(first_y), [square, square], swap(turned, "pencil"), *fwd_y)
    block, spec_one = run(loaded(x_stage((1, 3))), [pair, square], outward(spectrum), kappa, *tab_x)
    spectrum, slope_one, cubic_one = run(loaded(second_y), [square] * 3, homeward(block), eta, *both_y)
    block, spec_two = run(loaded(x_stage((1, 2))), [pair, square], outward(spectrum), kappa, *tab_x, spec_one
    )
    spectrum, slope_two, curve_one = run(loaded(third_y), [square] * 3, homeward(block), eta, *both_y)
    block, _ = run(loaded(x_stage((1, 2))), [pair, square], outward(spectrum), kappa, *tab_x, spec_two)
    (vertical,) = run(loaded(last_y),
        [(16, 8, LANES)],
        homeward(block),
        eta,
        slope_one,
        cubic_one,
        slope_two,
        curve_one,
        *inv_y,
    )
    return swap(vertical, "pencil").reshape(square)


def wavenumber(index, length):
    folded = jnp.minimum(index, length - index)
    return 2.0 * math.pi / length * folded.astype(jnp.float32)


def ramp_weight(distance, reach_len):
    ratio = jnp.clip(1.0 - distance / reach_len, 0.0, 1.0)
    return ratio * ratio


def relax_of(pos_x, pos_y):
    reach_x = float(ZONE * CX)
    reach_y = float(CY)
    along_x = jnp.maximum(ramp_weight(pos_x, reach_x), ramp_weight(NX - 1.0 - pos_x, reach_x))
    across = jnp.maximum(ramp_weight(pos_y, reach_y), ramp_weight(NY - 1.0 - pos_y, reach_y))
    inside = (pos_x >= 0.0) & (pos_x < NX) & (pos_y >= 0.0) & (pos_y < NY)
    return jnp.maximum(along_x, across), inside.astype(jnp.float32)


def thirds(values):
    terms = []
    for _ in range(3):
        term = values.astype(jnp.bfloat16)
        terms.append(term)
        values = values - term.astype(jnp.float32)
    return jnp.concatenate(terms, axis=1)


def chosen(terms, lanes):
    count = lanes.shape[1]
    iota = lax.broadcasted_iota(jnp.int32, (LANES, count), 0)
    hot = jnp.where(iota == lanes, 1.0, 0.0).astype(jnp.bfloat16)
    picked = jnp.dot(
        terms, jnp.concatenate([hot] * 3, axis=0), preferred_element_type=jnp.float32
    )
    return picked, iota


def listed(columns, points, row_count):
    terms = thirds(columns)
    rows = []
    for i in range(row_count):
        point = points[i : i + 1, :]
        picked, iota = chosen(terms, lax.shift_right_arithmetic(point, 7))
        found = jnp.where(iota == (point & (LANES - 1)), picked, 0.0)
        rows.append(jnp.sum(found, axis=0, keepdims=True))
    return rows


POINT_ROWS = 11


def pick_elevation(eta, points):
    rows = listed(eta[...].T, points, POINT_ROWS)
    return ([(slice(i, i + 1), row) for i, row in enumerate(rows)],)


def pick_vertical(columns, points, eta_rows):
    columns = columns[...]
    rows = listed(columns, points, POINT_ROWS)
    pieces = [((slice(None), slice(None)), jnp.zeros((LANES, LANES), jnp.float32))]

    def put(slab, place, row, half):
        at = slice(half * LANES, (half + 1) * LANES)
        for field, value in enumerate((eta_rows[row : row + 1, at], rows[row][:, at])):
            line = 4 * slab + 2 * place + field
            pieces.append(((slice(line, line + 1), slice(None)), value))

    for row, slab in enumerate((0, 1, 30, 31)):
        for half in range(2):
            put(slab, half, row, half)
    for slab in range(2, 30):
        put(slab, 0, 4 + (slab - 2) // 4, (slab - 2) % 4 // 2)
    return pieces, columns.T


def sample(arrived, lines, lanes, shares):
    terms = thirds(arrived[...])
    totals = [0.0, 0.0]
    for q in range(4):
        picked, iota = chosen(terms, lanes[q : q + 1, :])
        picked = picked * shares[q : q + 1, :]
        line = lines[q : q + 1, :]
        for field in range(2):
            totals[field] = totals[field] + jnp.where(iota == line + field, picked, 0.0)
    rows = [jnp.sum(total, axis=0, keepdims=True) for total in totals]
    return (jnp.concatenate(rows + [jnp.zeros((6, 256), jnp.float32)], axis=0),)


def roll(values, shift, axis):
    return pltpu.roll(values, shift, axis)


def predicted_of(centers, neighbours):
    lane = lax.broadcasted_iota(jnp.int32, centers[0].shape, centers[0].ndim - 1)
    last = centers[0].ndim - 1
    results = []
    for center, (plus_x, minus_x, plus_y, minus_y) in zip(centers, neighbours, strict=True):
        plus_z = jnp.where(lane == CZ - 1, 0.0, roll(center, CZ - 1, last))
        minus_z = jnp.where(lane == 0, 0.0, roll(center, 1, last))
        laplace = plus_x + minus_x + (plus_y + minus_y) + (plus_z + minus_z) - 6.0 * center
        advect = (
            centers[0] * (plus_x - minus_x)
            + centers[1] * (plus_y - minus_y)
            + centers[2] * (plus_z - minus_z)
        )
        results.append(center + TIME_STEP * (VISCOSITY * laplace - 0.5 * advect))
    return results


def first_substep(padded, keep, keep_x, keep_y):
    def region(x_at, x_to, y_at, y_to):
        def part(c, shift_x, shift_y):
            return padded[c, x_at + shift_x : x_to + shift_x, y_at + shift_y : y_to + shift_y, :]

        steps = ((1, 0), (-1, 0), (0, 1), (0, -1))
        centers = [part(c, 0, 0) for c in range(3)]
        return predicted_of(centers, [[part(c, *step) for step in steps] for c in range(3)])

    own, face_x, face_y = [], [], []
    for c, value in enumerate(region(2, 18, 2, 18)):
        own.append(((c,), value * keep[...]))
    for side, x_at in enumerate((1, 18)):
        for c, value in enumerate(region(x_at, x_at + 1, 2, 18)):
            face_x.append(((c, slice(side, side + 1)), value * keep_x[side : side + 1]))
    for row, y_at in ((0, 1), (15, 18)):
        for c, value in enumerate(region(2, 18, y_at, y_at + 1)):
            where = (slice(None), slice(row, row + 1))
            face_y.append(((c, *where), value * keep_y[where]))
    return own, face_x, face_y


def second_substep(
    own, face_x, face_y, keep, pull, pull_x, pull_y, here, from_up_x, from_down_x, from_up_y, from_down_y
):
    lane = lax.broadcasted_iota(jnp.int32, (8, 256), 1)
    across_y = jnp.where(
        lane % CY == 0, roll(from_down_y[...], 241, 1), roll(from_up_y[...], 15, 1)
    )
    across_x = jnp.where(lane < CY, roll(from_down_x[...], 16, 1), roll(from_up_x[...], 240, 1))
    surface = jnp.concatenate([here[...], across_x, across_y], axis=0).T

    def column(index):
        return surface[:, index : index + 1].reshape(CX, CY, 1)

    shape = (CX, CY, CZ)
    row = lax.broadcasted_iota(jnp.int32, shape, 1)
    centers, neighbours, targets = [], [], []
    for c in range(3):
        center = own[c]
        outer_x = [face_x[c, 0:1], face_x[c, 1:2]]
        outer_y = face_y[c]
        target = None
        if c != 1:
            field = c // 2
            target = pull[...] * column(field)
            center = center + target
            line = column(8 + field)
            outer_x = [
                outer_x[0] + pull_x[0:1] * line[0:1],
                outer_x[1] + pull_x[1:2] * line[CX - 1 : CX],
            ]
            outer_y = outer_y + pull_y[...] * column(16 + field)
        plus_x = jnp.concatenate([center[1:], outer_x[1]], axis=0)
        minus_x = jnp.concatenate([outer_x[0], center[:-1]], axis=0)
        plus_y = jnp.where(row == CY - 1, outer_y, roll(center, CY - 1, 1))
        minus_y = jnp.where(row == 0, outer_y, roll(center, 1, 1))
        centers.append(center)
        neighbours.append((plus_x, minus_x, plus_y, minus_y))
        targets.append(target)
    pieces = []
    for c, value in enumerate(predicted_of(centers, neighbours)):
        value = value * keep[...]
        pieces.append(((c,), value if targets[c] is None else value + targets[c]))
    return (pieces,)


def shifted(values, axis, step):
    size = lax.axis_size(axis)
    pairs = [(i, i + step) for i in range(size) if 0 <= i + step < size]
    return lax.ppermute(values, axis, pairs)


def padded_2(shard, sides, width):
    for axis, dim in sides:
        length = shard.shape[dim]
        last = lax.slice_in_dim(shard, length - width, length, axis=dim)
        leading = lax.slice_in_dim(shard, 0, width, axis=dim)
        before = shifted(last, axis, 1)
        after = shifted(leading, axis, -1)
        shard = jnp.concatenate([before, shard, after], axis=dim)
    return shard


def list_points(send_point, send_count):
    slot = lax.broadcasted_iota(jnp.int32, (32, 256), 1)
    points = jnp.where(slot < send_count[0, 0][:, None], send_point[0, 0], -1)
    inner = points[2:30, :64].reshape(7, 256)
    return jnp.concatenate(
        [points[:2], points[30:], inner, jnp.full((5, 256), -1, jnp.int32)], axis=0
    )


def on_device(
    surface_eta, surface_potential, velocity, send_point, send_count, stencil, interp_weight
):
    slab_index = lax.axis_index("slab")
    pencil_index = lax.axis_index("pencil")
    square = (LANES, LANES)

    cell_x = lax.broadcasted_iota(jnp.int32, (CX, CY, CZ), 0)
    cell_y = lax.broadcasted_iota(jnp.int32, (CX, CY, CZ), 1)
    level = lax.broadcasted_iota(jnp.int32, (CX, CY, CZ), 2).astype(jnp.float32)
    decay = jnp.exp(-DEPTH_RATE * (CZ - 1.0 - level) / CZ)
    pos_x = (slab_index * CX + cell_x).astype(jnp.float32)
    pos_y = (pencil_index * CY + cell_y).astype(jnp.float32)
    relax, _ = relax_of(pos_x, pos_y)
    keep, pull = 1.0 - relax, relax * decay
    out_y = jnp.where(cell_y == 0, pos_y - 1.0, jnp.where(cell_y == CY - 1, pos_y + 1.0, pos_y))
    relax, inside = relax_of(pos_x, out_y)
    keep_y, pull_y = (1.0 - relax) * inside, relax * inside * decay
    out_x = pos_x[:2] + jnp.where(cell_x[:2] == 0, -1.0, CX - 1.0)
    relax, inside = relax_of(out_x, pos_y[:2])
    keep_x, pull_x = (1.0 - relax) * inside, relax * inside * decay[:2]
    padded = padded_2(velocity, (("slab", 1), ("pencil", 2)), 2)
    block = (3, CX, CY, CZ)
    own, face_x, face_y = run(
        first_substep, [block, (3, 2, CY, CZ), block], padded, keep, keep_x, keep_y
    )

    points = list_points(send_point, send_count)
    (eta_rows,) = run(pick_elevation, [(POINT_ROWS, 256)], surface_eta, points)
    flat = stencil.reshape(4, CX * CY)
    slot = flat & 255
    in_zone = (slab_index < ZONE) | (slab_index >= 32 - ZONE)
    lines = 4 * (flat >> 8) + jnp.where(in_zone, 2 * (slot >> 7), 0)
    lanes = jnp.where(in_zone, slot & 127, (slot & 63) + 64 * (slab_index & 1))
    weights = interp_weight.reshape(4, CX * CY)
    shares = weights / jnp.sum(weights, axis=0)

    columns = wave_surface(surface_eta, surface_potential)
    outgoing, vertical = run(pick_vertical, [square, square], columns, points, eta_rows)
    arrived = swap(outgoing.reshape(32, 4, LANES), "slab").reshape(square)
    (here,) = run(sample, [(8, 256)], arrived, lines, lanes, shares)
    neighbours = [shifted(here, axis, step) for axis in ("slab", "pencil") for step in (-1, 1)]
    (velocity,) = run(
        second_substep,
        [block],
        own,
        face_x,
        face_y,
        keep,
        pull,
        pull_x,
        pull_y,
        here,
        *neighbours,
    )
    return (vertical, velocity)


def solution(mesh):
    in_specs = (
        P("pencil", "slab"),
        P("pencil", "slab"),
        P(None, "slab", "pencil", None),
        P("slab", "pencil", None, None),
        P("slab", "pencil", None),
        P(None, "slab", "pencil"),
        P(None, "slab", "pencil"),
    )
    out_specs = (P("pencil", "slab"), P(None, "slab", "pencil", None))
    return jax.shard_map(
        on_device, mesh=mesh, in_specs=in_specs, out_specs=out_specs, check_vma=False
    )
```

```python
import math

import jax
import jax.numpy as jnp
import ml_dtypes
import numpy as np
from jax import lax
from jax.experimental import pallas as pl
from jax.experimental.pallas import tpu as pltpu
from jax.sharding import PartitionSpec as P

NXW = 4096
NYW = 2048
LANES = 128
CX = 16
CY = 16
CZ = 128
NX = 512
NY = 256
ZONE = 2

TIME_STEP = 0.2
VISCOSITY = 0.6
DEPTH_RATE = 3.0


def stage_tables(peers):
    copies = LANES // peers
    length = peers * LANES
    outer = np.arange(peers)
    inner = np.arange(LANES)
    eye = np.eye(copies)
    angle_a = 2.0 * np.pi / peers * (outer[:, None] * outer[None, :] % peers)
    angle_t = 2.0 * np.pi / length * (outer[:, None] * inner[None, :] % length)
    angle_b = 2.0 * np.pi / LANES * (inner[:, None] * inner[None, :] % LANES)
    cos_a, sin_a = np.kron(np.cos(angle_a), eye), np.kron(np.sin(angle_a), eye)
    cos_b, sin_b = np.cos(angle_b), np.sin(angle_b)
    tables = {
        "fa": np.concatenate([cos_a, -sin_a], axis=0),
        "cos_t": np.repeat(np.cos(angle_t), copies, axis=0),
        "sin_t": np.repeat(np.sin(angle_t), copies, axis=0),
        "fb": np.concatenate([cos_b + sin_b, sin_b - cos_b], axis=0),
        "ib": np.concatenate([cos_b, -sin_b], axis=1),
        "ia": np.concatenate([cos_a + sin_a, sin_a - cos_a], axis=1),
    }
    return tables


TAB_Y = stage_tables(16)
TAB_X = stage_tables(32)


def pair_inverse_b(ib):
    rows = ib.reshape(32, 4, 2 * LANES)
    big = np.zeros((32, 2, 4, 2, 2 * LANES))
    for field in range(2):
        big[:, field, :, field, :] = rows
    return big.reshape(2 * LANES, 4 * LANES)


def pair_inverse_a(ia):
    rows = ia.reshape(32, 4, 2 * LANES)
    big = np.zeros((32, 2, 4, 2, 2 * LANES))
    for field in range(2):
        big[:, field, :, field, :] = rows
    return big.reshape(2 * LANES, 4 * LANES)


Y_IB_PAIR = pair_inverse_b(TAB_Y["ib"])
X_IA_PAIR = pair_inverse_a(TAB_X["ia"])


def f32(array):
    return jnp.asarray(np.asarray(array, np.float32))


def halves_of(table):
    high = table.astype(ml_dtypes.bfloat16)
    return high, (table - high.astype(np.float64)).astype(ml_dtypes.bfloat16)


def left_table(table):
    high, low = halves_of(table)
    return jnp.asarray(np.concatenate([high, high, low], axis=1))


def right_table(table):
    high, low = halves_of(table)
    return jnp.asarray(np.concatenate([high, low, high], axis=0))


def halves(values):
    high = values.astype(jnp.bfloat16)
    return high, (values - high.astype(jnp.float32)).astype(jnp.bfloat16)


def from_left(table, values):
    high, low = halves(values)
    stacked = jnp.concatenate([high, low, high], axis=0)
    return jnp.dot(table, stacked, preferred_element_type=jnp.float32)


def from_right(values, table):
    high, low = halves(values)
    joined = jnp.concatenate([high, high, low], axis=1)
    return jnp.dot(joined, table, preferred_element_type=jnp.float32)


def twiddle(real, imag, cos_t, sin_t):
    return real * cos_t + imag * sin_t, imag * cos_t - real * sin_t


def forward(block, fa, cos_t, sin_t, fb):
    outer = from_left(fa, block)
    real, imag = twiddle(outer[:LANES], outer[LANES:], cos_t, sin_t)
    return from_right(jnp.concatenate([real, imag], axis=1), fb)


def run(body, outs, *args, room=8):
    shapes = [jax.ShapeDtypeStruct(shape, jnp.float32) for shape in outs]

    def kernel(*refs):
        results = body(*refs[: len(args)])
        for ref, result in zip(refs[len(args) :], results, strict=True):
            for index, piece in result if isinstance(result, list) else [(..., result)]:
                ref[index] = piece.reshape(ref.shape) if index is ... else piece

    params = pltpu.CompilerParams(vmem_limit_bytes=room << 20)
    return pl.pallas_call(kernel, out_shape=shapes, compiler_params=params)(*args)


def loaded(body):
    return lambda *refs: body(*[ref[...] for ref in refs])


def turn_inputs(eta, potential):
    eta_t = eta.T.reshape(16, 8, LANES)
    potential_t = potential.T.reshape(16, 8, LANES)
    return (jnp.concatenate([eta_t, potential_t], axis=1),)


def turn(block):
    return (block.reshape(-1, LANES).T,)


def first_y(both, fa, cos_t, sin_t, fb):
    eta = both[:, :8].reshape(LANES, LANES)
    potential = both[:, 8:].reshape(LANES, LANES)
    return forward(potential, fa, cos_t, sin_t, fb), eta


def x_stage(powers):
    def multiply(spec, kappa, power):
        factor = kappa
        for _ in range(power - 1):
            factor = factor * kappa
        return spec * (factor * (1.0 / (NXW * NYW)))

    def body(block, kappa, fa, cos_t, sin_t, fb, ib, ia_pair, *older):
        spec = forward(block.reshape(LANES, LANES), fa, cos_t, sin_t, fb)
        other = older[0] if older else spec
        pair = jnp.concatenate(
            [multiply(spec, kappa, powers[0]), multiply(other, kappa, powers[1])], axis=0
        )
        inner = from_right(pair, ib)
        parts = []
        for field in range(2):
            rows = inner[field * LANES : (field + 1) * LANES]
            parts += twiddle(rows[:, :LANES], rows[:, LANES:], cos_t, sin_t)
        return from_left(ia_pair, jnp.concatenate(parts, axis=0)), spec

    return body


def back_y(block, cos_t, sin_t, ib_pair, ia):
    inner = from_right(block.reshape(LANES, 2 * LANES), ib_pair)
    reals, imags = [], []
    for field in range(2):
        part = inner[:, 2 * field * LANES : 2 * (field + 1) * LANES]
        real, imag = twiddle(part[:, :LANES], part[:, LANES:], cos_t, sin_t)
        reals.append(real)
        imags.append(imag)
    stacked = jnp.concatenate(
        [jnp.concatenate(reals, axis=1), jnp.concatenate(imags, axis=1)], axis=0
    )
    fields = from_left(ia, stacked)
    return fields[:, :LANES], fields[:, LANES:]


def second_y(block, eta, fa, cos_t, sin_t, fb, ib_pair, ia):
    slope_one, cubic_one = back_y(block, cos_t, sin_t, ib_pair, ia)
    spectrum = forward(-eta * slope_one, fa, cos_t, sin_t, fb)
    return spectrum, slope_one, cubic_one


def third_y(block, eta, fa, cos_t, sin_t, fb, ib_pair, ia):
    slope_two, curve_one = back_y(block, cos_t, sin_t, ib_pair, ia)
    potential_three = -eta * slope_two - 0.5 * eta * eta * curve_one
    return forward(potential_three, fa, cos_t, sin_t, fb), slope_two, curve_one


def last_y(block, eta, slope_one, cubic_one, slope_two, curve_one, cos_t, sin_t, ib_pair, ia):
    slope_three, curve_two = back_y(block, cos_t, sin_t, ib_pair, ia)
    vertical = (
        slope_one
        + slope_two
        + eta * curve_one
        + slope_three
        + eta * curve_two
        + 0.5 * eta * eta * cubic_one
    )
    return (vertical,)


def swap(values, axis):
    return lax.all_to_all(values, axis, 0, 0, tiled=True)


def beside(values, axis, work, *inputs):
    values, inputs = lax.optimization_barrier((values, inputs))
    moved = swap(values, axis)
    return lax.optimization_barrier((moved, work(*inputs)))


INDEX_X = np.arange(LANES)[:, None] // 4 + 32 * np.arange(LANES)[None, :]
WAVE_X = np.float32(2.0 * math.pi / NXW) * np.minimum(INDEX_X, NXW - INDEX_X).astype(np.float32)
LINE_Y = np.repeat(16 * (np.arange(LANES)[:, None] % 4), LANES, axis=1).astype(np.int32)


def magnitude(slab_index, pencil_index):
    index_y = pencil_index + 64 * slab_index + jnp.asarray(LINE_Y)
    wave_y = wavenumber(index_y, NYW)
    return jnp.sqrt(jnp.asarray(WAVE_X * WAVE_X) + wave_y * wave_y)


def wave_surface(surface_eta, surface_potential, works):
    slab_index = lax.axis_index("slab")
    pencil_index = lax.axis_index("pencil")
    square = (LANES, LANES)
    turns_y = [f32(TAB_Y["cos_t"]), f32(TAB_Y["sin_t"])]
    turns_x = [f32(TAB_X["cos_t"]), f32(TAB_X["sin_t"])]
    fwd_y = [left_table(TAB_Y["fa"]), *turns_y, right_table(TAB_Y["fb"])]
    inv_y = [right_table(Y_IB_PAIR), left_table(TAB_Y["ia"])]
    tab_x = [
        left_table(TAB_X["fa"]),
        *turns_x,
        right_table(TAB_X["fb"]),
        right_table(TAB_X["ib"]),
        left_table(X_IA_PAIR),
    ]

    def to_slab(block):
        (turned,) = run(loaded(turn), [square], swap(block.reshape(16, 8, LANES), "pencil"))
        return turned.reshape(32, 4, LANES)

    def outward(block):
        return swap(to_slab(block), "slab").reshape(square)

    def to_pencil(block):
        (turned,) = run(loaded(turn), [(LANES, 2 * LANES)], block)
        return swap(turned.reshape(16, 8, 2 * LANES), "pencil")

    def homeward(block):
        return to_pencil(swap(block, "slab"))

    def first_work(slab_index, pencil_index, *inputs):
        return magnitude(slab_index, pencil_index), works[0][0](*inputs)

    pair = (32, 8, LANES)
    (turned,) = run(
        loaded(turn_inputs), [(16, 16, LANES)], surface_eta, surface_potential, room=48
    )
    both, (kappa, given) = beside(
        turned, "pencil", first_work, slab_index, pencil_index, *works[0][1]
    )
    spectrum, eta = run(loaded(first_y), [square, square], both, *fwd_y)
    block, given = beside(to_slab(spectrum), "slab", works[1][0], given, *works[1][1])
    block, spec_one = run(
        loaded(x_stage((1, 3))), [pair, square], block.reshape(square), kappa, *tab_x
    )
    block, given = beside(block, "slab", works[2][0], given, *works[2][1])
    spectrum, slope_one, cubic_one = run(
        loaded(second_y), [square] * 3, to_pencil(block), eta, *fwd_y, *inv_y
    )
    block, spec_two = run(
        loaded(x_stage((1, 2))), [pair, square], outward(spectrum), kappa, *tab_x, spec_one
    )
    spectrum, slope_two, curve_one = run(
        loaded(third_y), [square] * 3, homeward(block), eta, *fwd_y, *inv_y
    )
    block, _ = run(
        loaded(x_stage((1, 2))), [pair, square], outward(spectrum), kappa, *tab_x, spec_two
    )
    (vertical,) = run(
        loaded(last_y),
        [(16, 8, LANES)],
        homeward(block),
        eta,
        slope_one,
        cubic_one,
        slope_two,
        curve_one,
        *turns_y,
        *inv_y,
    )
    return swap(vertical, "pencil").reshape(square), given


def wavenumber(index, length):
    folded = jnp.minimum(index, length - index)
    return 2.0 * math.pi / length * folded.astype(jnp.float32)


def ramp_weight(distance, reach_len):
    ratio = jnp.clip(1.0 - distance / reach_len, 0.0, 1.0)
    return ratio * ratio


def relax_of(pos_x, pos_y):
    reach_x = float(ZONE * CX)
    reach_y = float(CY)
    along_x = jnp.maximum(ramp_weight(pos_x, reach_x), ramp_weight(NX - 1.0 - pos_x, reach_x))
    across = jnp.maximum(ramp_weight(pos_y, reach_y), ramp_weight(NY - 1.0 - pos_y, reach_y))
    inside = (pos_x >= 0.0) & (pos_x < NX) & (pos_y >= 0.0) & (pos_y < NY)
    return jnp.maximum(along_x, across), inside.astype(jnp.float32)


def thirds(values):
    terms = []
    for _ in range(3):
        term = values.astype(jnp.bfloat16)
        terms.append(term)
        values = values - term.astype(jnp.float32)
    return jnp.concatenate(terms, axis=1)


def chosen(terms, lanes):
    count = lanes.shape[1]
    iota = lax.broadcasted_iota(jnp.int32, (LANES, count), 0)
    hot = jnp.where(iota == lanes, 1.0, 0.0).astype(jnp.bfloat16)
    picked = jnp.dot(
        terms, jnp.concatenate([hot] * 3, axis=0), preferred_element_type=jnp.float32
    )
    return picked, iota


def listed(columns, points, row_count):
    terms = thirds(columns)
    rows = []
    for i in range(row_count):
        point = points[i : i + 1, :]
        picked, iota = chosen(terms, lax.shift_right_arithmetic(point, 7))
        found = jnp.where(iota == (point & (LANES - 1)), picked, 0.0)
        rows.append(jnp.sum(found, axis=0, keepdims=True))
    return rows


POINT_ROWS = 11


def pick_elevation(eta, points):
    rows = listed(eta[...].T, points, POINT_ROWS)
    return ([(slice(i, i + 1), row) for i, row in enumerate(rows)],)


def pick_vertical(columns, points, eta_rows):
    columns = columns[...]
    rows = listed(columns, points, POINT_ROWS)
    pieces = [((slice(None), slice(None)), jnp.zeros((LANES, LANES), jnp.float32))]

    def put(slab, place, row, half):
        at = slice(half * LANES, (half + 1) * LANES)
        for field, value in enumerate((eta_rows[row : row + 1, at], rows[row][:, at])):
            line = 4 * slab + 2 * place + field
            pieces.append(((slice(line, line + 1), slice(None)), value))

    for row, slab in enumerate((0, 1, 30, 31)):
        for half in range(2):
            put(slab, half, row, half)
    for slab in range(2, 30):
        put(slab, 0, 4 + (slab - 2) // 4, (slab - 2) % 4 // 2)
    return pieces, columns.T


def sample(arrived, lines, lanes, shares):
    terms = thirds(arrived[...])
    totals = [0.0, 0.0]
    for q in range(4):
        picked, iota = chosen(terms, lanes[q : q + 1, :])
        picked = picked * shares[q : q + 1, :]
        line = lines[q : q + 1, :]
        for field in range(2):
            totals[field] = totals[field] + jnp.where(iota == line + field, picked, 0.0)
    rows = [jnp.sum(total, axis=0, keepdims=True) for total in totals]
    return (jnp.concatenate(rows + [jnp.zeros((6, 256), jnp.float32)], axis=0),)


def roll(values, shift, axis):
    return pltpu.roll(values, shift, axis)


def predicted_of(centers, neighbours):
    lane = lax.broadcasted_iota(jnp.int32, centers[0].shape, centers[0].ndim - 1)
    last = centers[0].ndim - 1
    results = []
    for center, (plus_x, minus_x, plus_y, minus_y) in zip(centers, neighbours, strict=True):
        plus_z = jnp.where(lane == CZ - 1, 0.0, roll(center, CZ - 1, last))
        minus_z = jnp.where(lane == 0, 0.0, roll(center, 1, last))
        laplace = plus_x + minus_x + (plus_y + minus_y) + (plus_z + minus_z) - 6.0 * center
        advect = (
            centers[0] * (plus_x - minus_x)
            + centers[1] * (plus_y - minus_y)
            + centers[2] * (plus_z - minus_z)
        )
        results.append(center + TIME_STEP * (VISCOSITY * laplace - 0.5 * advect))
    return results


def first_substep(padded, keep, keep_x, keep_y):
    def region(x_at, x_to, y_at, y_to):
        def part(c, shift_x, shift_y):
            return padded[c, x_at + shift_x : x_to + shift_x, y_at + shift_y : y_to + shift_y, :]

        steps = ((1, 0), (-1, 0), (0, 1), (0, -1))
        centers = [part(c, 0, 0) for c in range(3)]
        return predicted_of(centers, [[part(c, *step) for step in steps] for c in range(3)])

    own, face_x, face_y = [], [], []
    for c, value in enumerate(region(2, 18, 2, 18)):
        own.append(((c,), value * keep[...]))
    for side, x_at in enumerate((1, 18)):
        for c, value in enumerate(region(x_at, x_at + 1, 2, 18)):
            face_x.append(((c, slice(side, side + 1)), value * keep_x[side : side + 1]))
    for row, y_at in ((0, 1), (15, 18)):
        for c, value in enumerate(region(2, 18, y_at, y_at + 1)):
            where = (slice(None), slice(row, row + 1))
            face_y.append(((c, *where), value * keep_y[where]))
    return own, face_x, face_y


def second_substep(
    own, face_x, face_y, keep, pull, pull_x, pull_y, here, from_up_x, from_down_x, from_up_y, from_down_y
):
    lane = lax.broadcasted_iota(jnp.int32, (8, 256), 1)
    across_y = jnp.where(
        lane % CY == 0, roll(from_down_y[...], 241, 1), roll(from_up_y[...], 15, 1)
    )
    across_x = jnp.where(lane < CY, roll(from_down_x[...], 16, 1), roll(from_up_x[...], 240, 1))
    surface = jnp.concatenate([here[...], across_x, across_y], axis=0).T

    def column(index):
        return surface[:, index : index + 1].reshape(CX, CY, 1)

    shape = (CX, CY, CZ)
    row = lax.broadcasted_iota(jnp.int32, shape, 1)
    centers, neighbours, targets = [], [], []
    for c in range(3):
        center = own[c]
        outer_x = [face_x[c, 0:1], face_x[c, 1:2]]
        outer_y = face_y[c]
        target = None
        if c != 1:
            field = c // 2
            target = pull[...] * column(field)
            center = center + target
            line = column(8 + field)
            outer_x = [
                outer_x[0] + pull_x[0:1] * line[0:1],
                outer_x[1] + pull_x[1:2] * line[CX - 1 : CX],
            ]
            outer_y = outer_y + pull_y[...] * column(16 + field)
        plus_x = jnp.concatenate([center[1:], outer_x[1]], axis=0)
        minus_x = jnp.concatenate([outer_x[0], center[:-1]], axis=0)
        plus_y = jnp.where(row == CY - 1, outer_y, roll(center, CY - 1, 1))
        minus_y = jnp.where(row == 0, outer_y, roll(center, 1, 1))
        centers.append(center)
        neighbours.append((plus_x, minus_x, plus_y, minus_y))
        targets.append(target)
    pieces = []
    for c, value in enumerate(predicted_of(centers, neighbours)):
        value = value * keep[...]
        pieces.append(((c,), value if targets[c] is None else value + targets[c]))
    return (pieces,)


def shifted(values, axis, step):
    size = lax.axis_size(axis)
    pairs = [(i, i + step) for i in range(size) if 0 <= i + step < size]
    return lax.ppermute(values, axis, pairs)


def halo(shard, axis, dim, width):
    length = shard.shape[dim]
    last = lax.slice_in_dim(shard, length - width, length, axis=dim)
    leading = lax.slice_in_dim(shard, 0, width, axis=dim)
    return shifted(last, axis, 1), shifted(leading, axis, -1)


def list_points(send_point, send_count):
    slot = lax.broadcasted_iota(jnp.int32, (32, 256), 1)
    points = jnp.where(slot < send_count[0, 0][:, None], send_point[0, 0], -1)
    inner = points[2:30, :64].reshape(7, 256)
    return jnp.concatenate([points[:2], points[30:], inner], axis=0)


DECAY = np.exp(-DEPTH_RATE * (CZ - 1.0 - np.arange(CZ)) / CZ).astype(np.float32)


def relax_fields(slab_index, pencil_index):
    decay = jnp.asarray(DECAY)
    cell_x = slab_index * CX + lax.broadcasted_iota(jnp.int32, (CX, CY, CZ), 0)
    cell_y = pencil_index * CY + lax.broadcasted_iota(jnp.int32, (CX, CY, CZ), 1)
    pos_x, pos_y = cell_x.astype(jnp.float32), cell_y.astype(jnp.float32)
    relax, _ = relax_of(pos_x, pos_y)
    keep, pull = 1.0 - relax, relax * decay
    low, high = cell_y == pencil_index * CY, cell_y == pencil_index * CY + CY - 1
    out_y = jnp.where(low, pos_y - 1.0, jnp.where(high, pos_y + 1.0, pos_y))
    relax, inside = relax_of(pos_x, out_y)
    keep_y, pull_y = (1.0 - relax) * inside, relax * inside * decay
    out_x = jnp.where(cell_x[:2] == slab_index * CX, pos_x[:2] - 1.0, pos_x[:2] + (CX - 1.0))
    relax, inside = relax_of(out_x, pos_y[:2])
    keep_x, pull_x = (1.0 - relax) * inside, relax * inside * decay
    return (keep, keep_x, keep_y), (pull, pull_x, pull_y)


def stencil_places(stencil, interp_weight, slab_index):
    flat = stencil.reshape(4, CX * CY)
    slot = flat & 255
    in_zone = (slab_index < ZONE) | (slab_index >= 32 - ZONE)
    lines = 4 * (flat >> 8) + jnp.where(in_zone, 2 * (slot >> 7), 0)
    lanes = jnp.where(in_zone, slot & 127, (slot & 63) + 64 * (slab_index & 1))
    shares = interp_weight / jnp.sum(interp_weight, axis=0)
    return lines, lanes, shares.reshape(4, CX * CY)


def on_device(
    surface_eta, surface_potential, velocity, send_point, send_count, stencil, interp_weight
):
    slab_index = lax.axis_index("slab")
    pencil_index = lax.axis_index("pencil")
    square = (LANES, LANES)
    block = (3, CX, CY, CZ)

    def halo_x(velocity):
        return halo(velocity, "slab", 1, 2)

    def halo_y(sides, velocity, send_point, send_count):
        joined = jnp.concatenate([sides[0], velocity, sides[1]], axis=1)
        points = list_points(send_point, send_count)
        return joined, halo(joined, "pencil", 2, 2), points

    def prepare(given, eta, stencil, interp_weight, slab_index, pencil_index):
        joined, sides, points = given
        padded = jnp.concatenate([sides[0], joined, sides[1]], axis=2)
        keeps, pulls = relax_fields(slab_index, pencil_index)
        ahead = run(first_substep, [block, (3, 2, CY, CZ), block], padded, *keeps)
        (eta_rows,) = run(pick_elevation, [(POINT_ROWS, 256)], eta, points)
        sampling = stencil_places(stencil, interp_weight, slab_index)
        return ahead, (keeps[0], *pulls), points, eta_rows, sampling

    works = (
        (halo_x, (velocity,)),
        (halo_y, (velocity, send_point, send_count)),
        (prepare, (surface_eta, stencil, interp_weight, slab_index, pencil_index)),
    )
    columns, given = wave_surface(surface_eta, surface_potential, works)
    ahead, fields, points, eta_rows, sampling = given
    outgoing, vertical = run(pick_vertical, [square, square], columns, points, eta_rows)
    arrived = swap(outgoing.reshape(32, 4, LANES), "slab").reshape(square)
    (here,) = run(sample, [(8, 256)], arrived, *sampling)
    neighbours = [shifted(here, axis, step) for axis in ("slab", "pencil") for step in (-1, 1)]
    (velocity,) = run(second_substep, [block], *ahead, *fields, here, *neighbours)
    return (vertical, velocity)


def solution(mesh):
    in_specs = (
        P("pencil", "slab"),
        P("pencil", "slab"),
        P(None, "slab", "pencil", None),
        P("slab", "pencil", None, None),
        P("slab", "pencil", None),
        P(None, "slab", "pencil"),
        P(None, "slab", "pencil"),
    )
    out_specs = (P("pencil", "slab"), P(None, "slab", "pencil", None))
    return jax.shard_map(
        on_device, mesh=mesh, in_specs=in_specs, out_specs=out_specs, check_vma=False
    )
```

```python
import math

import jax
import jax.numpy as jnp
import ml_dtypes
import numpy as np
from jax import lax
from jax.experimental import pallas as pl
from jax.experimental.pallas import tpu as pltpu
from jax.sharding import PartitionSpec as P

NXW = 4096
NYW = 2048
LANES = 128
CX = 16
CY = 16
CZ = 128
NX = 512
NY = 256
ZONE = 2

TIME_STEP = 0.2
VISCOSITY = 0.6
DEPTH_RATE = 3.0


def stage_tables(peers):
    copies = LANES // peers
    length = peers * LANES
    outer = np.arange(peers)
    inner = np.arange(LANES)
    eye = np.eye(copies)
    angle_a = 2.0 * np.pi / peers * (outer[:, None] * outer[None, :] % peers)
    angle_t = 2.0 * np.pi / length * (outer[:, None] * inner[None, :] % length)
    angle_b = 2.0 * np.pi / LANES * (inner[:, None] * inner[None, :] % LANES)
    cos_a, sin_a = np.kron(np.cos(angle_a), eye), np.kron(np.sin(angle_a), eye)
    cos_b, sin_b = np.cos(angle_b), np.sin(angle_b)
    tables = {
        "fa": np.concatenate([cos_a, -sin_a], axis=0),
        "cos_t": np.repeat(np.cos(angle_t), copies, axis=0),
        "sin_t": np.repeat(np.sin(angle_t), copies, axis=0),
        "fb": np.concatenate([cos_b + sin_b, sin_b - cos_b], axis=0),
        "ib": np.concatenate([cos_b, -sin_b], axis=1),
        "ia": np.concatenate([cos_a + sin_a, sin_a - cos_a], axis=1),
    }
    return tables


TAB_Y = stage_tables(16)
TAB_X = stage_tables(32)


def pair_inverse_b(ib):
    rows = ib.reshape(32, 4, 2 * LANES)
    big = np.zeros((32, 2, 4, 2, 2 * LANES))
    for field in range(2):
        big[:, field, :, field, :] = rows
    return big.reshape(2 * LANES, 4 * LANES)


def pair_inverse_a(ia):
    rows = ia.reshape(32, 4, 2 * LANES)
    big = np.zeros((32, 2, 4, 2, 2 * LANES))
    for field in range(2):
        big[:, field, :, field, :] = rows
    return big.reshape(2 * LANES, 4 * LANES)


Y_IB_PAIR = pair_inverse_b(TAB_Y["ib"])
X_IA_PAIR = pair_inverse_a(TAB_X["ia"])


def f32(array):
    return jnp.asarray(np.asarray(array, np.float32))


def halves_of(table):
    high = table.astype(ml_dtypes.bfloat16)
    return high, (table - high.astype(np.float64)).astype(ml_dtypes.bfloat16)


def left_table(table):
    high, low = halves_of(table)
    return jnp.asarray(np.concatenate([high, high, low], axis=1))


def right_table(table):
    high, low = halves_of(table)
    return jnp.asarray(np.concatenate([high, low, high], axis=0))


def halves(values):
    high = values.astype(jnp.bfloat16)
    return high, (values - high.astype(jnp.float32)).astype(jnp.bfloat16)


def from_left(table, values):
    high, low = halves(values)
    stacked = jnp.concatenate([high, low, high], axis=0)
    return jnp.dot(table, stacked, preferred_element_type=jnp.float32)


def from_right(values, table):
    high, low = halves(values)
    joined = jnp.concatenate([high, high, low], axis=1)
    return jnp.dot(joined, table, preferred_element_type=jnp.float32)


def twiddle(real, imag, cos_t, sin_t):
    return real * cos_t + imag * sin_t, imag * cos_t - real * sin_t


def forward(block, fa, cos_t, sin_t, fb):
    outer = from_left(fa, block)
    real, imag = twiddle(outer[:LANES], outer[LANES:], cos_t, sin_t)
    return from_right(jnp.concatenate([real, imag], axis=1), fb)


def run(body, outs, *args, room=8):
    shapes = [jax.ShapeDtypeStruct(shape, jnp.float32) for shape in outs]

    def kernel(*refs):
        results = body(*refs[: len(args)])
        for ref, result in zip(refs[len(args) :], results, strict=True):
            for index, piece in result if isinstance(result, list) else [(..., result)]:
                ref[index] = piece.reshape(ref.shape) if index is ... else piece

    params = pltpu.CompilerParams(vmem_limit_bytes=room << 20) if room else None
    places = [pl.BlockSpec(memory_space=pltpu.SMEM if is_place(arg) else None) for arg in args]
    call = pl.pallas_call(kernel, out_shape=shapes, in_specs=places, compiler_params=params)
    return call(*args)


def is_place(arg):
    return arg.shape == (2,)


def loaded(body):
    return lambda *refs: body(*[ref if is_place(ref) else ref[...] for ref in refs])


def turn_inputs(eta, potential):
    eta_t = eta.T.reshape(16, 8, LANES)
    potential_t = potential.T.reshape(16, 8, LANES)
    return (jnp.concatenate([eta_t, potential_t], axis=1),)


def turn(block):
    return (block.reshape(-1, LANES).T,)


def first_y(both, fa, cos_t, sin_t, fb):
    eta = both[:, :8].reshape(LANES, LANES)
    potential = both[:, 8:].reshape(LANES, LANES)
    return forward(potential, fa, cos_t, sin_t, fb), eta


def magnitude(place, wave_x):
    line = lax.broadcasted_iota(jnp.int32, (LANES, LANES), 0) & 3
    wave_y = wavenumber(place[1] + 64 * place[0] + 16 * line, NYW)
    return jnp.sqrt(wave_x * wave_x + wave_y * wave_y)


def x_stage(powers):
    def multiply(spec, kappa, power):
        factor = kappa
        for _ in range(power - 1):
            factor = factor * kappa
        return spec * (factor * (1.0 / (NXW * NYW)))

    def body(block, place, wave_x, fa, cos_t, sin_t, fb, ib, ia_pair, *older):
        kappa = magnitude(place, wave_x)
        spec = forward(block.reshape(LANES, LANES), fa, cos_t, sin_t, fb)
        other = older[0] if older else spec
        pair = jnp.concatenate(
            [multiply(spec, kappa, powers[0]), multiply(other, kappa, powers[1])], axis=0
        )
        inner = from_right(pair, ib)
        parts = []
        for field in range(2):
            rows = inner[field * LANES : (field + 1) * LANES]
            parts += twiddle(rows[:, :LANES], rows[:, LANES:], cos_t, sin_t)
        return from_left(ia_pair, jnp.concatenate(parts, axis=0)), spec

    return body


def back_y(block, cos_t, sin_t, ib_pair, ia):
    inner = from_right(block.reshape(LANES, 2 * LANES), ib_pair)
    reals, imags = [], []
    for field in range(2):
        part = inner[:, 2 * field * LANES : 2 * (field + 1) * LANES]
        real, imag = twiddle(part[:, :LANES], part[:, LANES:], cos_t, sin_t)
        reals.append(real)
        imags.append(imag)
    stacked = jnp.concatenate(
        [jnp.concatenate(reals, axis=1), jnp.concatenate(imags, axis=1)], axis=0
    )
    fields = from_left(ia, stacked)
    return fields[:, :LANES], fields[:, LANES:]


def second_y(block, eta, fa, cos_t, sin_t, fb, ib_pair, ia):
    slope_one, cubic_one = back_y(block, cos_t, sin_t, ib_pair, ia)
    spectrum = forward(-eta * slope_one, fa, cos_t, sin_t, fb)
    return spectrum, slope_one, cubic_one


def third_y(block, eta, fa, cos_t, sin_t, fb, ib_pair, ia):
    slope_two, curve_one = back_y(block, cos_t, sin_t, ib_pair, ia)
    potential_three = -eta * slope_two - 0.5 * eta * eta * curve_one
    return forward(potential_three, fa, cos_t, sin_t, fb), slope_two, curve_one


def last_y(block, eta, slope_one, cubic_one, slope_two, curve_one, cos_t, sin_t, ib_pair, ia):
    slope_three, curve_two = back_y(block, cos_t, sin_t, ib_pair, ia)
    vertical = (
        slope_one
        + slope_two
        + eta * curve_one
        + slope_three
        + eta * curve_two
        + 0.5 * eta * eta * cubic_one
    )
    return (vertical,)


def swap(values, axis):
    return lax.all_to_all(values, axis, 0, 0, tiled=True)


def beside(values, axis, work, *inputs):
    values, inputs = lax.optimization_barrier((values, inputs))
    moved = swap(values, axis)
    return lax.optimization_barrier((moved, work(*inputs)))


INDEX_X = np.arange(LANES)[:, None] // 4 + 32 * np.arange(LANES)[None, :]
WAVE_X = np.float32(2.0 * math.pi / NXW) * np.minimum(INDEX_X, NXW - INDEX_X).astype(np.float32)


def wave_surface(surface_eta, surface_potential, place, works):
    square = (LANES, LANES)
    turns_y = [f32(TAB_Y["cos_t"]), f32(TAB_Y["sin_t"])]
    turns_x = [f32(TAB_X["cos_t"]), f32(TAB_X["sin_t"])]
    fwd_y = [left_table(TAB_Y["fa"]), *turns_y, right_table(TAB_Y["fb"])]
    inv_y = [right_table(Y_IB_PAIR), left_table(TAB_Y["ia"])]
    tab_x = [
        place,
        f32(WAVE_X),
        left_table(TAB_X["fa"]),
        *turns_x,
        right_table(TAB_X["fb"]),
        right_table(TAB_X["ib"]),
        left_table(X_IA_PAIR),
    ]

    given = ()

    def slab_round(index, values):
        nonlocal given
        work, inputs = works[index]
        values, given = beside(values, "slab", work, given, *inputs)
        return values

    def outward(index, block):
        (turned,) = run(loaded(turn), [square], swap(block.reshape(16, 8, LANES), "pencil"))
        return slab_round(index, turned.reshape(32, 4, LANES)).reshape(square)

    def homeward(index, block):
        (turned,) = run(loaded(turn), [(LANES, 2 * LANES)], slab_round(index, block))
        return swap(turned.reshape(16, 8, 2 * LANES), "pencil")

    pair = (32, 8, LANES)
    (turned,) = run(
        loaded(turn_inputs), [(16, 16, LANES)], surface_eta, surface_potential, room=None
    )
    spectrum, eta = run(loaded(first_y), [square, square], swap(turned, "pencil"), *fwd_y)
    block = outward(0, spectrum)
    block, spec_one = run(loaded(x_stage((1, 3))), [pair, square], block, *tab_x)
    spectrum, slope_one, cubic_one = run(
        loaded(second_y), [square] * 3, homeward(1, block), eta, *fwd_y, *inv_y
    )
    block, spec_two = run(
        loaded(x_stage((1, 2))), [pair, square], outward(2, spectrum), *tab_x, spec_one
    )
    spectrum, slope_two, curve_one = run(
        loaded(third_y), [square] * 3, homeward(3, block), eta, *fwd_y, *inv_y
    )
    block, _ = run(
        loaded(x_stage((1, 2))), [pair, square], outward(4, spectrum), *tab_x, spec_two
    )
    (vertical,) = run(
        loaded(last_y),
        [(16, 8, LANES)],
        homeward(5, block),
        eta,
        slope_one,
        cubic_one,
        slope_two,
        curve_one,
        *turns_y,
        *inv_y,
    )
    return swap(vertical, "pencil").reshape(square), given


def wavenumber(index, length):
    folded = jnp.minimum(index, length - index)
    return 2.0 * math.pi / length * folded.astype(jnp.float32)


def ramp_weight(distance, reach_len):
    ratio = jnp.clip(1.0 - distance / reach_len, 0.0, 1.0)
    return ratio * ratio


def relax_of(cell_x, cell_y):
    pos_x, pos_y = cell_x.astype(jnp.float32), cell_y.astype(jnp.float32)
    reach_x = float(ZONE * CX)
    reach_y = float(CY)
    along_x = jnp.maximum(ramp_weight(pos_x, reach_x), ramp_weight(NX - 1.0 - pos_x, reach_x))
    across = jnp.maximum(ramp_weight(pos_y, reach_y), ramp_weight(NY - 1.0 - pos_y, reach_y))
    in_x = jnp.where((cell_x >= 0) & (cell_x < NX), 1.0, 0.0)
    in_y = jnp.where((cell_y >= 0) & (cell_y < NY), 1.0, 0.0)
    return jnp.maximum(along_x, across), in_x * in_y


def thirds(values):
    terms = []
    for _ in range(3):
        term = values.astype(jnp.bfloat16)
        terms.append(term)
        values = values - term.astype(jnp.float32)
    return jnp.concatenate(terms, axis=1)


def chosen(terms, lanes):
    count = lanes.shape[1]
    iota = lax.broadcasted_iota(jnp.int32, (LANES, count), 0)
    hot = jnp.where(iota == lanes, 1.0, 0.0).astype(jnp.bfloat16)
    picked = jnp.dot(
        terms, jnp.concatenate([hot] * 3, axis=0), preferred_element_type=jnp.float32
    )
    return picked, iota


def listed(columns, points, row_count):
    terms = thirds(columns)
    rows = []
    for i in range(row_count):
        point = points[i : i + 1, :]
        picked, iota = chosen(terms, lax.shift_right_arithmetic(point, 7))
        found = jnp.where(iota == (point & (LANES - 1)), picked, 0.0)
        rows.append(jnp.sum(found, axis=0, keepdims=True))
    return rows


POINT_ROWS = 11


def pick_elevation(eta, points):
    rows = listed(eta[...].T, points, POINT_ROWS)
    return ([(slice(i, i + 1), row) for i, row in enumerate(rows)],)


def pick_vertical(columns, points, eta_rows):
    columns = columns[...]
    rows = listed(columns, points, POINT_ROWS)
    pieces = [((slice(None), slice(None)), jnp.zeros((LANES, LANES), jnp.float32))]

    def put(slab, place, row, half):
        at = slice(half * LANES, (half + 1) * LANES)
        for field, value in enumerate((eta_rows[row : row + 1, at], rows[row][:, at])):
            line = 4 * slab + 2 * place + field
            pieces.append(((slice(line, line + 1), slice(None)), value))

    for row, slab in enumerate((0, 1, 30, 31)):
        for half in range(2):
            put(slab, half, row, half)
    for slab in range(2, 30):
        put(slab, 0, 4 + (slab - 2) // 4, (slab - 2) % 4 // 2)
    return pieces, columns.T


def sample(arrived, place, stencil, weights):
    source, slot = lax.shift_right_logical(stencil[...], 8), stencil[...] & 255
    in_zone = jnp.where((place[0] < ZONE) | (place[0] >= 32 - ZONE), 1, 0)
    lines = 4 * source + 2 * in_zone * lax.shift_right_logical(slot, 7)
    lanes = in_zone * (slot & 127) + (1 - in_zone) * ((slot & 63) + 64 * (place[0] & 1))
    shares = weights[...] / jnp.sum(weights[...], axis=0, keepdims=True)
    terms = thirds(arrived[...])
    totals = [0.0, 0.0]
    for q in range(4):
        picked, iota = chosen(terms, lanes[q : q + 1, :])
        picked = picked * shares[q : q + 1, :]
        line = lines[q : q + 1, :]
        for field in range(2):
            totals[field] = totals[field] + jnp.where(iota == line + field, picked, 0.0)
    rows = [jnp.sum(total, axis=0, keepdims=True) for total in totals]
    return (jnp.concatenate(rows + [jnp.zeros((6, 256), jnp.float32)], axis=0),)


def roll(values, shift, axis):
    return pltpu.roll(values, shift, axis)


def predicted_of(centers, neighbours):
    lane = lax.broadcasted_iota(jnp.int32, centers[0].shape, centers[0].ndim - 1)
    last = centers[0].ndim - 1
    results = []
    for center, (plus_x, minus_x, plus_y, minus_y) in zip(centers, neighbours, strict=True):
        plus_z = jnp.where(lane == CZ - 1, 0.0, roll(center, CZ - 1, last))
        minus_z = jnp.where(lane == 0, 0.0, roll(center, 1, last))
        laplace = plus_x + minus_x + (plus_y + minus_y) + (plus_z + minus_z) - 6.0 * center
        advect = (
            centers[0] * (plus_x - minus_x)
            + centers[1] * (plus_y - minus_y)
            + centers[2] * (plus_z - minus_z)
        )
        results.append(center + TIME_STEP * (VISCOSITY * laplace - 0.5 * advect))
    return results


def first_substep(padded, place, decay):
    (keep, keep_x, keep_y), pulls = relax_fields(place, decay[...])

    def region(x_at, x_to, y_at, y_to):
        def part(c, shift_x, shift_y):
            return padded[c, x_at + shift_x : x_to + shift_x, y_at + shift_y : y_to + shift_y, :]

        steps = ((1, 0), (-1, 0), (0, 1), (0, -1))
        centers = [part(c, 0, 0) for c in range(3)]
        return predicted_of(centers, [[part(c, *step) for step in steps] for c in range(3)])

    own, face_x, face_y = [], [], []
    for c, value in enumerate(region(2, 18, 2, 18)):
        own.append(((c,), value * keep))
    for side, x_at in enumerate((1, 18)):
        for c, value in enumerate(region(x_at, x_at + 1, 2, 18)):
            face_x.append(((c, slice(side, side + 1)), value * keep_x[side : side + 1]))
    for row, y_at in ((0, 1), (15, 18)):
        for c, value in enumerate(region(2, 18, y_at, y_at + 1)):
            where = (slice(None), slice(row, row + 1))
            face_y.append(((c, *where), value * keep_y[:, row : row + 1]))
    return own, face_x, face_y, keep, *pulls


def second_substep(
    own, face_x, face_y, keep, pull, pull_x, pull_y, here, from_up_x, from_down_x, from_up_y, from_down_y
):
    lane = lax.broadcasted_iota(jnp.int32, (8, 256), 1)
    across_y = jnp.where(
        lane % CY == 0, roll(from_down_y[...], 241, 1), roll(from_up_y[...], 15, 1)
    )
    across_x = jnp.where(lane < CY, roll(from_down_x[...], 16, 1), roll(from_up_x[...], 240, 1))
    surface = jnp.concatenate([here[...], across_x, across_y], axis=0).T

    def column(index):
        return surface[:, index : index + 1].reshape(CX, CY, 1)

    shape = (CX, CY, CZ)
    row = lax.broadcasted_iota(jnp.int32, shape, 1)
    centers, neighbours, targets = [], [], []
    for c in range(3):
        center = own[c]
        outer_x = [face_x[c, 0:1], face_x[c, 1:2]]
        outer_y = face_y[c]
        target = None
        if c != 1:
            field = c // 2
            target = pull[...] * column(field)
            center = center + target
            line = column(8 + field)
            outer_x = [
                outer_x[0] + pull_x[0:1] * line[0:1],
                outer_x[1] + pull_x[1:2] * line[CX - 1 : CX],
            ]
            outer_y = outer_y + pull_y[...] * column(16 + field)
        plus_x = jnp.concatenate([center[1:], outer_x[1]], axis=0)
        minus_x = jnp.concatenate([outer_x[0], center[:-1]], axis=0)
        plus_y = jnp.where(row == CY - 1, outer_y, roll(center, CY - 1, 1))
        minus_y = jnp.where(row == 0, outer_y, roll(center, 1, 1))
        centers.append(center)
        neighbours.append((plus_x, minus_x, plus_y, minus_y))
        targets.append(target)
    pieces = []
    for c, value in enumerate(predicted_of(centers, neighbours)):
        value = value * keep[...]
        pieces.append(((c,), value if targets[c] is None else value + targets[c]))
    return (pieces,)


def shifted(values, axis, step):
    size = lax.axis_size(axis)
    pairs = [(i, i + step) for i in range(size) if 0 <= i + step < size]
    return lax.ppermute(values, axis, pairs)


def list_points(send_point, send_count):
    slot = lax.broadcasted_iota(jnp.int32, (32, 256), 1)
    points = jnp.where(slot < send_count[0, 0][:, None], send_point[0, 0], -1)
    inner = points[2:30, :64].reshape(7, 256)
    return jnp.concatenate([points[:2], points[30:], inner], axis=0)


DECAY = np.exp(-DEPTH_RATE * (CZ - 1.0 - np.arange(CZ)) / CZ).astype(np.float32)


def relax_fields(place, decay):
    def fields(cell_x, cell_y):
        relax, inside = relax_of(cell_x, cell_y)
        return (1.0 - relax) * inside, relax * inside * decay.reshape(1, 1, CZ)

    side = lax.broadcasted_iota(jnp.int32, (2, 1, CZ), 0)
    row = lax.broadcasted_iota(jnp.int32, (1, CY, CZ), 1)
    cell_x = place[0] * CX + lax.broadcasted_iota(jnp.int32, (CX, 1, CZ), 0)
    cell_y = place[1] * CY + row
    out_x = place[0] * CX - 1 + (CX + 1) * side
    out_y = cell_y + jnp.where(row == 0, -1, jnp.where(row == CY - 1, 1, 0))
    own, across_x, across_y = fields(cell_x, cell_y), fields(out_x, cell_y), fields(cell_x, out_y)
    return (own[0], across_x[0], across_y[0]), (own[1], across_x[1], across_y[1])


def flat_stencil(stencil, interp_weight):
    return stencil.reshape(4, CX * CY), interp_weight.reshape(4, CX * CY)


def on_device(
    surface_eta, surface_potential, velocity, send_point, send_count, stencil, interp_weight
):
    place = jnp.stack([lax.axis_index("slab"), lax.axis_index("pencil")])
    surface_eta, place = lax.optimization_barrier((surface_eta, place))
    square = (LANES, LANES)
    block = (3, CX, CY, CZ)
    face = (2, CY, CZ)

    def send(values, axis, dim, step):
        length = values.shape[dim]
        start = length - 2 if step > 0 else 0
        return shifted(lax.slice_in_dim(values, start, start + 2, axis=dim), axis, step)

    def first(given, velocity):
        return send(velocity, "slab", 1, 1)

    def second(given, velocity):
        return given, send(velocity, "slab", 1, -1)

    def third(given, velocity):
        joined = jnp.concatenate([given[0], velocity, given[1]], axis=1)
        return joined, send(joined, "pencil", 2, 1)

    def fourth(given):
        return *given, send(given[0], "pencil", 2, -1)

    def fifth(given, place):
        joined, before, after = given
        padded = jnp.concatenate([before, joined, after], axis=2)
        shapes = [block, (3, *face), block, block[1:], block[1:], face, block[1:]]
        return run(first_substep, shapes, padded, place, jnp.asarray(DECAY[None]))

    def sixth(given, eta, send_point, send_count):
        points = list_points(send_point, send_count)
        return given, points, run(pick_elevation, [(POINT_ROWS, 256)], eta, points)[0]

    works = (
        (first, (velocity,)),
        (second, (velocity,)),
        (third, (velocity,)),
        (fourth, ()),
        (fifth, (place,)),
        (sixth, (surface_eta, send_point, send_count)),
    )
    columns, (ahead, points, eta_rows) = wave_surface(
        surface_eta, surface_potential, place, works
    )
    outgoing, vertical = run(pick_vertical, [square, square], columns, points, eta_rows)
    arrived, sampling = beside(
        outgoing.reshape(32, 4, LANES),
        "slab",
        flat_stencil,
        stencil,
        interp_weight,
    )
    arrived = arrived.reshape(square)
    (here,) = run(sample, [(8, 256)], arrived, place, *sampling)
    neighbours = [shifted(here, axis, step) for axis in ("slab", "pencil") for step in (-1, 1)]
    (velocity,) = run(second_substep, [block], *ahead, here, *neighbours)
    return (vertical, velocity)


def solution(mesh):
    in_specs = (
        P("pencil", "slab"),
        P("pencil", "slab"),
        P(None, "slab", "pencil", None),
        P("slab", "pencil", None, None),
        P("slab", "pencil", None),
        P(None, "slab", "pencil"),
        P(None, "slab", "pencil"),
    )
    out_specs = (P("pencil", "slab"), P(None, "slab", "pencil", None))
    return jax.shard_map(
        on_device, mesh=mesh, in_specs=in_specs, out_specs=out_specs, check_vma=False
    )
```

```python
import math

import jax
import jax.numpy as jnp
import ml_dtypes
import numpy as np
from jax import lax
from jax.experimental import pallas as pl
from jax.experimental.pallas import tpu as pltpu
from jax.sharding import PartitionSpec as P

NXW = 4096
NYW = 2048
LANES = 128
CX = 16
CY = 16
CZ = 128
NX = 512
NY = 256
ZONE = 2

TIME_STEP = 0.2
VISCOSITY = 0.6
DEPTH_RATE = 3.0


def stage_tables(peers):
    copies = LANES // peers
    length = peers * LANES
    outer = np.arange(peers)
    inner = np.arange(LANES)
    eye = np.eye(copies)
    angle_a = 2.0 * np.pi / peers * (outer[:, None] * outer[None, :] % peers)
    angle_t = 2.0 * np.pi / length * (outer[:, None] * inner[None, :] % length)
    angle_b = 2.0 * np.pi / LANES * (inner[:, None] * inner[None, :] % LANES)
    cos_a, sin_a = np.kron(np.cos(angle_a), eye), np.kron(np.sin(angle_a), eye)
    cos_b, sin_b = np.cos(angle_b), np.sin(angle_b)
    tables = {
        "fa": np.concatenate([cos_a, -sin_a], axis=0),
        "cos_t": np.repeat(np.cos(angle_t), copies, axis=0),
        "sin_t": np.repeat(np.sin(angle_t), copies, axis=0),
        "fb": np.concatenate([cos_b + sin_b, sin_b - cos_b], axis=0),
        "ib": np.concatenate([cos_b, -sin_b], axis=1),
        "ia": np.concatenate([cos_a + sin_a, sin_a - cos_a], axis=1),
    }
    return tables


TAB_Y = stage_tables(16)
TAB_X = stage_tables(32)


def pair_inverse_b(ib):
    rows = ib.reshape(32, 4, 2 * LANES)
    big = np.zeros((32, 2, 4, 2, 2 * LANES))
    for field in range(2):
        big[:, field, :, field, :] = rows
    return big.reshape(2 * LANES, 4 * LANES)


def pair_inverse_a(ia):
    rows = ia.reshape(32, 4, 2 * LANES)
    big = np.zeros((32, 2, 4, 2, 2 * LANES))
    for field in range(2):
        big[:, field, :, field, :] = rows
    return big.reshape(2 * LANES, 4 * LANES)


Y_IB_PAIR = pair_inverse_b(TAB_Y["ib"])
X_IA_PAIR = pair_inverse_a(TAB_X["ia"])


def f32(array):
    return jnp.asarray(np.asarray(array, np.float32))


def halves_of(table):
    high = table.astype(ml_dtypes.bfloat16)
    return high, (table - high.astype(np.float64)).astype(ml_dtypes.bfloat16)


def left_table(table):
    high, low = halves_of(table)
    return jnp.asarray(np.concatenate([high, high, low], axis=1))


def right_table(table):
    high, low = halves_of(table)
    return jnp.asarray(np.concatenate([high, low, high], axis=0))


def halves(values):
    high = values.astype(jnp.bfloat16)
    return high, (values - high.astype(jnp.float32)).astype(jnp.bfloat16)


def from_left(table, values):
    high, low = halves(values)
    stacked = jnp.concatenate([high, low, high], axis=0)
    return jnp.dot(table, stacked, preferred_element_type=jnp.float32)


def from_right(values, table):
    high, low = halves(values)
    joined = jnp.concatenate([high, high, low], axis=1)
    return jnp.dot(joined, table, preferred_element_type=jnp.float32)


def twiddle(real, imag, cos_t, sin_t):
    return real * cos_t + imag * sin_t, imag * cos_t - real * sin_t


def forward(block, fa, cos_t, sin_t, fb):
    outer = from_left(fa, block)
    real, imag = twiddle(outer[:LANES], outer[LANES:], cos_t, sin_t)
    return from_right(jnp.concatenate([real, imag], axis=1), fb)


def run(body, outs, *args, room=8):
    shapes = [jax.ShapeDtypeStruct(shape, jnp.float32) for shape in outs]

    def kernel(*refs):
        results = body(*refs[: len(args)])
        for ref, result in zip(refs[len(args) :], results, strict=True):
            for index, piece in result if isinstance(result, list) else [(..., result)]:
                ref[index] = piece.reshape(ref.shape) if index is ... else piece

    params = pltpu.CompilerParams(vmem_limit_bytes=room << 20) if room else None
    places = [pl.BlockSpec(memory_space=pltpu.SMEM if is_place(arg) else None) for arg in args]
    call = pl.pallas_call(kernel, out_shape=shapes, in_specs=places, compiler_params=params)
    return call(*args)


def is_place(arg):
    return arg.shape == (2,)


def loaded(body):
    return lambda *refs: body(*[ref if is_place(ref) else ref[...] for ref in refs])


def turn_inputs(eta, potential):
    eta_t = eta.T.reshape(16, 8, LANES)
    potential_t = potential.T.reshape(16, 8, LANES)
    return (jnp.concatenate([eta_t, potential_t], axis=1),)


def turn(block):
    return (block.reshape(-1, LANES).T,)


def first_y(both, fa, cos_t, sin_t, fb):
    eta = both[:, :8].reshape(LANES, LANES)
    potential = both[:, 8:].reshape(LANES, LANES)
    return forward(potential, fa, cos_t, sin_t, fb), eta


def magnitude(place, wave_x):
    line = lax.broadcasted_iota(jnp.int32, (LANES, LANES), 0) & 3
    wave_y = wavenumber(place[1] + 64 * place[0] + 16 * line, NYW)
    return jnp.sqrt(wave_x * wave_x + wave_y * wave_y)


def x_stage(powers):
    def multiply(spec, kappa, power):
        factor = kappa
        for _ in range(power - 1):
            factor = factor * kappa
        return spec * (factor * (1.0 / (NXW * NYW)))

    def body(block, place, wave_x, fa, cos_t, sin_t, fb, ib, ia_pair, *older):
        kappa = magnitude(place, wave_x)
        spec = forward(block.reshape(LANES, LANES), fa, cos_t, sin_t, fb)
        other = older[0] if older else spec
        pair = jnp.concatenate(
            [multiply(spec, kappa, powers[0]), multiply(other, kappa, powers[1])], axis=0
        )
        inner = from_right(pair, ib)
        parts = []
        for field in range(2):
            rows = inner[field * LANES : (field + 1) * LANES]
            parts += twiddle(rows[:, :LANES], rows[:, LANES:], cos_t, sin_t)
        return from_left(ia_pair, jnp.concatenate(parts, axis=0)), spec

    return body


def back_y(block, cos_t, sin_t, ib_pair, ia):
    inner = from_right(block.reshape(LANES, 2 * LANES), ib_pair)
    reals, imags = [], []
    for field in range(2):
        part = inner[:, 2 * field * LANES : 2 * (field + 1) * LANES]
        real, imag = twiddle(part[:, :LANES], part[:, LANES:], cos_t, sin_t)
        reals.append(real)
        imags.append(imag)
    stacked = jnp.concatenate(
        [jnp.concatenate(reals, axis=1), jnp.concatenate(imags, axis=1)], axis=0
    )
    fields = from_left(ia, stacked)
    return fields[:, :LANES], fields[:, LANES:]


def second_y(block, eta, fa, cos_t, sin_t, fb, ib_pair, ia):
    slope_one, cubic_one = back_y(block, cos_t, sin_t, ib_pair, ia)
    spectrum = forward(-eta * slope_one, fa, cos_t, sin_t, fb)
    return spectrum, slope_one, cubic_one


def third_y(block, eta, fa, cos_t, sin_t, fb, ib_pair, ia):
    slope_two, curve_one = back_y(block, cos_t, sin_t, ib_pair, ia)
    potential_three = -eta * slope_two - 0.5 * eta * eta * curve_one
    return forward(potential_three, fa, cos_t, sin_t, fb), slope_two, curve_one


def last_y(block, eta, slope_one, cubic_one, slope_two, curve_one, cos_t, sin_t, ib_pair, ia):
    slope_three, curve_two = back_y(block, cos_t, sin_t, ib_pair, ia)
    vertical = (
        slope_one
        + slope_two
        + eta * curve_one
        + slope_three
        + eta * curve_two
        + 0.5 * eta * eta * cubic_one
    )
    return (vertical,)


def swap(values, axis):
    return lax.all_to_all(values, axis, 0, 0, tiled=True)


def beside(values, axis, work, *inputs):
    values, inputs = lax.optimization_barrier((values, inputs))
    moved = swap(values, axis)
    return lax.optimization_barrier((moved, work(*inputs)))


INDEX_X = np.arange(LANES)[:, None] // 4 + 32 * np.arange(LANES)[None, :]
WAVE_X = np.float32(2.0 * math.pi / NXW) * np.minimum(INDEX_X, NXW - INDEX_X).astype(np.float32)


def wave_surface(surface_eta, surface_potential, place, works):
    square = (LANES, LANES)
    turns_y = [f32(TAB_Y["cos_t"]), f32(TAB_Y["sin_t"])]
    turns_x = [f32(TAB_X["cos_t"]), f32(TAB_X["sin_t"])]
    fwd_y = [left_table(TAB_Y["fa"]), *turns_y, right_table(TAB_Y["fb"])]
    inv_y = [right_table(Y_IB_PAIR), left_table(TAB_Y["ia"])]
    tab_x = [
        place,
        f32(WAVE_X),
        left_table(TAB_X["fa"]),
        *turns_x,
        right_table(TAB_X["fb"]),
        right_table(TAB_X["ib"]),
        left_table(X_IA_PAIR),
    ]

    given = ()

    def slab_round(index, values):
        nonlocal given
        if index >= len(works):
            return swap(values, "slab")
        work, inputs = works[index]
        values, given = beside(values, "slab", work, given, *inputs)
        return values

    def outward(index, block):
        (turned,) = run(loaded(turn), [square], swap(block.reshape(16, 8, LANES), "pencil"))
        return slab_round(index, turned.reshape(32, 4, LANES)).reshape(square)

    def homeward(index, block):
        (turned,) = run(loaded(turn), [(LANES, 2 * LANES)], slab_round(index, block))
        return swap(turned.reshape(16, 8, 2 * LANES), "pencil")

    pair = (32, 8, LANES)
    (turned,) = run(
        loaded(turn_inputs), [(16, 16, LANES)], surface_eta, surface_potential, room=None
    )
    spectrum, eta = run(loaded(first_y), [square, square], swap(turned, "pencil"), *fwd_y)
    block = outward(0, spectrum)
    block, spec_one = run(loaded(x_stage((1, 3))), [pair, square], block, *tab_x)
    spectrum, slope_one, cubic_one = run(
        loaded(second_y), [square] * 3, homeward(1, block), eta, *fwd_y, *inv_y
    )
    block, spec_two = run(
        loaded(x_stage((1, 2))), [pair, square], outward(2, spectrum), *tab_x, spec_one
    )
    spectrum, slope_two, curve_one = run(
        loaded(third_y), [square] * 3, homeward(3, block), eta, *fwd_y, *inv_y
    )
    block, _ = run(
        loaded(x_stage((1, 2))), [pair, square], outward(4, spectrum), *tab_x, spec_two
    )
    (vertical,) = run(
        loaded(last_y),
        [(16, 8, LANES)],
        homeward(5, block),
        eta,
        slope_one,
        cubic_one,
        slope_two,
        curve_one,
        *turns_y,
        *inv_y,
    )
    return swap(vertical, "pencil").reshape(square), given


def wavenumber(index, length):
    folded = jnp.minimum(index, length - index)
    return 2.0 * math.pi / length * folded.astype(jnp.float32)


def ramp_weight(distance, reach_len):
    ratio = jnp.clip(1.0 - distance / reach_len, 0.0, 1.0)
    return ratio * ratio


def relax_of(cell_x, cell_y):
    pos_x, pos_y = cell_x.astype(jnp.float32), cell_y.astype(jnp.float32)
    reach_x = float(ZONE * CX)
    reach_y = float(CY)
    along_x = jnp.maximum(ramp_weight(pos_x, reach_x), ramp_weight(NX - 1.0 - pos_x, reach_x))
    across = jnp.maximum(ramp_weight(pos_y, reach_y), ramp_weight(NY - 1.0 - pos_y, reach_y))
    in_x = jnp.where((cell_x >= 0) & (cell_x < NX), 1.0, 0.0)
    in_y = jnp.where((cell_y >= 0) & (cell_y < NY), 1.0, 0.0)
    return jnp.maximum(along_x, across), in_x * in_y


def thirds(values):
    terms = []
    for _ in range(3):
        term = values.astype(jnp.bfloat16)
        terms.append(term)
        values = values - term.astype(jnp.float32)
    return jnp.concatenate(terms, axis=1)


def chosen(terms, lanes):
    count, parts = lanes.shape[1], terms.shape[1] // LANES
    iota = lax.broadcasted_iota(jnp.int32, (LANES, count), 0)
    hot = jnp.where(iota == lanes, 1.0, 0.0).astype(jnp.bfloat16)
    picked = jnp.dot(
        terms, jnp.concatenate([hot] * parts, axis=0), preferred_element_type=jnp.float32
    )
    return picked, lax.broadcasted_iota(jnp.int32, picked.shape, 0)


def listed(columns, points, row_count):
    terms = thirds(columns)
    rows = []
    for i in range(row_count):
        point = points[i : i + 1, :]
        picked, iota = chosen(terms, lax.shift_right_arithmetic(point, 7))
        found = jnp.where(iota == (point & (LANES - 1)), picked, 0.0)
        rows.append(jnp.sum(found, axis=0, keepdims=True))
    return rows


POINT_ROWS = 11


def pick_elevation(eta, points):
    rows = listed(eta[...].T, points, POINT_ROWS)
    return ([(slice(i, i + 1), row) for i, row in enumerate(rows)],)


def pick_vertical(columns, points, eta_rows):
    columns = columns[...]
    rows = listed(columns, points, POINT_ROWS)
    pieces = [((slice(None), slice(None)), jnp.zeros((3 * LANES, LANES), jnp.float32))]

    def put(slab, place, row, half):
        at = slice(half * LANES, (half + 1) * LANES)
        for field, value in enumerate((eta_rows[row : row + 1, at], rows[row][:, at])):
            for block in range(3):
                line = 12 * (slab + 1 - block) + 4 * block + 2 * place + field
                if 0 <= line < 3 * LANES:
                    pieces.append(((slice(line, line + 1), slice(None)), value))

    for row, slab in enumerate((0, 1, 30, 31)):
        for half in range(2):
            put(slab, half, row, half)
    for slab in range(2, 30):
        put(slab, 0, 4 + (slab - 2) // 4, (slab - 2) % 4 // 2)
    return pieces, columns.T


def slots_of(stencil, slab, block):
    source, slot = lax.shift_right_logical(stencil, 8), stencil & 255
    in_zone = jnp.where((slab < ZONE) | (slab >= 32 - ZONE), 1, 0)
    lines = 12 * source + 4 * block + 2 * in_zone * lax.shift_right_logical(slot, 7)
    lanes = in_zone * (slot & 127) + (1 - in_zone) * ((slot & 63) + 64 * (slab & 1))
    return lines, lanes


def both_fields(terms, lines, lanes, shares):
    picked, iota = chosen(terms, lanes)
    picked = picked * shares
    return [jnp.where(iota == lines + field, picked, 0.0) for field in range(2)]


def summed(values):
    return jnp.sum(values, axis=0, keepdims=True)


def over_q(values):
    values = values + roll(values, 64, 1)
    return values + roll(values, 32, 1)


def sample(arrived, place, stencil, weights, from_low, from_high):
    slab = place[0]
    terms = thirds(arrived[...])[:, : 2 * LANES]
    lines, lanes = slots_of(stencil[...], slab, 1)
    shares = weights[...] / jnp.sum(weights[...], axis=0, keepdims=True)
    totals = [0.0, 0.0]
    for q in range(4):
        at = slice(q, q + 1)
        found = both_fields(terms, lines[at], lanes[at], shares[at])
        totals = [total + part for total, part in zip(totals, found, strict=True)]
    rows = [summed(total) for total in totals]

    lane = lax.broadcasted_iota(jnp.int32, (8, LANES), 1)
    side = lax.shift_right_logical(lane, 4) & 1
    beside_x = from_low[...] + from_high[...]
    points, weight = in_lanes(beside_x[0:8], lane), in_lanes(beside_x[8:16], lane)
    lines, lanes = slots_of(points.astype(jnp.int32), slab - 1 + 2 * side, 2 * side)
    total = over_q(weight)
    shares = weight / jnp.where(total > 0.0, total, 1.0)
    for part in both_fields(terms, lines[0:1], lanes[0:1], shares[0:1]):
        value = over_q(jnp.broadcast_to(summed(part), (8, LANES)))[0:1]
        rows.append(jnp.concatenate([value, value], axis=1))
    return (jnp.concatenate(rows + [jnp.zeros((4, 256), jnp.float32)], axis=0),)


def in_lanes(values, lane):
    result = jnp.zeros(values.shape, jnp.float32)
    for q in range(4):
        moved = jnp.broadcast_to(values[q : q + 1], values.shape)
        if q:
            moved = roll(moved, 32 * q, 1)
        result = jnp.where(lax.shift_right_logical(lane, 5) == q, moved, result)
    return result


def roll(values, shift, axis):
    return pltpu.roll(values, shift, axis)


def predicted_of(centers, neighbours):
    lane = lax.broadcasted_iota(jnp.int32, centers[0].shape, centers[0].ndim - 1)
    last = centers[0].ndim - 1
    results = []
    for center, (plus_x, minus_x, plus_y, minus_y) in zip(centers, neighbours, strict=True):
        plus_z = jnp.where(lane == CZ - 1, 0.0, roll(center, CZ - 1, last))
        minus_z = jnp.where(lane == 0, 0.0, roll(center, 1, last))
        laplace = plus_x + minus_x + (plus_y + minus_y) + (plus_z + minus_z) - 6.0 * center
        advect = (
            centers[0] * (plus_x - minus_x)
            + centers[1] * (plus_y - minus_y)
            + centers[2] * (plus_z - minus_z)
        )
        results.append(center + TIME_STEP * (VISCOSITY * laplace - 0.5 * advect))
    return results


def first_substep(padded, place, decay):
    (keep, keep_x, keep_y), pulls = relax_fields(place, decay[...])

    def region(x_at, x_to, y_at, y_to):
        def part(c, shift_x, shift_y):
            return padded[c, x_at + shift_x : x_to + shift_x, y_at + shift_y : y_to + shift_y, :]

        steps = ((1, 0), (-1, 0), (0, 1), (0, -1))
        centers = [part(c, 0, 0) for c in range(3)]
        return predicted_of(centers, [[part(c, *step) for step in steps] for c in range(3)])

    own, face_x, face_y = [], [], []
    for c, value in enumerate(region(2, 18, 2, 18)):
        own.append(((c,), value * keep))
    for side, x_at in enumerate((1, 18)):
        for c, value in enumerate(region(x_at, x_at + 1, 2, 18)):
            face_x.append(((c, slice(side, side + 1)), value * keep_x[side : side + 1]))
    for row, y_at in ((0, 1), (15, 18)):
        for c, value in enumerate(region(2, 18, y_at, y_at + 1)):
            where = (slice(None), slice(row, row + 1))
            face_y.append(((c, *where), value * keep_y[:, row : row + 1]))
    return own, face_x, face_y, keep, *pulls


def second_substep(
    own, face_x, face_y, keep, pull, pull_x, pull_y, here, from_up_y, from_down_y
):
    lane = lax.broadcasted_iota(jnp.int32, (8, 256), 1)
    across_y = jnp.where(
        lane % CY == 0, roll(from_down_y[...], 241, 1), roll(from_up_y[...], 15, 1)
    )
    surface = jnp.concatenate([here[...], across_y], axis=0).T

    def column(index):
        return surface[:, index : index + 1].reshape(CX, CY, 1)

    shape = (CX, CY, CZ)
    row = lax.broadcasted_iota(jnp.int32, shape, 1)
    centers, neighbours, targets = [], [], []
    for c in range(3):
        center = own[c]
        outer_x = [face_x[c, 0:1], face_x[c, 1:2]]
        outer_y = face_y[c]
        target = None
        if c != 1:
            field = c // 2
            target = pull[...] * column(field)
            center = center + target
            line = column(2 + field)
            outer_x = [
                outer_x[0] + pull_x[0:1] * line[0:1],
                outer_x[1] + pull_x[1:2] * line[CX - 1 : CX],
            ]
            outer_y = outer_y + pull_y[...] * column(8 + field)
        plus_x = jnp.concatenate([center[1:], outer_x[1]], axis=0)
        minus_x = jnp.concatenate([outer_x[0], center[:-1]], axis=0)
        plus_y = jnp.where(row == CY - 1, outer_y, roll(center, CY - 1, 1))
        minus_y = jnp.where(row == 0, outer_y, roll(center, 1, 1))
        centers.append(center)
        neighbours.append((plus_x, minus_x, plus_y, minus_y))
        targets.append(target)
    pieces = []
    for c, value in enumerate(predicted_of(centers, neighbours)):
        value = value * keep[...]
        pieces.append(((c,), value if targets[c] is None else value + targets[c]))
    return (pieces,)


def shifted(values, axis, step):
    size = lax.axis_size(axis)
    pairs = [(i, i + step) for i in range(size) if 0 <= i + step < size]
    return lax.ppermute(values, axis, pairs)


def list_points(send_point, send_count):
    slot = lax.broadcasted_iota(jnp.int32, (32, 256), 1)
    points = jnp.where(slot < send_count[0, 0][:, None], send_point[0, 0], -1)
    inner = points[2:30, :64].reshape(7, 256)
    return jnp.concatenate([points[:2], points[30:], inner], axis=0)


DECAY = np.exp(-DEPTH_RATE * (CZ - 1.0 - np.arange(CZ)) / CZ).astype(np.float32)


def relax_fields(place, decay):
    def fields(cell_x, cell_y):
        relax, inside = relax_of(cell_x, cell_y)
        return (1.0 - relax) * inside, relax * inside * decay.reshape(1, 1, CZ)

    side = lax.broadcasted_iota(jnp.int32, (2, 1, CZ), 0)
    row = lax.broadcasted_iota(jnp.int32, (1, CY, CZ), 1)
    cell_x = place[0] * CX + lax.broadcasted_iota(jnp.int32, (CX, 1, CZ), 0)
    cell_y = place[1] * CY + row
    out_x = place[0] * CX - 1 + (CX + 1) * side
    out_y = cell_y + jnp.where(row == 0, -1, jnp.where(row == CY - 1, 1, 0))
    own, across_x, across_y = fields(cell_x, cell_y), fields(out_x, cell_y), fields(cell_x, out_y)
    return (own[0], across_x[0], across_y[0]), (own[1], across_x[1], across_y[1])


def flat_stencil(stencil, interp_weight):
    return stencil.reshape(4, CX * CY), interp_weight.reshape(4, CX * CY)


def on_device(
    surface_eta, surface_potential, velocity, send_point, send_count, stencil, interp_weight
):
    place = jnp.stack([lax.axis_index("slab"), lax.axis_index("pencil")])
    surface_eta, place = lax.optimization_barrier((surface_eta, place))
    square = (LANES, LANES)
    block = (3, CX, CY, CZ)
    face = (2, CY, CZ)

    def send_x(velocity, stencil, interp_weight, step):
        start, edge, side = (CX - 2, CX - 1, 0) if step > 0 else (0, 0, 1)
        layers = lax.slice_in_dim(velocity, start, start + 2, axis=1).reshape(6, CY, CZ)
        ends = (stencil[:, edge].astype(jnp.float32), interp_weight[:, edge])
        spare = ((0, 4), (CY * side, LANES - CY - CY * side))
        lines = jnp.concatenate([jnp.pad(end, spare) for end in ends], axis=0)
        return shifted(jnp.concatenate([layers, lines[None]], axis=0), "slab", step)

    def send_y(joined, step):
        start = CY - 2 if step > 0 else 0
        return shifted(lax.slice_in_dim(joined, start, start + 2, axis=2), "pencil", step)

    def first(given, *inputs):
        return [send_x(*inputs, step) for step in (1, -1)]

    def second(given, velocity):
        low, high = [sent[:6].reshape(3, 2, CY, CZ) for sent in given]
        joined = jnp.concatenate([low, velocity, high], axis=1)
        return joined, [send_y(joined, step) for step in (1, -1)], [sent[6] for sent in given]

    def third(given, eta, send_point, send_count, stencil, interp_weight):
        points = list_points(send_point, send_count)
        rows = run(pick_elevation, [(POINT_ROWS, 256)], eta, points)[0]
        return given, points, rows, flat_stencil(stencil, interp_weight)

    works = (
        (first, (velocity, stencil, interp_weight)),
        (second, (velocity,)),
        (third, (surface_eta, send_point, send_count, stencil, interp_weight)),
    )
    columns, (halo, points, eta_rows, flat) = wave_surface(
        surface_eta, surface_potential, place, works
    )
    joined, (low, high), beside_x = halo
    outgoing, vertical = run(
        pick_vertical, [(3 * LANES, LANES), square], columns, points, eta_rows
    )
    arrived = swap(outgoing.reshape(32, 3, 4, LANES), "slab").reshape(3 * LANES, LANES)
    (here,) = run(sample, [(8, 256)], arrived, place, *flat, *beside_x)
    here, (low, joined, high) = lax.optimization_barrier((here, (low, joined, high)))
    neighbours = [shifted(here, "pencil", step) for step in (-1, 1)]
    padded = jnp.concatenate([low, joined, high], axis=2)
    shapes = [block, (3, *face), block, block[1:], block[1:], face, block[1:]]
    ahead = run(first_substep, shapes, padded, place, jnp.asarray(DECAY[None]))
    (velocity,) = run(second_substep, [block], *ahead, here, *neighbours)
    return (vertical, velocity)


def solution(mesh):
    in_specs = (
        P("pencil", "slab"),
        P("pencil", "slab"),
        P(None, "slab", "pencil", None),
        P("slab", "pencil", None, None),
        P("slab", "pencil", None),
        P(None, "slab", "pencil"),
        P(None, "slab", "pencil"),
    )
    out_specs = (P("pencil", "slab"), P(None, "slab", "pencil", None))
    return jax.shard_map(
        on_device, mesh=mesh, in_specs=in_specs, out_specs=out_specs, check_vma=False
    )
```

```python
import math

import jax
import jax.numpy as jnp
import ml_dtypes
import numpy as np
from jax import lax
from jax.experimental import pallas as pl
from jax.experimental.pallas import tpu as pltpu
from jax.sharding import PartitionSpec as P

NXW = 4096
NYW = 2048
LANES = 128
CX = 16
CY = 16
CZ = 128
NX = 512
NY = 256
ZONE = 2

TIME_STEP = 0.2
VISCOSITY = 0.6
DEPTH_RATE = 3.0


def stage_tables(peers):
    copies = LANES // peers
    length = peers * LANES
    outer = np.arange(peers)
    inner = np.arange(LANES)
    eye = np.eye(copies)
    angle_a = 2.0 * np.pi / peers * (outer[:, None] * outer[None, :] % peers)
    angle_t = 2.0 * np.pi / length * (outer[:, None] * inner[None, :] % length)
    angle_b = 2.0 * np.pi / LANES * (inner[:, None] * inner[None, :] % LANES)
    cos_a, sin_a = np.kron(np.cos(angle_a), eye), np.kron(np.sin(angle_a), eye)
    cos_b, sin_b = np.cos(angle_b), np.sin(angle_b)
    tables = {
        "fa": np.concatenate([cos_a, -sin_a], axis=0),
        "cos_t": np.repeat(np.cos(angle_t), copies, axis=0),
        "sin_t": np.repeat(np.sin(angle_t), copies, axis=0),
        "fb": np.concatenate([cos_b + sin_b, sin_b - cos_b], axis=0),
        "ib": np.concatenate([cos_b, -sin_b], axis=1),
        "ia": np.concatenate([cos_a + sin_a, sin_a - cos_a], axis=1),
    }
    return tables


TAB_Y = stage_tables(16)
TAB_X = stage_tables(32)


def pair_inverse_b(ib):
    rows = ib.reshape(32, 4, 2 * LANES)
    big = np.zeros((32, 2, 4, 2, 2 * LANES))
    for field in range(2):
        big[:, field, :, field, :] = rows
    return big.reshape(2 * LANES, 4 * LANES)


def pair_inverse_a(ia):
    rows = ia.reshape(32, 4, 2 * LANES)
    big = np.zeros((32, 2, 4, 2, 2 * LANES))
    for field in range(2):
        big[:, field, :, field, :] = rows
    return big.reshape(2 * LANES, 4 * LANES)


Y_IB_PAIR = pair_inverse_b(TAB_Y["ib"])
X_IA_PAIR = pair_inverse_a(TAB_X["ia"])


def f32(array):
    return jnp.asarray(np.asarray(array, np.float32))


def halves_of(table):
    high = table.astype(ml_dtypes.bfloat16)
    return high, (table - high.astype(np.float64)).astype(ml_dtypes.bfloat16)


def left_table(table):
    high, low = halves_of(table)
    return jnp.asarray(np.concatenate([high, high, low], axis=1))


def right_table(table):
    high, low = halves_of(table)
    return jnp.asarray(np.concatenate([high, low, high], axis=0))


def halves(values):
    high = values.astype(jnp.bfloat16)
    return high, (values - high.astype(jnp.float32)).astype(jnp.bfloat16)


def from_left(table, values):
    high, low = halves(values)
    stacked = jnp.concatenate([high, low, high], axis=0)
    return jnp.dot(table, stacked, preferred_element_type=jnp.float32)


def from_right(values, table):
    high, low = halves(values)
    joined = jnp.concatenate([high, high, low], axis=1)
    return jnp.dot(joined, table, preferred_element_type=jnp.float32)


def twiddle(real, imag, cos_t, sin_t):
    return real * cos_t + imag * sin_t, imag * cos_t - real * sin_t


def forward(block, fa, cos_t, sin_t, fb):
    outer = from_left(fa, block)
    real, imag = twiddle(outer[:LANES], outer[LANES:], cos_t, sin_t)
    return from_right(jnp.concatenate([real, imag], axis=1), fb)


def run(body, outs, *args, room=8, scratch=()):
    shapes = [jax.ShapeDtypeStruct(shape, jnp.float32) for shape in outs]

    def kernel(*refs):
        inputs, rest = refs[: len(args)], refs[len(args) :]
        results = body(*inputs, *rest[len(outs) :])
        for ref, result in zip(rest[: len(outs)], results, strict=True):
            for index, piece in result if isinstance(result, list) else [(..., result)]:
                ref[index] = piece.reshape(ref.shape) if index is ... else piece

    params = pltpu.CompilerParams(vmem_limit_bytes=room << 20) if room else None
    places = [pl.BlockSpec(memory_space=pltpu.SMEM if is_place(arg) else None) for arg in args]
    call = pl.pallas_call(
        kernel,
        out_shape=shapes,
        in_specs=places,
        scratch_shapes=[pltpu.VMEM(shape, jnp.float32) for shape in scratch],
        compiler_params=params,
    )
    return call(*args)


def is_place(arg):
    return arg.shape == (2,)


def loaded(body):
    return lambda *refs: body(*[ref if is_place(ref) else ref[...] for ref in refs])


def turn_inputs(eta, potential):
    eta_t = eta.T.reshape(16, 8, LANES)
    potential_t = potential.T.reshape(16, 8, LANES)
    return (jnp.concatenate([eta_t, potential_t], axis=1),)


def turn(block):
    return (block.reshape(-1, LANES).T,)


def turn_fields(block):
    return (block[:, 0:8].reshape(-1, LANES).T,)


def first_y(both, fa, cos_t, sin_t, fb):
    eta = both[:, :8].reshape(LANES, LANES)
    potential = both[:, 8:].reshape(LANES, LANES)
    return forward(potential, fa, cos_t, sin_t, fb), eta


def magnitude(place, wave_x):
    line = lax.broadcasted_iota(jnp.int32, (LANES, LANES), 0) & 3
    wave_y = wavenumber(place[1] + 64 * place[0] + 16 * line, NYW)
    return jnp.sqrt(wave_x * wave_x + wave_y * wave_y)


def x_stage(powers, extra=None):
    def multiply(spec, kappa, power):
        factor = kappa
        for _ in range(power - 1):
            factor = factor * kappa
        return spec * (factor * (1.0 / (NXW * NYW)))

    def body(block, place, wave_x, fa, cos_t, sin_t, fb, ib, ia_pair, *more):
        older, inputs = (more[:-2], more[-2:]) if extra else (more, ())
        kappa = magnitude(place, wave_x)
        spec = forward(block.reshape(LANES, LANES), fa, cos_t, sin_t, fb)
        other = older[0] if older else spec
        pair = jnp.concatenate(
            [multiply(spec, kappa, powers[0]), multiply(other, kappa, powers[1])], axis=0
        )
        inner = from_right(pair, ib)
        parts = []
        for field in range(2):
            rows = inner[field * LANES : (field + 1) * LANES]
            parts += twiddle(rows[:, :LANES], rows[:, LANES:], cos_t, sin_t)
        back = from_left(ia_pair, jnp.concatenate(parts, axis=0))
        if not extra:
            return back, spec
        every = slice(None)
        pieces = [((every, slice(0, 8)), back.reshape(32, 8, LANES))]
        pieces += [((peer, slice(8, 16)), tile) for peer, tile in extra(place, *inputs)]
        return pieces, spec

    return body


def halo_tiles(place, velocity, flat):
    edges = roll(flat, CY, 1)[:, :LANES]
    side = lax.shift_right_logical(lax.broadcasted_iota(jnp.int32, edges.shape, 1), 4)
    for start, first in ((0, CX - 2), (1, 0)):
        for tile in range(12):
            c, layer, half = tile // 4, tile // 2 % 2, tile % 2
            yield 16 * start + tile, velocity[c, first + layer, 8 * half : 8 * half + 8]
        yield 16 * start + 12, jnp.where(side == start, edges, 0.0)
        for tile in range(13, 16):
            yield 16 * start + tile, jnp.zeros((8, LANES), jnp.float32)


def forward_tiles(place, relay, unused):
    nothing = jnp.zeros((8, LANES), jnp.float32)
    for slab in range(32):
        below = relay[slab - 1, 8:16] if slab > 0 else nothing
        above = relay[slab + 1, 8:16] if slab < 31 else nothing
        yield slab, jnp.where(place[0] < 16, below, above)


def back_y(block, cos_t, sin_t, ib_pair, ia):
    inner = from_right(block.reshape(LANES, 2 * LANES), ib_pair)
    reals, imags = [], []
    for field in range(2):
        part = inner[:, 2 * field * LANES : 2 * (field + 1) * LANES]
        real, imag = twiddle(part[:, :LANES], part[:, LANES:], cos_t, sin_t)
        reals.append(real)
        imags.append(imag)
    stacked = jnp.concatenate(
        [jnp.concatenate(reals, axis=1), jnp.concatenate(imags, axis=1)], axis=0
    )
    fields = from_left(ia, stacked)
    return fields[:, :LANES], fields[:, LANES:]


def second_y(block, eta, fa, cos_t, sin_t, fb, ib_pair, ia):
    slope_one, cubic_one = back_y(block, cos_t, sin_t, ib_pair, ia)
    spectrum = forward(-eta * slope_one, fa, cos_t, sin_t, fb)
    return spectrum, slope_one, cubic_one


def third_y(block, eta, fa, cos_t, sin_t, fb, ib_pair, ia):
    slope_two, curve_one = back_y(block, cos_t, sin_t, ib_pair, ia)
    potential_three = -eta * slope_two - 0.5 * eta * eta * curve_one
    return forward(potential_three, fa, cos_t, sin_t, fb), slope_two, curve_one


def last_y(block, eta, slope_one, cubic_one, slope_two, curve_one, cos_t, sin_t, ib_pair, ia):
    slope_three, curve_two = back_y(block, cos_t, sin_t, ib_pair, ia)
    vertical = (
        slope_one
        + slope_two
        + eta * curve_one
        + slope_three
        + eta * curve_two
        + 0.5 * eta * eta * cubic_one
    )
    return (vertical,)


def swap(values, axis):
    return lax.all_to_all(values, axis, 0, 0, tiled=True)


def beside(values, axis, work, *inputs):
    values, inputs = lax.optimization_barrier((values, inputs))
    moved = swap(values, axis)
    return lax.optimization_barrier((moved, work(*inputs)))


INDEX_X = np.arange(LANES)[:, None] // 4 + 32 * np.arange(LANES)[None, :]
WAVE_X = np.float32(2.0 * math.pi / NXW) * np.minimum(INDEX_X, NXW - INDEX_X).astype(np.float32)


def wave_surface(surface_eta, surface_potential, velocity, place, work, inputs):
    square = (LANES, LANES)
    turns_y = [f32(TAB_Y["cos_t"]), f32(TAB_Y["sin_t"])]
    turns_x = [f32(TAB_X["cos_t"]), f32(TAB_X["sin_t"])]
    fwd_y = [left_table(TAB_Y["fa"]), *turns_y, right_table(TAB_Y["fb"])]
    inv_y = [right_table(Y_IB_PAIR), left_table(TAB_Y["ia"])]
    tab_x = [
        place,
        f32(WAVE_X),
        left_table(TAB_X["fa"]),
        *turns_x,
        right_table(TAB_X["fb"]),
        right_table(TAB_X["ib"]),
        left_table(X_IA_PAIR),
    ]

    def to_slab(block):
        (turned,) = run(loaded(turn), [square], swap(block.reshape(16, 8, LANES), "pencil"))
        return turned.reshape(32, 4, LANES)

    def to_pencil(block):
        (turned,) = run(turn_fields, [(LANES, 2 * LANES)], block)
        return swap(turned.reshape(16, 8, 2 * LANES), "pencil")

    pair, wide = (32, 8, LANES), (32, 16, LANES)
    (turned,) = run(
        loaded(turn_inputs), [(16, 16, LANES)], surface_eta, surface_potential, room=None
    )
    spectrum, eta = run(loaded(first_y), [square, square], swap(turned, "pencil"), *fwd_y)
    block, given = beside(to_slab(spectrum), "slab", work, *inputs)
    stage = x_stage((1, 3), halo_tiles)
    block, spec_one = run(
        loaded(stage), [wide, square], block.reshape(square), *tab_x, velocity, given[0]
    )
    relay = swap(block, "slab")
    spectrum, slope_one, cubic_one = run(
        loaded(second_y), [square] * 3, to_pencil(relay), eta, *fwd_y, *inv_y
    )
    block = swap(to_slab(spectrum), "slab").reshape(square)
    stage = x_stage((1, 2), forward_tiles)
    block, spec_two = run(loaded(stage), [wide, square], block, *tab_x, spec_one, relay, eta)
    halo = swap(block, "slab")
    spectrum, slope_two, curve_one = run(
        loaded(third_y), [square] * 3, to_pencil(halo), eta, *fwd_y, *inv_y
    )
    block = swap(to_slab(spectrum), "slab").reshape(square)
    block, _ = run(loaded(x_stage((1, 2))), [pair, square], block, *tab_x, spec_two)
    (vertical,) = run(
        loaded(last_y),
        [(16, 8, LANES)],
        to_pencil(swap(block, "slab")),
        eta,
        slope_one,
        cubic_one,
        slope_two,
        curve_one,
        *turns_y,
        *inv_y,
    )
    return swap(vertical, "pencil").reshape(square), halo, given


def wavenumber(index, length):
    folded = jnp.minimum(index, length - index)
    return 2.0 * math.pi / length * folded.astype(jnp.float32)


def ramp_weight(distance, reach_len):
    ratio = jnp.clip(1.0 - distance / reach_len, 0.0, 1.0)
    return ratio * ratio


def relax_of(cell_x, cell_y):
    pos_x, pos_y = cell_x.astype(jnp.float32), cell_y.astype(jnp.float32)
    reach_x = float(ZONE * CX)
    reach_y = float(CY)
    along_x = jnp.maximum(ramp_weight(pos_x, reach_x), ramp_weight(NX - 1.0 - pos_x, reach_x))
    across = jnp.maximum(ramp_weight(pos_y, reach_y), ramp_weight(NY - 1.0 - pos_y, reach_y))
    in_x = jnp.where((cell_x >= 0) & (cell_x < NX), 1.0, 0.0)
    in_y = jnp.where((cell_y >= 0) & (cell_y < NY), 1.0, 0.0)
    return jnp.maximum(along_x, across), in_x * in_y


def thirds(values):
    terms = []
    for _ in range(3):
        term = values.astype(jnp.bfloat16)
        terms.append(term)
        values = values - term.astype(jnp.float32)
    return jnp.concatenate(terms, axis=1)


def chosen(terms, lanes):
    count, parts = lanes.shape[1], terms.shape[1] // LANES
    iota = lax.broadcasted_iota(jnp.int32, (LANES, count), 0)
    hot = jnp.where(iota == lanes, 1.0, 0.0).astype(jnp.bfloat16)
    picked = jnp.dot(
        terms, jnp.concatenate([hot] * parts, axis=0), preferred_element_type=jnp.float32
    )
    return picked, lax.broadcasted_iota(jnp.int32, picked.shape, 0)


def listed(columns, points, row_count):
    terms = thirds(columns)
    rows = []
    for i in range(row_count):
        point = points[i : i + 1, :]
        picked, iota = chosen(terms, lax.shift_right_arithmetic(point, 7))
        found = jnp.where(iota == (point & (LANES - 1)), picked, 0.0)
        rows.append(jnp.sum(found, axis=0, keepdims=True))
    return rows


POINT_ROWS = 11


def pick_elevation(eta, points):
    rows = listed(eta[...].T, points, POINT_ROWS)
    return ([(slice(i, i + 1), row) for i, row in enumerate(rows)],)


def pick_vertical(columns, points, eta_rows):
    columns = columns[...]
    rows = listed(columns, points, POINT_ROWS)
    pieces = [((slice(None), slice(None)), jnp.zeros((3 * LANES, LANES), jnp.float32))]

    def put(slab, place, row, half):
        at = slice(half * LANES, (half + 1) * LANES)
        for field, value in enumerate((eta_rows[row : row + 1, at], rows[row][:, at])):
            for block in range(3):
                line = 12 * (slab + 1 - block) + 4 * block + 2 * place + field
                if 0 <= line < 3 * LANES:
                    pieces.append(((slice(line, line + 1), slice(None)), value))

    for row, slab in enumerate((0, 1, 30, 31)):
        for half in range(2):
            put(slab, half, row, half)
    for slab in range(2, 30):
        put(slab, 0, 4 + (slab - 2) // 4, (slab - 2) % 4 // 2)
    return pieces, columns.T


def slots_of(stencil, slab, block):
    source, slot = lax.shift_right_logical(stencil, 8), stencil & 255
    in_zone = jnp.where((slab < ZONE) | (slab >= 32 - ZONE), 1, 0)
    lines = 12 * source + 4 * block + 2 * in_zone * lax.shift_right_logical(slot, 7)
    lanes = in_zone * (slot & 127) + (1 - in_zone) * ((slot & 63) + 64 * (slab & 1))
    return lines, lanes


def both_fields(terms, lines, lanes, shares):
    picked, iota = chosen(terms, lanes)
    picked = picked * shares
    return [jnp.where(iota == lines + field, picked, 0.0) for field in range(2)]


def summed(values):
    return jnp.sum(values, axis=0, keepdims=True)


def over_q(values):
    values = values + roll(values, 64, 1)
    return values + roll(values, 32, 1)


def sample(arrived, place, flat, halo, velocity):
    slab = place[0]
    terms = thirds(arrived[...])[:, : 2 * LANES]
    flat = flat[...]
    lines, lanes = slots_of(flat[0:4].astype(jnp.int32), slab, 1)
    weights = flat[4:8]
    shares = weights / jnp.sum(weights, axis=0, keepdims=True)
    totals = [0.0, 0.0]
    for q in range(4):
        at = slice(q, q + 1)
        found = both_fields(terms, lines[at], lanes[at], shares[at])
        totals = [total + part for total, part in zip(totals, found, strict=True)]
    rows = [summed(total) for total in totals]

    lane = lax.broadcasted_iota(jnp.int32, (8, LANES), 1)
    side = lax.shift_right_logical(lane, 4) & 1
    beside_x = halo[12, 8:16] + halo[28, 8:16]
    points, weight = in_lanes(beside_x, lane, 0), in_lanes(beside_x, lane, 4)
    lines, lanes = slots_of(points.astype(jnp.int32), slab - 1 + 2 * side, 2 * side)
    total = over_q(weight)
    shares = weight / jnp.where(total > 0.0, total, 1.0)
    for part in both_fields(terms, lines[0:1], lanes[0:1], shares[0:1]):
        value = over_q(jnp.broadcast_to(summed(part), (8, LANES)))[0:1]
        rows.append(jnp.concatenate([value, value], axis=1))

    sent = []
    for y_at in (CY - 2, 0):
        pieces = []
        for c in range(3):
            line = 20 * c
            for x in range(2):
                tile = 4 * c + 2 * x + y_at // 8
                at = slice(8 + y_at % 8, 10 + y_at % 8)
                pieces.append((line + x, halo[tile, at]))
                pieces.append((line + 18 + x, halo[16 + tile, at]))
            pieces.append((slice(line + 2, line + 18), velocity[c, :, y_at : y_at + 2]))
        for field in range(2):
            for half in range(2):
                at = (60 + field, slice(half, half + 1))
                pieces.append((at, rows[field][:, half * LANES : (half + 1) * LANES]))
        sent.append(pieces)
    here = jnp.concatenate(rows + [jnp.zeros((4, 256), jnp.float32)], axis=0)
    return here, *sent


def in_lanes(values, lane, first):
    result = jnp.zeros(values.shape, jnp.float32)
    for q in range(4):
        moved = jnp.broadcast_to(values[first + q : first + q + 1], values.shape)
        if q:
            moved = roll(moved, 32 * q, 1)
        result = jnp.where(lax.shift_right_logical(lane, 5) == q, moved, result)
    return result


def roll(values, shift, axis):
    return pltpu.roll(values, shift, axis)


def predicted_of(centers, neighbours):
    lane = lax.broadcasted_iota(jnp.int32, centers[0].shape, centers[0].ndim - 1)
    last = centers[0].ndim - 1
    results = []
    for center, (plus_x, minus_x, plus_y, minus_y) in zip(centers, neighbours, strict=True):
        plus_z = jnp.where(lane == CZ - 1, 0.0, roll(center, CZ - 1, last))
        minus_z = jnp.where(lane == 0, 0.0, roll(center, 1, last))
        laplace = plus_x + minus_x + (plus_y + minus_y) + (plus_z + minus_z) - 6.0 * center
        advect = (
            centers[0] * (plus_x - minus_x)
            + centers[1] * (plus_y - minus_y)
            + centers[2] * (plus_z - minus_z)
        )
        results.append(center + TIME_STEP * (VISCOSITY * laplace - 0.5 * advect))
    return results


def surface_columns(here, from_low, from_high):
    def lines_of(sent):
        lines = [
            jnp.concatenate([sent[60 + field, half : half + 1] for half in range(2)], axis=1)
            for field in range(2)
        ]
        return jnp.concatenate(lines + [jnp.zeros((6, 256), jnp.float32)], axis=0)

    lane = lax.broadcasted_iota(jnp.int32, (8, 256), 1)
    below, above = roll(lines_of(from_low), 241, 1), roll(lines_of(from_high), 15, 1)
    across_y = jnp.where(lane % CY == 0, below, above)
    surface = jnp.concatenate([here[...], across_y], axis=0).T
    return lambda index: surface[:, index : index + 1].reshape(CX, CY, 1)


def both_substeps(velocity, halo, from_low, from_high, here, place, decay, padded):
    for c in range(3):
        padded[c, 2:18, 8:24] = velocity[c]
        for tile in range(4):
            layer, half = tile // 2, tile % 2
            at = slice(8 + 8 * half, 16 + 8 * half)
            padded[c, layer, at] = halo[4 * c + tile, 8:16]
            padded[c, 18 + layer, at] = halo[16 + 4 * c + tile, 8:16]
        padded[c, :, 6:8] = from_low[20 * c : 20 * c + 20]
        padded[c, :, 24:26] = from_high[20 * c : 20 * c + 20]
    column = surface_columns(here, from_low, from_high)
    (keep, keep_x, keep_y), (pull, pull_x, pull_y) = relax_fields(place, decay[...])

    def region(x_at, x_to, y_at, y_to):
        def part(c, shift_x, shift_y):
            return padded[c, x_at + shift_x : x_to + shift_x, y_at + shift_y : y_to + shift_y]

        steps = ((1, 0), (-1, 0), (0, 1), (0, -1))
        centers = [part(c, 0, 0) for c in range(3)]
        return predicted_of(centers, [[part(c, *step) for step in steps] for c in range(3)])

    own = region(2, 18, 8, 24)
    sides_x = [region(1, 2, 8, 24), region(18, 19, 8, 24)]
    sides_y = [region(2, 18, 7, 8), region(2, 18, 24, 25)]

    shape = (CX, CY, CZ)
    row = lax.broadcasted_iota(jnp.int32, shape, 1)
    centers, neighbours, targets = [], [], []
    for c in range(3):
        center = own[c] * keep
        outer_x = [sides_x[side][c] * keep_x[side : side + 1] for side in range(2)]
        low, high = [jnp.broadcast_to(side[c], shape) for side in sides_y]
        outer_y = jnp.where(row == 0, low, high) * keep_y
        target = None
        if c != 1:
            field = c // 2
            target = pull * column(field)
            center = center + target
            line = column(2 + field)
            outer_x = [
                outer_x[0] + pull_x[0:1] * line[0:1],
                outer_x[1] + pull_x[1:2] * line[CX - 1 : CX],
            ]
            outer_y = outer_y + pull_y * column(8 + field)
        plus_x = jnp.concatenate([center[1:], outer_x[1]], axis=0)
        minus_x = jnp.concatenate([outer_x[0], center[:-1]], axis=0)
        plus_y = jnp.where(row == CY - 1, outer_y, roll(center, CY - 1, 1))
        minus_y = jnp.where(row == 0, outer_y, roll(center, 1, 1))
        centers.append(center)
        neighbours.append((plus_x, minus_x, plus_y, minus_y))
        targets.append(target)
    pieces = []
    for c, value in enumerate(predicted_of(centers, neighbours)):
        value = value * keep
        pieces.append((c, value if targets[c] is None else value + targets[c]))
    return (pieces,)


def shifted(values, axis, step):
    size = lax.axis_size(axis)
    pairs = [(i, i + step) for i in range(size) if 0 <= i + step < size]
    return lax.ppermute(values, axis, pairs)


def list_points(send_point, send_count):
    slot = lax.broadcasted_iota(jnp.int32, (32, 256), 1)
    points = jnp.where(slot < send_count[0, 0][:, None], send_point[0, 0], -1)
    inner = points[2:30, :64].reshape(7, 256)
    return jnp.concatenate([points[:2], points[30:], inner], axis=0)


DECAY = np.exp(-DEPTH_RATE * (CZ - 1.0 - np.arange(CZ)) / CZ).astype(np.float32)


def relax_fields(place, decay):
    def fields(cell_x, cell_y):
        relax, inside = relax_of(cell_x, cell_y)
        return (1.0 - relax) * inside, relax * inside * decay.reshape(1, 1, CZ)

    side = lax.broadcasted_iota(jnp.int32, (2, 1, CZ), 0)
    row = lax.broadcasted_iota(jnp.int32, (1, CY, CZ), 1)
    cell_x = place[0] * CX + lax.broadcasted_iota(jnp.int32, (CX, 1, CZ), 0)
    cell_y = place[1] * CY + row
    out_x = place[0] * CX - 1 + (CX + 1) * side
    out_y = cell_y + jnp.where(row == 0, -1, jnp.where(row == CY - 1, 1, 0))
    own, across_x, across_y = fields(cell_x, cell_y), fields(out_x, cell_y), fields(cell_x, out_y)
    return (own[0], across_x[0], across_y[0]), (own[1], across_x[1], across_y[1])


def flat_stencil(stencil, interp_weight):
    rows = [stencil.astype(jnp.float32), interp_weight]
    return jnp.concatenate(rows, axis=0).reshape(8, CX * CY)


def on_device(
    surface_eta, surface_potential, velocity, send_point, send_count, stencil, interp_weight
):
    place = jnp.stack([lax.axis_index("slab"), lax.axis_index("pencil")])
    surface_eta, place = lax.optimization_barrier((surface_eta, place))
    square = (LANES, LANES)

    def lists(eta, send_point, send_count, stencil, interp_weight):
        points = list_points(send_point, send_count)
        rows = run(pick_elevation, [(POINT_ROWS, 256)], eta, points)[0]
        return flat_stencil(stencil, interp_weight), points, rows

    columns, halo, (flat, points, eta_rows) = wave_surface(
        surface_eta,
        surface_potential,
        velocity,
        place,
        lists,
        (surface_eta, send_point, send_count, stencil, interp_weight),
    )
    outgoing, vertical = run(
        pick_vertical, [(3 * LANES, LANES), square], columns, points, eta_rows
    )
    arrived = swap(outgoing.reshape(32, 3, 4, LANES), "slab").reshape(3 * LANES, LANES)
    sent = (62, 2, LANES)
    here, upward, downward = run(
        sample, [(8, 256), sent, sent], arrived, place, flat, halo, velocity
    )
    from_low, from_high = shifted(upward, "pencil", 1), shifted(downward, "pencil", -1)
    (velocity,) = run(
        both_substeps,
        [(3, CX, CY, CZ)],
        velocity,
        halo,
        from_low,
        from_high,
        here,
        place,
        jnp.asarray(DECAY[None]),
        scratch=[(3, 20, 32, CZ)],
    )
    return (vertical, velocity)


def solution(mesh):
    in_specs = (
        P("pencil", "slab"),
        P("pencil", "slab"),
        P(None, "slab", "pencil", None),
        P("slab", "pencil", None, None),
        P("slab", "pencil", None),
        P(None, "slab", "pencil"),
        P(None, "slab", "pencil"),
    )
    out_specs = (P("pencil", "slab"), P(None, "slab", "pencil", None))
    return jax.shard_map(
        on_device, mesh=mesh, in_specs=in_specs, out_specs=out_specs, check_vma=False
    )
```

```python
import math

import jax
import jax.numpy as jnp
import ml_dtypes
import numpy as np
from jax import lax
from jax.experimental import pallas as pl
from jax.experimental.pallas import tpu as pltpu
from jax.sharding import PartitionSpec as P

NXW = 4096
NYW = 2048
LANES = 128
CX = 16
CY = 16
CZ = 128
NX = 512
NY = 256
ZONE = 2

TIME_STEP = 0.2
VISCOSITY = 0.6
DEPTH_RATE = 3.0


def stage_tables(peers):
    copies = LANES // peers
    length = peers * LANES
    outer = np.arange(peers)
    inner = np.arange(LANES)
    eye = np.eye(copies)
    angle_a = 2.0 * np.pi / peers * (outer[:, None] * outer[None, :] % peers)
    angle_t = 2.0 * np.pi / length * (outer[:, None] * inner[None, :] % length)
    angle_b = 2.0 * np.pi / LANES * (inner[:, None] * inner[None, :] % LANES)
    cos_a, sin_a = np.kron(np.cos(angle_a), eye), np.kron(np.sin(angle_a), eye)
    cos_b, sin_b = np.cos(angle_b), np.sin(angle_b)
    tables = {
        "fa": np.concatenate([cos_a, -sin_a], axis=0),
        "cos_t": np.repeat(np.cos(angle_t), copies, axis=0),
        "sin_t": np.repeat(np.sin(angle_t), copies, axis=0),
        "fb": np.concatenate([cos_b + sin_b, sin_b - cos_b], axis=0),
        "ib": np.concatenate([cos_b, -sin_b], axis=1),
        "ia": np.concatenate([cos_a + sin_a, sin_a - cos_a], axis=1),
    }
    return tables


TAB_Y = stage_tables(16)
TAB_X = stage_tables(32)


def pair_inverse_b(ib):
    rows = ib.reshape(32, 4, 2 * LANES)
    big = np.zeros((32, 2, 4, 2, 2 * LANES))
    for field in range(2):
        big[:, field, :, field, :] = rows
    return big.reshape(2 * LANES, 4 * LANES)


def pair_inverse_a(ia):
    rows = ia.reshape(32, 4, 2 * LANES)
    big = np.zeros((32, 2, 4, 2, 2 * LANES))
    for field in range(2):
        big[:, field, :, field, :] = rows
    return big.reshape(2 * LANES, 4 * LANES)


Y_IB_PAIR = pair_inverse_b(TAB_Y["ib"])
X_IA_PAIR = pair_inverse_a(TAB_X["ia"])


def f32(array):
    return jnp.asarray(np.asarray(array, np.float32))


def halves_of(table):
    high = table.astype(ml_dtypes.bfloat16)
    return high, (table - high.astype(np.float64)).astype(ml_dtypes.bfloat16)


def left_table(table):
    high, low = halves_of(table)
    return jnp.asarray(np.concatenate([high, high, low], axis=1))


def right_table(table):
    high, low = halves_of(table)
    return jnp.asarray(np.concatenate([high, low, high], axis=0))


def halves(values):
    high = values.astype(jnp.bfloat16)
    return high, (values - high.astype(jnp.float32)).astype(jnp.bfloat16)


def from_left(table, values):
    high, low = halves(values)
    stacked = jnp.concatenate([high, low, high], axis=0)
    return jnp.dot(table, stacked, preferred_element_type=jnp.float32)


def from_right(values, table):
    high, low = halves(values)
    joined = jnp.concatenate([high, high, low], axis=1)
    return jnp.dot(joined, table, preferred_element_type=jnp.float32)


INDEX_X = np.arange(LANES)[:, None] // 4 + 32 * np.arange(LANES)[None, :]
WAVE_X = np.float32(2.0 * math.pi / NXW) * np.minimum(INDEX_X, NXW - INDEX_X).astype(np.float32)
TURNS_X = np.concatenate([TAB_X["cos_t"], TAB_X["sin_t"], WAVE_X])


def twiddle(real, imag, cos_t, sin_t):
    return real * cos_t + imag * sin_t, imag * cos_t - real * sin_t


def forward(block, fa, cos_t, sin_t, fb):
    outer = from_left(fa, block)
    real, imag = twiddle(outer[:LANES], outer[LANES:], cos_t, sin_t)
    return from_right(jnp.concatenate([real, imag], axis=1), fb)


def run(body, outs, *args, room=8, scratch=()):
    shapes = [jax.ShapeDtypeStruct(shape, jnp.float32) for shape in outs]

    def kernel(*refs):
        inputs, rest = refs[: len(args)], refs[len(args) :]
        results = body(*inputs, *rest[len(outs) :])
        for ref, result in zip(rest[: len(outs)], results, strict=True):
            for index, piece in result if isinstance(result, list) else [(..., result)]:
                ref[index] = piece.reshape(ref.shape) if index is ... else piece

    params = pltpu.CompilerParams(vmem_limit_bytes=room << 20) if room else None
    places = [pl.BlockSpec(memory_space=pltpu.SMEM if is_place(arg) else None) for arg in args]
    call = pl.pallas_call(
        kernel,
        out_shape=shapes,
        in_specs=places,
        scratch_shapes=[pltpu.VMEM(shape, jnp.float32) for shape in scratch],
        compiler_params=params,
    )
    return call(*args)


def is_place(arg):
    return arg.shape == (2,)


def loaded(body):
    return lambda *refs: body(*[ref if is_place(ref) else ref[...] for ref in refs])


def turn_inputs(eta, potential):
    eta_t = eta.T.reshape(16, 8, LANES)
    potential_t = potential.T.reshape(16, 8, LANES)
    return (jnp.concatenate([eta_t, potential_t], axis=1),)


def turn(block):
    return (block.reshape(-1, LANES).T,)


def turn_fields(block):
    return (block[:, 0:8].reshape(-1, LANES).T,)


def first_y(both, fa, turns, fb):
    eta = both[:, :8].reshape(LANES, LANES)
    potential = both[:, 8:].reshape(LANES, LANES)
    return forward(potential, fa, turns[:LANES], turns[LANES:], fb), eta


def magnitude(place, wave_x):
    line = lax.broadcasted_iota(jnp.int32, (LANES, LANES), 0) & 3
    wave_y = wavenumber(place[1] + 64 * place[0] + 16 * line, NYW)
    return jnp.sqrt(wave_x * wave_x + wave_y * wave_y)


def x_stage(powers, extra=None):
    def multiply(spec, kappa, power):
        factor = kappa
        for _ in range(power - 1):
            factor = factor * kappa
        return spec * (factor * (1.0 / (NXW * NYW)))

    def body(block, place, turns, fa, fb, ib, ia_pair, *more):
        cos_t, sin_t, wave_x = [turns[i * LANES : (i + 1) * LANES] for i in range(3)]
        older, inputs = (more[:-2], more[-2:]) if extra else (more, ())
        kappa = magnitude(place, wave_x)
        spec = forward(block.reshape(LANES, LANES), fa, cos_t, sin_t, fb)
        other = older[0] if older else spec
        pair = jnp.concatenate(
            [multiply(spec, kappa, powers[0]), multiply(other, kappa, powers[1])], axis=0
        )
        inner = from_right(pair, ib)
        parts = []
        for field in range(2):
            rows = inner[field * LANES : (field + 1) * LANES]
            parts += twiddle(rows[:, :LANES], rows[:, LANES:], cos_t, sin_t)
        back = from_left(ia_pair, jnp.concatenate(parts, axis=0))
        if not extra:
            return (back,)
        every = slice(None)
        pieces = [((every, slice(0, 8)), back.reshape(32, 8, LANES))]
        pieces += [((peer, slice(8, 16)), tile) for peer, tile in extra(place, *inputs)]
        return pieces, spec

    return body


def halo_tiles(place, velocity, flat):
    edges = roll(flat, CY, 1)[:, :LANES]
    side = lax.shift_right_logical(lax.broadcasted_iota(jnp.int32, edges.shape, 1), 4)
    for start, first in ((0, CX - 2), (1, 0)):
        for tile in range(12):
            c, layer, half = tile // 4, tile // 2 % 2, tile % 2
            yield 16 * start + tile, velocity[c, first + layer, 8 * half : 8 * half + 8]
        yield 16 * start + 12, jnp.where(side == start, edges, 0.0)
        for tile in range(13, 16):
            yield 16 * start + tile, jnp.zeros((8, LANES), jnp.float32)


def forward_tiles(place, relay, unused):
    nothing = jnp.zeros((8, LANES), jnp.float32)
    for slab in range(32):
        below = relay[slab - 1, 8:16] if slab > 0 else nothing
        above = relay[slab + 1, 8:16] if slab < 31 else nothing
        yield slab, jnp.where(place[0] < 16, below, above)


def back_y(block, cos_t, sin_t, ib_pair, ia):
    inner = from_right(block.reshape(LANES, 2 * LANES), ib_pair)
    reals, imags = [], []
    for field in range(2):
        part = inner[:, 2 * field * LANES : 2 * (field + 1) * LANES]
        real, imag = twiddle(part[:, :LANES], part[:, LANES:], cos_t, sin_t)
        reals.append(real)
        imags.append(imag)
    stacked = jnp.concatenate(
        [jnp.concatenate(reals, axis=1), jnp.concatenate(imags, axis=1)], axis=0
    )
    fields = from_left(ia, stacked)
    return fields[:, :LANES], fields[:, LANES:]


def second_y(block, eta, fa, turns, fb, ib_pair, ia):
    cos_t, sin_t = turns[:LANES], turns[LANES:]
    slope_one, cubic_one = back_y(block, cos_t, sin_t, ib_pair, ia)
    spectrum = forward(-eta * slope_one, fa, cos_t, sin_t, fb)
    return spectrum, slope_one, cubic_one


def third_y(block, eta, fa, turns, fb, ib_pair, ia):
    cos_t, sin_t = turns[:LANES], turns[LANES:]
    slope_two, curve_one = back_y(block, cos_t, sin_t, ib_pair, ia)
    potential_three = -eta * slope_two - 0.5 * eta * eta * curve_one
    return forward(potential_three, fa, cos_t, sin_t, fb), slope_two, curve_one


def last_y(block, eta, slope_one, cubic_one, slope_two, curve_one, turns, ib_pair, ia):
    cos_t, sin_t = turns[:LANES], turns[LANES:]
    slope_three, curve_two = back_y(block, cos_t, sin_t, ib_pair, ia)
    vertical = (
        slope_one
        + slope_two
        + eta * curve_one
        + slope_three
        + eta * curve_two
        + 0.5 * eta * eta * cubic_one
    )
    return (vertical,)


def swap(values, axis):
    return lax.all_to_all(values, axis, 0, 0, tiled=True)


def beside(values, axis, work, *inputs):
    values, inputs = lax.optimization_barrier((values, inputs))
    moved = swap(values, axis)
    return lax.optimization_barrier((moved, work(*inputs)))


def wave_surface(surface_eta, surface_potential, velocity, place, work, inputs):
    square = (LANES, LANES)
    turns_y = [f32(np.concatenate([TAB_Y["cos_t"], TAB_Y["sin_t"]]))]
    fwd_y = [left_table(TAB_Y["fa"]), *turns_y, right_table(TAB_Y["fb"])]
    inv_y = [right_table(Y_IB_PAIR), left_table(TAB_Y["ia"])]
    tab_x = [
        place,
        f32(TURNS_X),
        left_table(TAB_X["fa"]),
        right_table(TAB_X["fb"]),
        right_table(TAB_X["ib"]),
        left_table(X_IA_PAIR),
    ]

    def to_slab(block):
        (turned,) = run(loaded(turn), [square], swap(block.reshape(16, 8, LANES), "pencil"))
        return turned.reshape(32, 4, LANES)

    def to_pencil(block):
        (turned,) = run(turn_fields, [(LANES, 2 * LANES)], block)
        return swap(turned.reshape(16, 8, 2 * LANES), "pencil")

    pair, wide = (32, 8, LANES), (32, 16, LANES)
    (turned,) = run(
        loaded(turn_inputs), [(16, 16, LANES)], surface_eta, surface_potential, room=None
    )
    both, given = beside(turned, "pencil", work, *inputs)
    spectrum, eta = run(loaded(first_y), [square, square], both, *fwd_y)
    block = swap(to_slab(spectrum), "slab")
    stage = x_stage((1, 3), halo_tiles)
    block, spec_one = run(
        loaded(stage), [wide, square], block.reshape(square), *tab_x, velocity, given[0]
    )
    relay = swap(block, "slab")
    spectrum, slope_one, cubic_one = run(
        loaded(second_y), [square] * 3, to_pencil(relay), eta, *fwd_y, *inv_y
    )
    block = swap(to_slab(spectrum), "slab").reshape(square)
    stage = x_stage((1, 2), forward_tiles)
    block, spec_two = run(loaded(stage), [wide, square], block, *tab_x, spec_one, relay, eta)
    halo = swap(block, "slab")
    spectrum, slope_two, curve_one = run(
        loaded(third_y), [square] * 3, to_pencil(halo), eta, *fwd_y, *inv_y
    )
    block = swap(to_slab(spectrum), "slab").reshape(square)
    (block,) = run(loaded(x_stage((1, 2))), [pair], block, *tab_x, spec_two)
    (vertical,) = run(
        loaded(last_y),
        [(16, 8, LANES)],
        to_pencil(swap(block, "slab")),
        eta,
        slope_one,
        cubic_one,
        slope_two,
        curve_one,
        *turns_y,
        *inv_y,
    )
    return swap(vertical, "pencil").reshape(square), halo, given


def wavenumber(index, length):
    folded = jnp.minimum(index, length - index)
    return 2.0 * math.pi / length * folded.astype(jnp.float32)


def ramp_weight(distance, reach_len):
    ratio = jnp.clip(1.0 - distance / reach_len, 0.0, 1.0)
    return ratio * ratio


def relax_of(cell_x, cell_y):
    pos_x, pos_y = cell_x.astype(jnp.float32), cell_y.astype(jnp.float32)
    reach_x = float(ZONE * CX)
    reach_y = float(CY)
    along_x = jnp.maximum(ramp_weight(pos_x, reach_x), ramp_weight(NX - 1.0 - pos_x, reach_x))
    across = jnp.maximum(ramp_weight(pos_y, reach_y), ramp_weight(NY - 1.0 - pos_y, reach_y))
    in_x = jnp.where((cell_x >= 0) & (cell_x < NX), 1.0, 0.0)
    in_y = jnp.where((cell_y >= 0) & (cell_y < NY), 1.0, 0.0)
    return jnp.maximum(along_x, across), in_x * in_y


def thirds(values):
    terms = []
    for _ in range(3):
        term = values.astype(jnp.bfloat16)
        terms.append(term)
        values = values - term.astype(jnp.float32)
    return jnp.concatenate(terms, axis=1)


def chosen(terms, lanes):
    count, parts = lanes.shape[1], terms.shape[1] // LANES
    iota = lax.broadcasted_iota(jnp.int32, (LANES, count), 0)
    hot = jnp.where(iota == lanes, 1.0, 0.0).astype(jnp.bfloat16)
    picked = jnp.dot(
        terms, jnp.concatenate([hot] * parts, axis=0), preferred_element_type=jnp.float32
    )
    return picked, lax.broadcasted_iota(jnp.int32, picked.shape, 0)


def listed(columns, points, row_count):
    terms = thirds(columns)
    rows = []
    for i in range(row_count):
        point = points[i : i + 1, :]
        picked, iota = chosen(terms, lax.shift_right_arithmetic(point, 7))
        found = jnp.where(iota == (point & (LANES - 1)), picked, 0.0)
        rows.append(jnp.sum(found, axis=0, keepdims=True))
    return rows


POINT_ROWS = 11


def pick_elevation(eta, points):
    rows = listed(eta[...].T, points, POINT_ROWS)
    return ([(slice(i, i + 1), row) for i, row in enumerate(rows)],)


def pick_vertical(columns, points, eta_rows):
    columns = columns[...]
    rows = listed(columns, points, POINT_ROWS)
    pieces = [((slice(None), slice(None)), jnp.zeros((3 * LANES, LANES), jnp.float32))]

    def put(slab, place, row, half):
        at = slice(half * LANES, (half + 1) * LANES)
        for field, value in enumerate((eta_rows[row : row + 1, at], rows[row][:, at])):
            for block in range(3):
                line = 12 * (slab + 1 - block) + 4 * block + 2 * place + field
                if 0 <= line < 3 * LANES:
                    pieces.append(((slice(line, line + 1), slice(None)), value))

    for row, slab in enumerate((0, 1, 30, 31)):
        for half in range(2):
            put(slab, half, row, half)
    for slab in range(2, 30):
        put(slab, 0, 4 + (slab - 2) // 4, (slab - 2) % 4 // 2)
    return pieces, columns.T


def slots_of(stencil, slab, block):
    source, slot = lax.shift_right_logical(stencil, 8), stencil & 255
    in_zone = jnp.where((slab < ZONE) | (slab >= 32 - ZONE), 1, 0)
    lines = 12 * source + 4 * block + 2 * in_zone * lax.shift_right_logical(slot, 7)
    lanes = in_zone * (slot & 127) + (1 - in_zone) * ((slot & 63) + 64 * (slab & 1))
    return lines, lanes


def both_fields(terms, lines, lanes, shares):
    picked, iota = chosen(terms, lanes)
    picked = picked * shares
    return [jnp.where(iota == lines + field, picked, 0.0) for field in range(2)]


def summed(values):
    return jnp.sum(values, axis=0, keepdims=True)


def over_q(values):
    values = values + roll(values, 64, 1)
    return values + roll(values, 32, 1)


def sample(arrived, place, flat, halo, velocity):
    slab = place[0]
    terms = thirds(arrived[...])[:, : 2 * LANES]
    flat = flat[...]
    lines, lanes = slots_of(flat[0:4].astype(jnp.int32), slab, 1)
    weights = flat[4:8]
    shares = weights / jnp.sum(weights, axis=0, keepdims=True)
    totals = [0.0, 0.0]
    for q in range(4):
        at = slice(q, q + 1)
        found = both_fields(terms, lines[at], lanes[at], shares[at])
        totals = [total + part for total, part in zip(totals, found, strict=True)]
    rows = [summed(total) for total in totals]

    lane = lax.broadcasted_iota(jnp.int32, (8, LANES), 1)
    side = lax.shift_right_logical(lane, 4) & 1
    beside_x = halo[12, 8:16] + halo[28, 8:16]
    points, weight = in_lanes(beside_x, lane, 0), in_lanes(beside_x, lane, 4)
    lines, lanes = slots_of(points.astype(jnp.int32), slab - 1 + 2 * side, 2 * side)
    total = over_q(weight)
    shares = weight / jnp.where(total > 0.0, total, 1.0)
    for part in both_fields(terms, lines[0:1], lanes[0:1], shares[0:1]):
        value = over_q(jnp.broadcast_to(summed(part), (8, LANES)))[0:1]
        rows.append(jnp.concatenate([value, value], axis=1))

    sent = []
    for y_at in (CY - 2, 0):
        pieces = []
        for c in range(3):
            line = 20 * c
            for x in range(2):
                tile = 4 * c + 2 * x + y_at // 8
                at = slice(8 + y_at % 8, 10 + y_at % 8)
                pieces.append((line + x, halo[tile, at]))
                pieces.append((line + 18 + x, halo[16 + tile, at]))
            pieces.append((slice(line + 2, line + 18), velocity[c, :, y_at : y_at + 2]))
        for field in range(2):
            for half in range(2):
                at = (60 + field, slice(half, half + 1))
                pieces.append((at, rows[field][:, half * LANES : (half + 1) * LANES]))
        sent.append(pieces)
    here = jnp.concatenate(rows + [jnp.zeros((4, 256), jnp.float32)], axis=0)
    return here, *sent


def in_lanes(values, lane, first):
    result = jnp.zeros(values.shape, jnp.float32)
    for q in range(4):
        moved = jnp.broadcast_to(values[first + q : first + q + 1], values.shape)
        if q:
            moved = roll(moved, 32 * q, 1)
        result = jnp.where(lax.shift_right_logical(lane, 5) == q, moved, result)
    return result


def roll(values, shift, axis):
    return pltpu.roll(values, shift, axis)


def predicted_of(centers, neighbours):
    lane = lax.broadcasted_iota(jnp.int32, centers[0].shape, centers[0].ndim - 1)
    last = centers[0].ndim - 1
    results = []
    for center, (plus_x, minus_x, plus_y, minus_y) in zip(centers, neighbours, strict=True):
        plus_z = jnp.where(lane == CZ - 1, 0.0, roll(center, CZ - 1, last))
        minus_z = jnp.where(lane == 0, 0.0, roll(center, 1, last))
        laplace = plus_x + minus_x + (plus_y + minus_y) + (plus_z + minus_z) - 6.0 * center
        advect = (
            centers[0] * (plus_x - minus_x)
            + centers[1] * (plus_y - minus_y)
            + centers[2] * (plus_z - minus_z)
        )
        results.append(center + TIME_STEP * (VISCOSITY * laplace - 0.5 * advect))
    return results


def surface_columns(here, from_low, from_high):
    def lines_of(sent):
        lines = [
            jnp.concatenate([sent[60 + field, half : half + 1] for half in range(2)], axis=1)
            for field in range(2)
        ]
        return jnp.concatenate(lines + [jnp.zeros((6, 256), jnp.float32)], axis=0)

    lane = lax.broadcasted_iota(jnp.int32, (8, 256), 1)
    below, above = roll(lines_of(from_low), 241, 1), roll(lines_of(from_high), 15, 1)
    across_y = jnp.where(lane % CY == 0, below, above)
    surface = jnp.concatenate([here[...], across_y], axis=0).T
    return lambda index: surface[:, index : index + 1].reshape(CX, CY, 1)


def both_substeps(velocity, halo, from_low, from_high, here, place, decay, padded):
    for c in range(3):
        padded[c, 2:18, 8:24] = velocity[c]
        for tile in range(4):
            layer, half = tile // 2, tile % 2
            at = slice(8 + 8 * half, 16 + 8 * half)
            padded[c, layer, at] = halo[4 * c + tile, 8:16]
            padded[c, 18 + layer, at] = halo[16 + 4 * c + tile, 8:16]
        padded[c, :, 6:8] = from_low[20 * c : 20 * c + 20]
        padded[c, :, 24:26] = from_high[20 * c : 20 * c + 20]
    column = surface_columns(here, from_low, from_high)
    (keep, keep_x, keep_y), (pull, pull_x, pull_y) = relax_fields(place, decay[...])

    def region(x_at, x_to, y_at, y_to):
        def part(c, shift_x, shift_y):
            return padded[c, x_at + shift_x : x_to + shift_x, y_at + shift_y : y_to + shift_y]

        steps = ((1, 0), (-1, 0), (0, 1), (0, -1))
        centers = [part(c, 0, 0) for c in range(3)]
        return predicted_of(centers, [[part(c, *step) for step in steps] for c in range(3)])

    own = region(2, 18, 8, 24)
    sides_x = [region(1, 2, 8, 24), region(18, 19, 8, 24)]
    sides_y = [region(2, 18, 7, 8), region(2, 18, 24, 25)]

    shape = (CX, CY, CZ)
    row = lax.broadcasted_iota(jnp.int32, shape, 1)
    centers, neighbours, targets = [], [], []
    for c in range(3):
        center = own[c] * keep
        outer_x = [sides_x[side][c] * keep_x[side : side + 1] for side in range(2)]
        low, high = [jnp.broadcast_to(side[c], shape) for side in sides_y]
        outer_y = jnp.where(row == 0, low, high) * keep_y
        target = None
        if c != 1:
            field = c // 2
            target = pull * column(field)
            center = center + target
            line = column(2 + field)
            outer_x = [
                outer_x[0] + pull_x[0:1] * line[0:1],
                outer_x[1] + pull_x[1:2] * line[CX - 1 : CX],
            ]
            outer_y = outer_y + pull_y * column(8 + field)
        plus_x = jnp.concatenate([center[1:], outer_x[1]], axis=0)
        minus_x = jnp.concatenate([outer_x[0], center[:-1]], axis=0)
        plus_y = jnp.where(row == CY - 1, outer_y, roll(center, CY - 1, 1))
        minus_y = jnp.where(row == 0, outer_y, roll(center, 1, 1))
        centers.append(center)
        neighbours.append((plus_x, minus_x, plus_y, minus_y))
        targets.append(target)
    pieces = []
    for c, value in enumerate(predicted_of(centers, neighbours)):
        value = value * keep
        pieces.append((c, value if targets[c] is None else value + targets[c]))
    return (pieces,)


def shifted(values, axis, step):
    size = lax.axis_size(axis)
    pairs = [(i, i + step) for i in range(size) if 0 <= i + step < size]
    return lax.ppermute(values, axis, pairs)


def list_points(send_point, send_count):
    slot = lax.broadcasted_iota(jnp.int32, (32, 256), 1)
    points = jnp.where(slot < send_count[0, 0][:, None], send_point[0, 0], -1)
    inner = points[2:30, :64].reshape(7, 256)
    return jnp.concatenate([points[:2], points[30:], inner], axis=0)


DECAY = np.exp(-DEPTH_RATE * (CZ - 1.0 - np.arange(CZ)) / CZ).astype(np.float32)


def relax_fields(place, decay):
    def fields(cell_x, cell_y):
        relax, inside = relax_of(cell_x, cell_y)
        return (1.0 - relax) * inside, relax * inside * decay.reshape(1, 1, CZ)

    side = lax.broadcasted_iota(jnp.int32, (2, 1, CZ), 0)
    row = lax.broadcasted_iota(jnp.int32, (1, CY, CZ), 1)
    cell_x = place[0] * CX + lax.broadcasted_iota(jnp.int32, (CX, 1, CZ), 0)
    cell_y = place[1] * CY + row
    out_x = place[0] * CX - 1 + (CX + 1) * side
    out_y = cell_y + jnp.where(row == 0, -1, jnp.where(row == CY - 1, 1, 0))
    own, across_x, across_y = fields(cell_x, cell_y), fields(out_x, cell_y), fields(cell_x, out_y)
    return (own[0], across_x[0], across_y[0]), (own[1], across_x[1], across_y[1])


def flat_stencil(stencil, interp_weight):
    rows = [stencil.astype(jnp.float32), interp_weight]
    return jnp.concatenate(rows, axis=0).reshape(8, CX * CY)


def on_device(
    surface_eta, surface_potential, velocity, send_point, send_count, stencil, interp_weight
):
    place = jnp.stack([lax.axis_index("slab"), lax.axis_index("pencil")])
    surface_eta, place = lax.optimization_barrier((surface_eta, place))
    square = (LANES, LANES)

    def lists(eta, send_point, send_count, stencil, interp_weight):
        points = list_points(send_point, send_count)
        rows = run(pick_elevation, [(POINT_ROWS, 256)], eta, points)[0]
        return flat_stencil(stencil, interp_weight), points, rows

    columns, halo, (flat, points, eta_rows) = wave_surface(
        surface_eta,
        surface_potential,
        velocity,
        place,
        lists,
        (surface_eta, send_point, send_count, stencil, interp_weight),
    )
    outgoing, vertical = run(
        pick_vertical, [(3 * LANES, LANES), square], columns, points, eta_rows
    )
    arrived = swap(outgoing.reshape(32, 3, 4, LANES), "slab").reshape(3 * LANES, LANES)
    sent = (62, 2, LANES)
    here, upward, downward = run(
        sample, [(8, 256), sent, sent], arrived, place, flat, halo, velocity
    )
    from_low, from_high = shifted(upward, "pencil", 1), shifted(downward, "pencil", -1)
    (velocity,) = run(
        both_substeps,
        [(3, CX, CY, CZ)],
        velocity,
        halo,
        from_low,
        from_high,
        here,
        place,
        jnp.asarray(DECAY[None]),
        scratch=[(3, 20, 32, CZ)],
    )
    return (vertical, velocity)


def solution(mesh):
    in_specs = (
        P("pencil", "slab"),
        P("pencil", "slab"),
        P(None, "slab", "pencil", None),
        P("slab", "pencil", None, None),
        P("slab", "pencil", None),
        P(None, "slab", "pencil"),
        P(None, "slab", "pencil"),
    )
    out_specs = (P("pencil", "slab"), P(None, "slab", "pencil", None))
    return jax.shard_map(
        on_device, mesh=mesh, in_specs=in_specs, out_specs=out_specs, check_vma=False
    )
```

```python
import math

import jax
import jax.numpy as jnp
import ml_dtypes
import numpy as np
from jax import lax
from jax.experimental import pallas as pl
from jax.experimental.pallas import tpu as pltpu
from jax.sharding import PartitionSpec as P

NXW = 4096
NYW = 2048
LANES = 128
CX = 16
CY = 16
CZ = 128
NX = 512
NY = 256
ZONE = 2

TIME_STEP = 0.2
VISCOSITY = 0.6
DEPTH_RATE = 3.0


def stage_tables(peers):
    copies = LANES // peers
    length = peers * LANES
    outer = np.arange(peers)
    inner = np.arange(LANES)
    eye = np.eye(copies)
    angle_a = 2.0 * np.pi / peers * (outer[:, None] * outer[None, :] % peers)
    angle_t = 2.0 * np.pi / length * (outer[:, None] * inner[None, :] % length)
    angle_b = 2.0 * np.pi / LANES * (inner[:, None] * inner[None, :] % LANES)
    cos_a, sin_a = np.kron(np.cos(angle_a), eye), np.kron(np.sin(angle_a), eye)
    cos_b, sin_b = np.cos(angle_b), np.sin(angle_b)
    tables = {
        "fa": np.concatenate([cos_a, -sin_a], axis=0),
        "cos_t": np.repeat(np.cos(angle_t), copies, axis=0),
        "sin_t": np.repeat(np.sin(angle_t), copies, axis=0),
        "fb": np.concatenate([cos_b + sin_b, sin_b - cos_b], axis=0),
        "ib": np.concatenate([cos_b, -sin_b], axis=1),
        "ia": np.concatenate([cos_a + sin_a, sin_a - cos_a], axis=1),
    }
    return tables


TAB_Y = stage_tables(16)
TAB_X = stage_tables(32)


def pair_inverse_b(ib):
    rows = ib.reshape(32, 4, 2 * LANES)
    big = np.zeros((32, 2, 4, 2, 2 * LANES))
    for field in range(2):
        big[:, field, :, field, :] = rows
    return big.reshape(2 * LANES, 4 * LANES)


def pair_inverse_a(ia):
    rows = ia.reshape(32, 4, 2 * LANES)
    big = np.zeros((32, 2, 4, 2, 2 * LANES))
    for field in range(2):
        big[:, field, :, field, :] = rows
    return big.reshape(2 * LANES, 4 * LANES)


Y_IB_PAIR = pair_inverse_b(TAB_Y["ib"])
X_IA_PAIR = pair_inverse_a(TAB_X["ia"])


def f32(array):
    return jnp.asarray(np.asarray(array, np.float32))


def halves_of(table):
    high = table.astype(ml_dtypes.bfloat16)
    return high, (table - high.astype(np.float64)).astype(ml_dtypes.bfloat16)


def left_table(table):
    high, low = halves_of(table)
    return jnp.asarray(np.concatenate([high, high, low], axis=1))


def right_table(table):
    high, low = halves_of(table)
    return jnp.asarray(np.concatenate([high, low, high], axis=0))


def halves(values):
    high = values.astype(jnp.bfloat16)
    return high, (values - high.astype(jnp.float32)).astype(jnp.bfloat16)


def from_left(table, values):
    high, low = halves(values)
    stacked = jnp.concatenate([high, low, high], axis=0)
    return jnp.dot(table, stacked, preferred_element_type=jnp.float32)


def from_right(values, table):
    high, low = halves(values)
    joined = jnp.concatenate([high, high, low], axis=1)
    return jnp.dot(joined, table, preferred_element_type=jnp.float32)


INDEX_X = np.arange(LANES)[:, None] // 4 + 32 * np.arange(LANES)[None, :]
WAVE_X = np.float32(2.0 * math.pi / NXW) * np.minimum(INDEX_X, NXW - INDEX_X).astype(np.float32)
TURNS_X = np.concatenate([TAB_X["cos_t"], TAB_X["sin_t"], WAVE_X])


def twiddle(real, imag, cos_t, sin_t):
    return real * cos_t + imag * sin_t, imag * cos_t - real * sin_t


def forward(block, fa, cos_t, sin_t, fb):
    outer = from_left(fa, block)
    real, imag = twiddle(outer[:LANES], outer[LANES:], cos_t, sin_t)
    return from_right(jnp.concatenate([real, imag], axis=1), fb)


def run(body, outs, *args, room=8, scratch=()):
    shapes = [jax.ShapeDtypeStruct(shape, jnp.float32) for shape in outs]

    def kernel(*refs):
        inputs, rest = refs[: len(args)], refs[len(args) :]
        results = body(*inputs, *rest[len(outs) :])
        for ref, result in zip(rest[: len(outs)], results, strict=True):
            for index, piece in result if isinstance(result, list) else [(..., result)]:
                ref[index] = piece.reshape(ref.shape) if index is ... else piece

    params = pltpu.CompilerParams(vmem_limit_bytes=room << 20) if room else None
    places = [pl.BlockSpec(memory_space=pltpu.SMEM if is_place(arg) else None) for arg in args]
    call = pl.pallas_call(
        kernel,
        out_shape=shapes,
        in_specs=places,
        scratch_shapes=[pltpu.VMEM(shape, jnp.float32) for shape in scratch],
        compiler_params=params,
    )
    return call(*args)


def is_place(arg):
    return arg.shape == (2,)


def loaded(body):
    return lambda *refs: body(*[ref if is_place(ref) else ref[...] for ref in refs])


def turn_inputs(eta, potential):
    eta_t = eta.T.reshape(16, 8, LANES)
    potential_t = potential.T.reshape(16, 8, LANES)
    return (jnp.concatenate([eta_t, potential_t], axis=1),)


def turn(block):
    return (block.reshape(-1, LANES).T,)


def turn_fields(block):
    return (block[:, 0:8].reshape(-1, LANES).T,)


def first_y(both, fa, turns, fb):
    eta = both[:, :8].reshape(LANES, LANES)
    potential = both[:, 8:].reshape(LANES, LANES)
    return forward(potential, fa, turns[:LANES], turns[LANES:], fb), eta


def magnitude(place, wave_x):
    line = lax.broadcasted_iota(jnp.int32, (LANES, LANES), 0) & 3
    wave_y = wavenumber(place[1] + 64 * place[0] + 16 * line, NYW)
    return jnp.sqrt(wave_x * wave_x + wave_y * wave_y)


def x_stage(powers, extra=None):
    def multiply(spec, kappa, power):
        factor = kappa
        for _ in range(power - 1):
            factor = factor * kappa
        return spec * (factor * (1.0 / (NXW * NYW)))

    def body(block, place, turns, fa, fb, ib, ia_pair, *more):
        cos_t, sin_t, kappa = [turns[i * LANES : (i + 1) * LANES] for i in range(3)]
        older, inputs = (more[:-2], more[-2:]) if extra else (more, ())
        spec = forward(block.reshape(LANES, LANES), fa, cos_t, sin_t, fb)
        other = older[0] if older else spec
        pair = jnp.concatenate(
            [multiply(spec, kappa, powers[0]), multiply(other, kappa, powers[1])], axis=0
        )
        inner = from_right(pair, ib)
        parts = []
        for field in range(2):
            rows = inner[field * LANES : (field + 1) * LANES]
            parts += twiddle(rows[:, :LANES], rows[:, LANES:], cos_t, sin_t)
        back = from_left(ia_pair, jnp.concatenate(parts, axis=0))
        if not extra:
            return (back,)
        every = slice(None)
        pieces = [((every, slice(0, 8)), back.reshape(32, 8, LANES))]
        pieces += [((peer, slice(8, 16)), tile) for peer, tile in extra(place, *inputs)]
        return pieces, spec

    return body


def halo_tiles(place, velocity, flat):
    edges = roll(flat, CY, 1)[:, :LANES]
    side = lax.shift_right_logical(lax.broadcasted_iota(jnp.int32, edges.shape, 1), 4)
    for start, first in ((0, CX - 2), (1, 0)):
        for tile in range(12):
            c, layer, half = tile // 4, tile // 2 % 2, tile % 2
            yield 16 * start + tile, velocity[c, first + layer, 8 * half : 8 * half + 8]
        yield 16 * start + 12, jnp.where(side == start, edges, 0.0)
        for tile in range(13, 16):
            yield 16 * start + tile, jnp.zeros((8, LANES), jnp.float32)


def forward_tiles(place, relay, unused):
    nothing = jnp.zeros((8, LANES), jnp.float32)
    for slab in range(32):
        below = relay[slab - 1, 8:16] if slab > 0 else nothing
        above = relay[slab + 1, 8:16] if slab < 31 else nothing
        yield slab, jnp.where(place[0] < 16, below, above)


def back_y(block, cos_t, sin_t, ib_pair, ia):
    inner = from_right(block.reshape(LANES, 2 * LANES), ib_pair)
    reals, imags = [], []
    for field in range(2):
        part = inner[:, 2 * field * LANES : 2 * (field + 1) * LANES]
        real, imag = twiddle(part[:, :LANES], part[:, LANES:], cos_t, sin_t)
        reals.append(real)
        imags.append(imag)
    stacked = jnp.concatenate(
        [jnp.concatenate(reals, axis=1), jnp.concatenate(imags, axis=1)], axis=0
    )
    fields = from_left(ia, stacked)
    return fields[:, :LANES], fields[:, LANES:]


def second_y(block, eta, fa, turns, fb, ib_pair, ia):
    cos_t, sin_t = turns[:LANES], turns[LANES:]
    slope_one, cubic_one = back_y(block, cos_t, sin_t, ib_pair, ia)
    spectrum = forward(-eta * slope_one, fa, cos_t, sin_t, fb)
    return spectrum, slope_one, cubic_one


def third_y(block, eta, fa, turns, fb, ib_pair, ia):
    cos_t, sin_t = turns[:LANES], turns[LANES:]
    slope_two, curve_one = back_y(block, cos_t, sin_t, ib_pair, ia)
    potential_three = -eta * slope_two - 0.5 * eta * eta * curve_one
    return forward(potential_three, fa, cos_t, sin_t, fb), slope_two, curve_one


def last_y(block, eta, slope_one, cubic_one, slope_two, curve_one, turns, ib_pair, ia):
    cos_t, sin_t = turns[:LANES], turns[LANES:]
    slope_three, curve_two = back_y(block, cos_t, sin_t, ib_pair, ia)
    vertical = (
        slope_one
        + slope_two
        + eta * curve_one
        + slope_three
        + eta * curve_two
        + 0.5 * eta * eta * cubic_one
    )
    return (vertical,)


def swap(values, axis):
    return lax.all_to_all(values, axis, 0, 0, tiled=True)


def beside(values, axis, work, *inputs):
    values, inputs = lax.optimization_barrier((values, inputs))
    moved = swap(values, axis)
    return lax.optimization_barrier((moved, work(*inputs)))


def wave_surface(surface_eta, surface_potential, velocity, place, work, inputs):
    square = (LANES, LANES)
    turns_y = [f32(np.concatenate([TAB_Y["cos_t"], TAB_Y["sin_t"]]))]
    fwd_y = [left_table(TAB_Y["fa"]), *turns_y, right_table(TAB_Y["fb"])]
    inv_y = [right_table(Y_IB_PAIR), left_table(TAB_Y["ia"])]

    def turn_to_slab(block):
        return run(loaded(turn), [square], block)[0].reshape(32, 4, LANES)

    def to_slab(block):
        return turn_to_slab(swap(block.reshape(16, 8, LANES), "pencil"))

    def to_pencil(block):
        (turned,) = run(turn_fields, [(LANES, 2 * LANES)], block)
        return swap(turned.reshape(16, 8, 2 * LANES), "pencil")

    pair, wide = (32, 8, LANES), (32, 16, LANES)
    (turned,) = run(
        loaded(turn_inputs), [(16, 16, LANES)], surface_eta, surface_potential, room=None
    )
    spectrum, eta = run(loaded(first_y), [square, square], swap(turned, "pencil"), *fwd_y)
    moved, (turns_x, *given) = beside(spectrum.reshape(16, 8, LANES), "pencil", work, *inputs)
    tab_x = [
        place,
        turns_x,
        left_table(TAB_X["fa"]),
        right_table(TAB_X["fb"]),
        right_table(TAB_X["ib"]),
        left_table(X_IA_PAIR),
    ]
    block = swap(turn_to_slab(moved), "slab")
    stage = x_stage((1, 3), halo_tiles)
    block, spec_one = run(
        loaded(stage), [wide, square], block.reshape(square), *tab_x, velocity, given[0]
    )
    relay = swap(block, "slab")
    spectrum, slope_one, cubic_one = run(
        loaded(second_y), [square] * 3, to_pencil(relay), eta, *fwd_y, *inv_y
    )
    block = swap(to_slab(spectrum), "slab").reshape(square)
    stage = x_stage((1, 2), forward_tiles)
    block, spec_two = run(loaded(stage), [wide, square], block, *tab_x, spec_one, relay, eta)
    halo = swap(block, "slab")
    spectrum, slope_two, curve_one = run(
        loaded(third_y), [square] * 3, to_pencil(halo), eta, *fwd_y, *inv_y
    )
    block = swap(to_slab(spectrum), "slab").reshape(square)
    (block,) = run(loaded(x_stage((1, 2))), [pair], block, *tab_x, spec_two)
    (vertical,) = run(
        loaded(last_y),
        [(16, 8, LANES)],
        to_pencil(swap(block, "slab")),
        eta,
        slope_one,
        cubic_one,
        slope_two,
        curve_one,
        *turns_y,
        *inv_y,
    )
    return swap(vertical, "pencil").reshape(square), halo, given


def wavenumber(index, length):
    folded = jnp.minimum(index, length - index)
    return 2.0 * math.pi / length * folded.astype(jnp.float32)


def ramp_weight(distance, reach_len):
    ratio = jnp.clip(1.0 - distance / reach_len, 0.0, 1.0)
    return ratio * ratio


def relax_of(cell_x, cell_y):
    pos_x, pos_y = cell_x.astype(jnp.float32), cell_y.astype(jnp.float32)
    reach_x = float(ZONE * CX)
    reach_y = float(CY)
    along_x = jnp.maximum(ramp_weight(pos_x, reach_x), ramp_weight(NX - 1.0 - pos_x, reach_x))
    across = jnp.maximum(ramp_weight(pos_y, reach_y), ramp_weight(NY - 1.0 - pos_y, reach_y))
    in_x = jnp.where((cell_x >= 0) & (cell_x < NX), 1.0, 0.0)
    in_y = jnp.where((cell_y >= 0) & (cell_y < NY), 1.0, 0.0)
    return jnp.maximum(along_x, across), in_x * in_y


def thirds(values):
    terms = []
    for _ in range(3):
        term = values.astype(jnp.bfloat16)
        terms.append(term)
        values = values - term.astype(jnp.float32)
    return jnp.concatenate(terms, axis=1)


def chosen(terms, lanes):
    count, parts = lanes.shape[1], terms.shape[1] // LANES
    iota = lax.broadcasted_iota(jnp.int32, (LANES, count), 0)
    hot = jnp.where(iota == lanes, 1.0, 0.0).astype(jnp.bfloat16)
    picked = jnp.dot(
        terms, jnp.concatenate([hot] * parts, axis=0), preferred_element_type=jnp.float32
    )
    return picked, lax.broadcasted_iota(jnp.int32, picked.shape, 0)


def listed(columns, points, row_count):
    terms = thirds(columns)
    rows = []
    for i in range(row_count):
        point = points[i : i + 1, :]
        picked, iota = chosen(terms, lax.shift_right_arithmetic(point, 7))
        found = jnp.where(iota == (point & (LANES - 1)), picked, 0.0)
        rows.append(jnp.sum(found, axis=0, keepdims=True))
    return rows


POINT_ROWS = 11


def pick_elevation(eta, points, place, turns):
    rows = listed(eta[...].T, points, POINT_ROWS)
    pieces = [(slice(i, i + 1), row) for i, row in enumerate(rows)]
    first = slice(0, 2 * LANES)
    kappa = magnitude(place, turns[2 * LANES : 3 * LANES])
    return pieces, [(first, turns[first]), (slice(2 * LANES, 3 * LANES), kappa)]


def pick_vertical(columns, points, eta_rows):
    columns = columns[...]
    rows = listed(columns, points, POINT_ROWS)
    pieces = [((slice(None), slice(None)), jnp.zeros((3 * LANES, LANES), jnp.float32))]

    def put(slab, place, row, half):
        at = slice(half * LANES, (half + 1) * LANES)
        for field, value in enumerate((eta_rows[row : row + 1, at], rows[row][:, at])):
            for block in range(3):
                line = 12 * (slab + 1 - block) + 4 * block + 2 * place + field
                if 0 <= line < 3 * LANES:
                    pieces.append(((slice(line, line + 1), slice(None)), value))

    for row, slab in enumerate((0, 1, 30, 31)):
        for half in range(2):
            put(slab, half, row, half)
    for slab in range(2, 30):
        put(slab, 0, 4 + (slab - 2) // 4, (slab - 2) % 4 // 2)
    return pieces, columns.T


def slots_of(stencil, slab, block):
    source, slot = lax.shift_right_logical(stencil, 8), stencil & 255
    in_zone = jnp.where((slab < ZONE) | (slab >= 32 - ZONE), 1, 0)
    lines = 12 * source + 4 * block + 2 * in_zone * lax.shift_right_logical(slot, 7)
    lanes = in_zone * (slot & 127) + (1 - in_zone) * ((slot & 63) + 64 * (slab & 1))
    return lines, lanes


def both_fields(terms, lines, lanes, shares):
    picked, iota = chosen(terms, lanes)
    picked = picked * shares
    return [jnp.where(iota == lines + field, picked, 0.0) for field in range(2)]


def summed(values):
    return jnp.sum(values, axis=0, keepdims=True)


def over_q(values):
    values = values + roll(values, 64, 1)
    return values + roll(values, 32, 1)


def sample(arrived, place, flat, halo, velocity):
    slab = place[0]
    terms = thirds(arrived[...])[:, : 2 * LANES]
    flat = flat[...]
    lines, lanes = slots_of(flat[0:4].astype(jnp.int32), slab, 1)
    weights = flat[4:8]
    shares = weights / jnp.sum(weights, axis=0, keepdims=True)
    totals = [0.0, 0.0]
    for q in range(4):
        at = slice(q, q + 1)
        found = both_fields(terms, lines[at], lanes[at], shares[at])
        totals = [total + part for total, part in zip(totals, found, strict=True)]
    rows = [summed(total) for total in totals]

    lane = lax.broadcasted_iota(jnp.int32, (8, LANES), 1)
    side = lax.shift_right_logical(lane, 4) & 1
    beside_x = halo[12, 8:16] + halo[28, 8:16]
    points, weight = in_lanes(beside_x, lane, 0), in_lanes(beside_x, lane, 4)
    lines, lanes = slots_of(points.astype(jnp.int32), slab - 1 + 2 * side, 2 * side)
    total = over_q(weight)
    shares = weight / jnp.where(total > 0.0, total, 1.0)
    for part in both_fields(terms, lines[0:1], lanes[0:1], shares[0:1]):
        value = over_q(jnp.broadcast_to(summed(part), (8, LANES)))[0:1]
        rows.append(jnp.concatenate([value, value], axis=1))

    sent = []
    for y_at in (CY - 2, 0):
        pieces = []
        for c in range(3):
            line = 20 * c
            for x in range(2):
                tile = 4 * c + 2 * x + y_at // 8
                at = slice(8 + y_at % 8, 10 + y_at % 8)
                pieces.append((line + x, halo[tile, at]))
                pieces.append((line + 18 + x, halo[16 + tile, at]))
            pieces.append((slice(line + 2, line + 18), velocity[c, :, y_at : y_at + 2]))
        for field in range(2):
            for half in range(2):
                at = (60 + field, slice(half, half + 1))
                pieces.append((at, rows[field][:, half * LANES : (half + 1) * LANES]))
        sent.append(pieces)
    here = jnp.concatenate(rows + [jnp.zeros((4, 256), jnp.float32)], axis=0)
    return here, *sent


def in_lanes(values, lane, first):
    result = jnp.zeros(values.shape, jnp.float32)
    for q in range(4):
        moved = jnp.broadcast_to(values[first + q : first + q + 1], values.shape)
        if q:
            moved = roll(moved, 32 * q, 1)
        result = jnp.where(lax.shift_right_logical(lane, 5) == q, moved, result)
    return result


def roll(values, shift, axis):
    return pltpu.roll(values, shift, axis)


def predicted_of(centers, neighbours):
    lane = lax.broadcasted_iota(jnp.int32, centers[0].shape, centers[0].ndim - 1)
    last = centers[0].ndim - 1
    results = []
    for center, (plus_x, minus_x, plus_y, minus_y) in zip(centers, neighbours, strict=True):
        plus_z = jnp.where(lane == CZ - 1, 0.0, roll(center, CZ - 1, last))
        minus_z = jnp.where(lane == 0, 0.0, roll(center, 1, last))
        laplace = plus_x + minus_x + (plus_y + minus_y) + (plus_z + minus_z) - 6.0 * center
        advect = (
            centers[0] * (plus_x - minus_x)
            + centers[1] * (plus_y - minus_y)
            + centers[2] * (plus_z - minus_z)
        )
        results.append(center + TIME_STEP * (VISCOSITY * laplace - 0.5 * advect))
    return results


def surface_columns(here, from_low, from_high):
    def lines_of(sent):
        lines = [
            jnp.concatenate([sent[60 + field, half : half + 1] for half in range(2)], axis=1)
            for field in range(2)
        ]
        return jnp.concatenate(lines + [jnp.zeros((6, 256), jnp.float32)], axis=0)

    lane = lax.broadcasted_iota(jnp.int32, (8, 256), 1)
    below, above = roll(lines_of(from_low), 241, 1), roll(lines_of(from_high), 15, 1)
    across_y = jnp.where(lane % CY == 0, below, above)
    surface = jnp.concatenate([here[...], across_y], axis=0).T
    return lambda index: surface[:, index : index + 1].reshape(CX, CY, 1)


def both_substeps(velocity, halo, from_low, from_high, here, place, decay, padded):
    for c in range(3):
        padded[c, 2:18, 8:24] = velocity[c]
        for tile in range(4):
            layer, half = tile // 2, tile % 2
            at = slice(8 + 8 * half, 16 + 8 * half)
            padded[c, layer, at] = halo[4 * c + tile, 8:16]
            padded[c, 18 + layer, at] = halo[16 + 4 * c + tile, 8:16]
        padded[c, :, 6:8] = from_low[20 * c : 20 * c + 20]
        padded[c, :, 24:26] = from_high[20 * c : 20 * c + 20]
    column = surface_columns(here, from_low, from_high)
    (keep, keep_x, keep_y), (pull, pull_x, pull_y) = relax_fields(place, decay[...])

    def region(x_at, x_to, y_at, y_to):
        def part(c, shift_x, shift_y):
            return padded[c, x_at + shift_x : x_to + shift_x, y_at + shift_y : y_to + shift_y]

        steps = ((1, 0), (-1, 0), (0, 1), (0, -1))
        centers = [part(c, 0, 0) for c in range(3)]
        return predicted_of(centers, [[part(c, *step) for step in steps] for c in range(3)])

    own = region(2, 18, 8, 24)
    sides_x = [region(1, 2, 8, 24), region(18, 19, 8, 24)]
    sides_y = [region(2, 18, 7, 8), region(2, 18, 24, 25)]

    shape = (CX, CY, CZ)
    row = lax.broadcasted_iota(jnp.int32, shape, 1)
    centers, neighbours, targets = [], [], []
    for c in range(3):
        center = own[c] * keep
        outer_x = [sides_x[side][c] * keep_x[side : side + 1] for side in range(2)]
        low, high = [jnp.broadcast_to(side[c], shape) for side in sides_y]
        outer_y = jnp.where(row == 0, low, high) * keep_y
        target = None
        if c != 1:
            field = c // 2
            target = pull * column(field)
            center = center + target
            line = column(2 + field)
            outer_x = [
                outer_x[0] + pull_x[0:1] * line[0:1],
                outer_x[1] + pull_x[1:2] * line[CX - 1 : CX],
            ]
            outer_y = outer_y + pull_y * column(8 + field)
        plus_x = jnp.concatenate([center[1:], outer_x[1]], axis=0)
        minus_x = jnp.concatenate([outer_x[0], center[:-1]], axis=0)
        plus_y = jnp.where(row == CY - 1, outer_y, roll(center, CY - 1, 1))
        minus_y = jnp.where(row == 0, outer_y, roll(center, 1, 1))
        centers.append(center)
        neighbours.append((plus_x, minus_x, plus_y, minus_y))
        targets.append(target)
    pieces = []
    for c, value in enumerate(predicted_of(centers, neighbours)):
        value = value * keep
        pieces.append((c, value if targets[c] is None else value + targets[c]))
    return (pieces,)


def shifted(values, axis, step):
    size = lax.axis_size(axis)
    pairs = [(i, i + step) for i in range(size) if 0 <= i + step < size]
    return lax.ppermute(values, axis, pairs)


def list_points(send_point, send_count):
    slot = lax.broadcasted_iota(jnp.int32, (32, 256), 1)
    points = jnp.where(slot < send_count[0, 0][:, None], send_point[0, 0], -1)
    inner = points[2:30, :64].reshape(7, 256)
    return jnp.concatenate([points[:2], points[30:], inner], axis=0)


DECAY = np.exp(-DEPTH_RATE * (CZ - 1.0 - np.arange(CZ)) / CZ).astype(np.float32)


def relax_fields(place, decay):
    def fields(cell_x, cell_y):
        relax, inside = relax_of(cell_x, cell_y)
        return (1.0 - relax) * inside, relax * inside * decay.reshape(1, 1, CZ)

    side = lax.broadcasted_iota(jnp.int32, (2, 1, CZ), 0)
    row = lax.broadcasted_iota(jnp.int32, (1, CY, CZ), 1)
    cell_x = place[0] * CX + lax.broadcasted_iota(jnp.int32, (CX, 1, CZ), 0)
    cell_y = place[1] * CY + row
    out_x = place[0] * CX - 1 + (CX + 1) * side
    out_y = cell_y + jnp.where(row == 0, -1, jnp.where(row == CY - 1, 1, 0))
    own, across_x, across_y = fields(cell_x, cell_y), fields(out_x, cell_y), fields(cell_x, out_y)
    return (own[0], across_x[0], across_y[0]), (own[1], across_x[1], across_y[1])


def flat_stencil(stencil, interp_weight):
    rows = [stencil.astype(jnp.float32), interp_weight]
    return jnp.concatenate(rows, axis=0).reshape(8, CX * CY)


def on_device(
    surface_eta, surface_potential, velocity, send_point, send_count, stencil, interp_weight
):
    place = jnp.stack([lax.axis_index("slab"), lax.axis_index("pencil")])
    surface_eta, place = lax.optimization_barrier((surface_eta, place))
    square = (LANES, LANES)

    def lists(eta, place, send_point, send_count, stencil, interp_weight):
        points = list_points(send_point, send_count)
        shapes = [(POINT_ROWS, 256), TURNS_X.shape]
        rows, turns_x = run(pick_elevation, shapes, eta, points, place, f32(TURNS_X))
        return turns_x, flat_stencil(stencil, interp_weight), points, rows

    columns, halo, (flat, points, eta_rows) = wave_surface(
        surface_eta,
        surface_potential,
        velocity,
        place,
        lists,
        (surface_eta, place, send_point, send_count, stencil, interp_weight),
    )
    outgoing, vertical = run(
        pick_vertical, [(3 * LANES, LANES), square], columns, points, eta_rows
    )
    arrived = swap(outgoing.reshape(32, 3, 4, LANES), "slab").reshape(3 * LANES, LANES)
    sent = (62, 2, LANES)
    here, upward, downward = run(
        sample, [(8, 256), sent, sent], arrived, place, flat, halo, velocity
    )
    from_low, from_high = shifted(upward, "pencil", 1), shifted(downward, "pencil", -1)
    (velocity,) = run(
        both_substeps,
        [(3, CX, CY, CZ)],
        velocity,
        halo,
        from_low,
        from_high,
        here,
        place,
        jnp.asarray(DECAY[None]),
        scratch=[(3, 20, 32, CZ)],
    )
    return (vertical, velocity)


def solution(mesh):
    in_specs = (
        P("pencil", "slab"),
        P("pencil", "slab"),
        P(None, "slab", "pencil", None),
        P("slab", "pencil", None, None),
        P("slab", "pencil", None),
        P(None, "slab", "pencil"),
        P(None, "slab", "pencil"),
    )
    out_specs = (P("pencil", "slab"), P(None, "slab", "pencil", None))
    return jax.shard_map(
        on_device, mesh=mesh, in_specs=in_specs, out_specs=out_specs, check_vma=False
    )
```

```python
import math

import jax
import jax.numpy as jnp
import ml_dtypes
import numpy as np
from jax import lax
from jax.experimental import pallas as pl
from jax.experimental.pallas import tpu as pltpu
from jax.sharding import PartitionSpec as P

NXW = 4096
NYW = 2048
LANES = 128
CX = 16
CY = 16
CZ = 128
NX = 512
NY = 256
ZONE = 2

TIME_STEP = 0.2
VISCOSITY = 0.6
DEPTH_RATE = 3.0


def stage_tables(peers):
    copies = LANES // peers
    length = peers * LANES
    outer = np.arange(peers)
    inner = np.arange(LANES)
    eye = np.eye(copies)
    angle_a = 2.0 * np.pi / peers * (outer[:, None] * outer[None, :] % peers)
    angle_t = 2.0 * np.pi / length * (outer[:, None] * inner[None, :] % length)
    angle_b = 2.0 * np.pi / LANES * (inner[:, None] * inner[None, :] % LANES)
    cos_a, sin_a = np.kron(np.cos(angle_a), eye), np.kron(np.sin(angle_a), eye)
    cos_b, sin_b = np.cos(angle_b), np.sin(angle_b)
    tables = {
        "fa": np.concatenate([cos_a, -sin_a], axis=0),
        "cos_t": np.repeat(np.cos(angle_t), copies, axis=0),
        "sin_t": np.repeat(np.sin(angle_t), copies, axis=0),
        "fb": np.concatenate([cos_b + sin_b, sin_b - cos_b], axis=0),
        "ib": np.concatenate([cos_b, -sin_b], axis=1),
        "ia": np.concatenate([cos_a + sin_a, sin_a - cos_a], axis=1),
    }
    return tables


TAB_Y = stage_tables(16)
TAB_X = stage_tables(32)


def pair_inverse_b(ib):
    rows = ib.reshape(32, 4, 2 * LANES)
    big = np.zeros((32, 2, 4, 2, 2 * LANES))
    for field in range(2):
        big[:, field, :, field, :] = rows
    return big.reshape(2 * LANES, 4 * LANES)


def pair_inverse_a(ia):
    rows = ia.reshape(32, 4, 2 * LANES)
    big = np.zeros((32, 2, 4, 2, 2 * LANES))
    for field in range(2):
        big[:, field, :, field, :] = rows
    return big.reshape(2 * LANES, 4 * LANES)


Y_IB_PAIR = pair_inverse_b(TAB_Y["ib"])
X_IA_PAIR = pair_inverse_a(TAB_X["ia"])


def f32(array):
    return jnp.asarray(np.asarray(array, np.float32))


def halves_of(table):
    high = table.astype(ml_dtypes.bfloat16)
    return high, (table - high.astype(np.float64)).astype(ml_dtypes.bfloat16)


def left_table(table):
    high, low = halves_of(table)
    return jnp.asarray(np.concatenate([high, high, low], axis=1))


def right_table(table):
    high, low = halves_of(table)
    return jnp.asarray(np.concatenate([high, low, high], axis=0))


def halves(values):
    high = values.astype(jnp.bfloat16)
    return high, (values - high.astype(jnp.float32)).astype(jnp.bfloat16)


def from_left(table, values):
    high, low = halves(values)
    stacked = jnp.concatenate([high, low, high], axis=0)
    return jnp.dot(table, stacked, preferred_element_type=jnp.float32)


def from_right(values, table):
    high, low = halves(values)
    joined = jnp.concatenate([high, high, low], axis=1)
    return jnp.dot(joined, table, preferred_element_type=jnp.float32)


INDEX_X = np.arange(LANES)[:, None] // 4 + 32 * np.arange(LANES)[None, :]
WAVE_X = np.float32(2.0 * math.pi / NXW) * np.minimum(INDEX_X, NXW - INDEX_X).astype(np.float32)
TURNS_X = np.concatenate([TAB_X["cos_t"], TAB_X["sin_t"], WAVE_X])


def twiddle(real, imag, cos_t, sin_t):
    return real * cos_t + imag * sin_t, imag * cos_t - real * sin_t


def forward(block, fa, cos_t, sin_t, fb):
    outer = from_left(fa, block)
    real, imag = twiddle(outer[:LANES], outer[LANES:], cos_t, sin_t)
    return from_right(jnp.concatenate([real, imag], axis=1), fb)


def run(body, outs, *args, room=8, scratch=()):
    shapes = [jax.ShapeDtypeStruct(shape, jnp.float32) for shape in outs]

    def kernel(*refs):
        inputs, rest = refs[: len(args)], refs[len(args) :]
        results = body(*inputs, *rest[len(outs) :])
        for ref, result in zip(rest[: len(outs)], results, strict=True):
            for index, piece in result if isinstance(result, list) else [(..., result)]:
                ref[index] = piece.reshape(ref.shape) if index is ... else piece

    params = pltpu.CompilerParams(vmem_limit_bytes=room << 20) if room else None
    call = pl.pallas_call(
        kernel,
        out_shape=shapes,
        scratch_shapes=[pltpu.VMEM(shape, jnp.float32) for shape in scratch],
        compiler_params=params,
    )
    return call(*args)


def loaded(body):
    return lambda *refs: body(*[ref[...] for ref in refs])


def turn_inputs(eta, potential):
    eta_t = eta.T.reshape(16, 8, LANES)
    potential_t = potential.T.reshape(16, 8, LANES)
    return (jnp.concatenate([eta_t, potential_t], axis=1),)


def turn(block):
    return (block.reshape(-1, LANES).T,)


def turn_fields(block):
    return (block[:, 0:8].reshape(-1, LANES).T,)


def first_y(both, fa, turns, fb):
    eta = both[:, :8].reshape(LANES, LANES)
    potential = both[:, 8:].reshape(LANES, LANES)
    return forward(potential, fa, turns[:LANES], turns[LANES:], fb), eta


def magnitude(place, wave_x):
    line = lax.broadcasted_iota(jnp.int32, (LANES, LANES), 0) & 3
    wave_y = wavenumber(place[1:2, :] + 64 * place[0:1, :] + 16 * line, NYW)
    return jnp.sqrt(wave_x * wave_x + wave_y * wave_y)


def x_stage(powers, extra=None):
    def multiply(spec, kappa, power):
        factor = kappa
        for _ in range(power - 1):
            factor = factor * kappa
        return spec * (factor * (1.0 / (NXW * NYW)))

    def body(block, turns, fa, fb, ib, ia_pair, *more):
        cos_t, sin_t, kappa = [turns[i * LANES : (i + 1) * LANES] for i in range(3)]
        older, inputs = (more[:-2], more[-2:]) if extra else (more, ())
        spec = forward(block.reshape(LANES, LANES), fa, cos_t, sin_t, fb)
        other = older[0] if older else spec
        pair = jnp.concatenate(
            [multiply(spec, kappa, powers[0]), multiply(other, kappa, powers[1])], axis=0
        )
        inner = from_right(pair, ib)
        parts = []
        for field in range(2):
            rows = inner[field * LANES : (field + 1) * LANES]
            parts += twiddle(rows[:, :LANES], rows[:, LANES:], cos_t, sin_t)
        back = from_left(ia_pair, jnp.concatenate(parts, axis=0))
        if not extra:
            return (back,)
        every = slice(None)
        pieces = [((every, slice(0, 8)), back.reshape(32, 8, LANES))]
        pieces += [((peer, slice(8, 16)), tile) for peer, tile in extra(*inputs)]
        return pieces, spec

    return body


def halo_tiles(velocity, flat):
    edges = roll(flat, CY, 1)[:, :LANES]
    side = lax.shift_right_logical(lax.broadcasted_iota(jnp.int32, edges.shape, 1), 4)
    for start, first in ((0, CX - 2), (1, 0)):
        for tile in range(12):
            c, layer, half = tile // 4, tile // 2 % 2, tile % 2
            yield 16 * start + tile, velocity[c, first + layer, 8 * half : 8 * half + 8]
        yield 16 * start + 12, jnp.where(side == start, edges, 0.0)
        for tile in range(13, 16):
            yield 16 * start + tile, jnp.zeros((8, LANES), jnp.float32)


def forward_tiles(relay, place):
    nothing = jnp.zeros((8, LANES), jnp.float32)
    for slab in range(32):
        below = relay[slab - 1, 8:16] if slab > 0 else nothing
        above = relay[slab + 1, 8:16] if slab < 31 else nothing
        yield slab, jnp.where(place[0:1, :] < 16, below, above)


def back_y(block, cos_t, sin_t, ib_pair, ia):
    inner = from_right(block.reshape(LANES, 2 * LANES), ib_pair)
    reals, imags = [], []
    for field in range(2):
        part = inner[:, 2 * field * LANES : 2 * (field + 1) * LANES]
        real, imag = twiddle(part[:, :LANES], part[:, LANES:], cos_t, sin_t)
        reals.append(real)
        imags.append(imag)
    stacked = jnp.concatenate(
        [jnp.concatenate(reals, axis=1), jnp.concatenate(imags, axis=1)], axis=0
    )
    fields = from_left(ia, stacked)
    return fields[:, :LANES], fields[:, LANES:]


def second_y(block, eta, fa, turns, fb, ib_pair, ia):
    cos_t, sin_t = turns[:LANES], turns[LANES:]
    slope_one, cubic_one = back_y(block, cos_t, sin_t, ib_pair, ia)
    spectrum = forward(-eta * slope_one, fa, cos_t, sin_t, fb)
    return spectrum, slope_one, cubic_one


def third_y(block, eta, fa, turns, fb, ib_pair, ia):
    cos_t, sin_t = turns[:LANES], turns[LANES:]
    slope_two, curve_one = back_y(block, cos_t, sin_t, ib_pair, ia)
    potential_three = -eta * slope_two - 0.5 * eta * eta * curve_one
    return forward(potential_three, fa, cos_t, sin_t, fb), slope_two, curve_one


def last_y(block, eta, slope_one, cubic_one, slope_two, curve_one, turns, ib_pair, ia):
    cos_t, sin_t = turns[:LANES], turns[LANES:]
    slope_three, curve_two = back_y(block, cos_t, sin_t, ib_pair, ia)
    vertical = (
        slope_one
        + slope_two
        + eta * curve_one
        + slope_three
        + eta * curve_two
        + 0.5 * eta * eta * cubic_one
    )
    return (vertical,)


def swap(values, axis):
    return lax.all_to_all(values, axis, 0, 0, tiled=True)


def beside(values, axis, work, *inputs):
    values, inputs = lax.optimization_barrier((values, inputs))
    moved = swap(values, axis)
    return lax.optimization_barrier((moved, work(*inputs)))


def wave_surface(surface_eta, surface_potential, velocity, place, work, inputs):
    square = (LANES, LANES)
    turns_y = [f32(np.concatenate([TAB_Y["cos_t"], TAB_Y["sin_t"]]))]
    fwd_y = [left_table(TAB_Y["fa"]), *turns_y, right_table(TAB_Y["fb"])]
    inv_y = [right_table(Y_IB_PAIR), left_table(TAB_Y["ia"])]

    def to_slab(block):
        (turned,) = run(loaded(turn), [square], swap(block.reshape(16, 8, LANES), "pencil"))
        return turned.reshape(32, 4, LANES)

    def to_pencil(block):
        (turned,) = run(turn_fields, [(LANES, 2 * LANES)], block)
        return swap(turned.reshape(16, 8, 2 * LANES), "pencil")

    pair, wide = (32, 8, LANES), (32, 16, LANES)
    (turned,) = run(
        loaded(turn_inputs), [(16, 16, LANES)], surface_eta, surface_potential, room=None
    )
    both, (turns_x, *given) = beside(turned, "pencil", work, *inputs)
    spectrum, eta = run(loaded(first_y), [square, square], both, *fwd_y)
    tab_x = [
        turns_x,
        left_table(TAB_X["fa"]),
        right_table(TAB_X["fb"]),
        right_table(TAB_X["ib"]),
        left_table(X_IA_PAIR),
    ]
    block = swap(to_slab(spectrum), "slab")
    stage = x_stage((1, 3), halo_tiles)
    block, spec_one = run(
        loaded(stage), [wide, square], block.reshape(square), *tab_x, velocity, given[0]
    )
    relay = swap(block, "slab")
    spectrum, slope_one, cubic_one = run(
        loaded(second_y), [square] * 3, to_pencil(relay), eta, *fwd_y, *inv_y
    )
    block = swap(to_slab(spectrum), "slab").reshape(square)
    stage = x_stage((1, 2), forward_tiles)
    block, spec_two = run(loaded(stage), [wide, square], block, *tab_x, spec_one, relay, place)
    halo = swap(block, "slab")
    spectrum, slope_two, curve_one = run(
        loaded(third_y), [square] * 3, to_pencil(halo), eta, *fwd_y, *inv_y
    )
    block = swap(to_slab(spectrum), "slab").reshape(square)
    (block,) = run(loaded(x_stage((1, 2))), [pair], block, *tab_x, spec_two)
    (vertical,) = run(
        loaded(last_y),
        [(16, 8, LANES)],
        to_pencil(swap(block, "slab")),
        eta,
        slope_one,
        cubic_one,
        slope_two,
        curve_one,
        *turns_y,
        *inv_y,
    )
    return swap(vertical, "pencil").reshape(square), halo, given


def wavenumber(index, length):
    folded = jnp.minimum(index, length - index)
    return 2.0 * math.pi / length * folded.astype(jnp.float32)


def ramp_weight(distance, reach_len):
    ratio = jnp.clip(1.0 - distance / reach_len, 0.0, 1.0)
    return ratio * ratio


def relax_of(cell_x, cell_y):
    pos_x, pos_y = cell_x.astype(jnp.float32), cell_y.astype(jnp.float32)
    reach_x = float(ZONE * CX)
    reach_y = float(CY)
    along_x = jnp.maximum(ramp_weight(pos_x, reach_x), ramp_weight(NX - 1.0 - pos_x, reach_x))
    across = jnp.maximum(ramp_weight(pos_y, reach_y), ramp_weight(NY - 1.0 - pos_y, reach_y))
    in_x = jnp.where((cell_x >= 0) & (cell_x < NX), 1.0, 0.0)
    in_y = jnp.where((cell_y >= 0) & (cell_y < NY), 1.0, 0.0)
    return jnp.maximum(along_x, across), in_x * in_y


def thirds(values):
    terms = []
    for _ in range(3):
        term = values.astype(jnp.bfloat16)
        terms.append(term)
        values = values - term.astype(jnp.float32)
    return jnp.concatenate(terms, axis=1)


def chosen(terms, lanes):
    count, parts = lanes.shape[1], terms.shape[1] // LANES
    iota = lax.broadcasted_iota(jnp.int32, (LANES, count), 0)
    hot = jnp.where(iota == lanes, 1.0, 0.0).astype(jnp.bfloat16)
    picked = jnp.dot(
        terms, jnp.concatenate([hot] * parts, axis=0), preferred_element_type=jnp.float32
    )
    return picked, lax.broadcasted_iota(jnp.int32, picked.shape, 0)


def listed(columns, points, row_count):
    terms = thirds(columns)
    rows = []
    for i in range(row_count):
        point = points[i : i + 1, :]
        picked, iota = chosen(terms, lax.shift_right_arithmetic(point, 7))
        found = jnp.where(iota == (point & (LANES - 1)), picked, 0.0)
        rows.append(jnp.sum(found, axis=0, keepdims=True))
    return rows


POINT_ROWS = 11


def pick_elevation(eta, points, place, turns):
    rows = listed(eta[...].T, points, POINT_ROWS)
    pieces = [(slice(i, i + 1), row) for i, row in enumerate(rows)]
    first = slice(0, 2 * LANES)
    kappa = magnitude(place, turns[2 * LANES : 3 * LANES])
    return pieces, [(first, turns[first]), (slice(2 * LANES, 3 * LANES), kappa)]


def pick_vertical(columns, points, eta_rows):
    columns = columns[...]
    rows = listed(columns, points, POINT_ROWS)
    pieces = [((slice(None), slice(None)), jnp.zeros((3 * LANES, LANES), jnp.float32))]

    def put(slab, place, row, half):
        at = slice(half * LANES, (half + 1) * LANES)
        for field, value in enumerate((eta_rows[row : row + 1, at], rows[row][:, at])):
            for block in range(3):
                line = 12 * (slab + 1 - block) + 4 * block + 2 * place + field
                if 0 <= line < 3 * LANES:
                    pieces.append(((slice(line, line + 1), slice(None)), value))

    for row, slab in enumerate((0, 1, 30, 31)):
        for half in range(2):
            put(slab, half, row, half)
    for slab in range(2, 30):
        put(slab, 0, 4 + (slab - 2) // 4, (slab - 2) % 4 // 2)
    return pieces, columns.T


def slots_of(stencil, slab, block):
    source, slot = lax.shift_right_logical(stencil, 8), stencil & 255
    in_zone = jnp.where((slab < ZONE) | (slab >= 32 - ZONE), 1, 0)
    lines = 12 * source + 4 * block + 2 * in_zone * lax.shift_right_logical(slot, 7)
    lanes = in_zone * (slot & 127) + (1 - in_zone) * ((slot & 63) + 64 * (slab & 1))
    return lines, lanes


def both_fields(terms, lines, lanes, shares):
    picked, iota = chosen(terms, lanes)
    picked = picked * shares
    return [jnp.where(iota == lines + field, picked, 0.0) for field in range(2)]


def summed(values):
    return jnp.sum(values, axis=0, keepdims=True)


def over_q(values):
    values = values + roll(values, 64, 1)
    return values + roll(values, 32, 1)


def sample(arrived, place, flat, halo, velocity):
    slab = jnp.concatenate([place[0:1, :]] * 2, axis=1)
    terms = thirds(arrived[...])[:, : 2 * LANES]
    flat = flat[...]
    lines, lanes = slots_of(flat[0:4].astype(jnp.int32), slab, 1)
    weights = flat[4:8]
    shares = weights / jnp.sum(weights, axis=0, keepdims=True)
    totals = [0.0, 0.0]
    for q in range(4):
        at = slice(q, q + 1)
        found = both_fields(terms, lines[at], lanes[at], shares[at])
        totals = [total + part for total, part in zip(totals, found, strict=True)]
    rows = [summed(total) for total in totals]

    lane = lax.broadcasted_iota(jnp.int32, (8, LANES), 1)
    side = lax.shift_right_logical(lane, 4) & 1
    beside_x = halo[12, 8:16] + halo[28, 8:16]
    points, weight = in_lanes(beside_x, lane, 0), in_lanes(beside_x, lane, 4)
    lines, lanes = slots_of(points.astype(jnp.int32), place[0:1, :] - 1 + 2 * side, 2 * side)
    total = over_q(weight)
    shares = weight / jnp.where(total > 0.0, total, 1.0)
    for part in both_fields(terms, lines[0:1], lanes[0:1], shares[0:1]):
        value = over_q(jnp.broadcast_to(summed(part), (8, LANES)))[0:1]
        rows.append(jnp.concatenate([value, value], axis=1))

    sent = []
    for y_at in (CY - 2, 0):
        pieces = []
        for c in range(3):
            line = 20 * c
            for x in range(2):
                tile = 4 * c + 2 * x + y_at // 8
                at = slice(8 + y_at % 8, 10 + y_at % 8)
                pieces.append((line + x, halo[tile, at]))
                pieces.append((line + 18 + x, halo[16 + tile, at]))
            pieces.append((slice(line + 2, line + 18), velocity[c, :, y_at : y_at + 2]))
        for field in range(2):
            for half in range(2):
                at = (60 + field, slice(half, half + 1))
                pieces.append((at, rows[field][:, half * LANES : (half + 1) * LANES]))
        sent.append(pieces)
    here = jnp.concatenate(rows + [jnp.zeros((4, 256), jnp.float32)], axis=0)
    return here, *sent


def in_lanes(values, lane, first):
    result = jnp.zeros(values.shape, jnp.float32)
    for q in range(4):
        moved = jnp.broadcast_to(values[first + q : first + q + 1], values.shape)
        if q:
            moved = roll(moved, 32 * q, 1)
        result = jnp.where(lax.shift_right_logical(lane, 5) == q, moved, result)
    return result


def roll(values, shift, axis):
    return pltpu.roll(values, shift, axis)


def predicted_of(centers, neighbours):
    lane = lax.broadcasted_iota(jnp.int32, centers[0].shape, centers[0].ndim - 1)
    last = centers[0].ndim - 1
    results = []
    for center, (plus_x, minus_x, plus_y, minus_y) in zip(centers, neighbours, strict=True):
        plus_z = jnp.where(lane == CZ - 1, 0.0, roll(center, CZ - 1, last))
        minus_z = jnp.where(lane == 0, 0.0, roll(center, 1, last))
        laplace = plus_x + minus_x + (plus_y + minus_y) + (plus_z + minus_z) - 6.0 * center
        advect = (
            centers[0] * (plus_x - minus_x)
            + centers[1] * (plus_y - minus_y)
            + centers[2] * (plus_z - minus_z)
        )
        results.append(center + TIME_STEP * (VISCOSITY * laplace - 0.5 * advect))
    return results


def surface_columns(here, from_low, from_high):
    def lines_of(sent):
        lines = [
            jnp.concatenate([sent[60 + field, half : half + 1] for half in range(2)], axis=1)
            for field in range(2)
        ]
        return jnp.concatenate(lines + [jnp.zeros((6, 256), jnp.float32)], axis=0)

    lane = lax.broadcasted_iota(jnp.int32, (8, 256), 1)
    below, above = roll(lines_of(from_low), 241, 1), roll(lines_of(from_high), 15, 1)
    across_y = jnp.where(lane % CY == 0, below, above)
    surface = jnp.concatenate([here[...], across_y], axis=0).T
    return lambda index: surface[:, index : index + 1].reshape(CX, CY, 1)


def both_substeps(velocity, halo, from_low, from_high, here, place, decay, padded):
    for c in range(3):
        padded[c, 2:18, 8:24] = velocity[c]
        for tile in range(4):
            layer, half = tile // 2, tile % 2
            at = slice(8 + 8 * half, 16 + 8 * half)
            padded[c, layer, at] = halo[4 * c + tile, 8:16]
            padded[c, 18 + layer, at] = halo[16 + 4 * c + tile, 8:16]
        padded[c, :, 6:8] = from_low[20 * c : 20 * c + 20]
        padded[c, :, 24:26] = from_high[20 * c : 20 * c + 20]
    column = surface_columns(here, from_low, from_high)
    (keep, keep_x, keep_y), (pull, pull_x, pull_y) = relax_fields(place, decay[...])

    def region(x_at, x_to, y_at, y_to):
        def part(c, shift_x, shift_y):
            return padded[c, x_at + shift_x : x_to + shift_x, y_at + shift_y : y_to + shift_y]

        steps = ((1, 0), (-1, 0), (0, 1), (0, -1))
        centers = [part(c, 0, 0) for c in range(3)]
        return predicted_of(centers, [[part(c, *step) for step in steps] for c in range(3)])

    own = region(2, 18, 8, 24)
    sides_x = [region(1, 2, 8, 24), region(18, 19, 8, 24)]
    sides_y = [region(2, 18, 7, 8), region(2, 18, 24, 25)]

    shape = (CX, CY, CZ)
    row = lax.broadcasted_iota(jnp.int32, shape, 1)
    centers, neighbours, targets = [], [], []
    for c in range(3):
        center = own[c] * keep
        outer_x = [sides_x[side][c] * keep_x[side : side + 1] for side in range(2)]
        low, high = [jnp.broadcast_to(side[c], shape) for side in sides_y]
        outer_y = jnp.where(row == 0, low, high) * keep_y
        target = None
        if c != 1:
            field = c // 2
            target = pull * column(field)
            center = center + target
            line = column(2 + field)
            outer_x = [
                outer_x[0] + pull_x[0:1] * line[0:1],
                outer_x[1] + pull_x[1:2] * line[CX - 1 : CX],
            ]
            outer_y = outer_y + pull_y * column(8 + field)
        plus_x = jnp.concatenate([center[1:], outer_x[1]], axis=0)
        minus_x = jnp.concatenate([outer_x[0], center[:-1]], axis=0)
        plus_y = jnp.where(row == CY - 1, outer_y, roll(center, CY - 1, 1))
        minus_y = jnp.where(row == 0, outer_y, roll(center, 1, 1))
        centers.append(center)
        neighbours.append((plus_x, minus_x, plus_y, minus_y))
        targets.append(target)
    pieces = []
    for c, value in enumerate(predicted_of(centers, neighbours)):
        value = value * keep
        pieces.append((c, value if targets[c] is None else value + targets[c]))
    return (pieces,)


def shifted(values, axis, step):
    size = lax.axis_size(axis)
    pairs = [(i, i + step) for i in range(size) if 0 <= i + step < size]
    return lax.ppermute(values, axis, pairs)


def list_points(send_point, send_count):
    slot = lax.broadcasted_iota(jnp.int32, (32, 256), 1)
    points = jnp.where(slot < send_count[0, 0][:, None], send_point[0, 0], -1)
    inner = points[2:30, :64].reshape(7, 256)
    return jnp.concatenate([points[:2], points[30:], inner], axis=0)


DECAY = np.exp(-DEPTH_RATE * (CZ - 1.0 - np.arange(CZ)) / CZ).astype(np.float32)


def relax_fields(place, decay):
    def fields(cell_x, cell_y):
        relax, inside = relax_of(cell_x, cell_y)
        return (1.0 - relax) * inside, relax * inside * decay.reshape(1, 1, CZ)

    side = lax.broadcasted_iota(jnp.int32, (2, 1, CZ), 0)
    row = lax.broadcasted_iota(jnp.int32, (1, CY, CZ), 1)
    slab, pencil = place[0:1, :].reshape(1, 1, CZ), place[1:2, :].reshape(1, 1, CZ)
    cell_x = slab * CX + lax.broadcasted_iota(jnp.int32, (CX, 1, CZ), 0)
    cell_y = pencil * CY + row
    out_x = slab * CX - 1 + (CX + 1) * side
    out_y = cell_y + jnp.where(row == 0, -1, jnp.where(row == CY - 1, 1, 0))
    own, across_x, across_y = fields(cell_x, cell_y), fields(out_x, cell_y), fields(cell_x, out_y)
    return (own[0], across_x[0], across_y[0]), (own[1], across_x[1], across_y[1])


def flat_stencil(stencil, interp_weight):
    rows = [stencil.astype(jnp.float32), interp_weight]
    return jnp.concatenate(rows, axis=0).reshape(8, CX * CY)


def on_device(
    surface_eta, surface_potential, velocity, send_point, send_count, stencil, interp_weight
):
    line = lax.broadcasted_iota(jnp.int32, (8, LANES), 0)
    place = jnp.where(line == 0, lax.axis_index("slab"), lax.axis_index("pencil"))
    surface_eta, place = lax.optimization_barrier((surface_eta, place))
    square = (LANES, LANES)

    def lists(eta, place, send_point, send_count, stencil, interp_weight):
        points = list_points(send_point, send_count)
        shapes = [(POINT_ROWS, 256), TURNS_X.shape]
        rows, turns_x = run(pick_elevation, shapes, eta, points, place, f32(TURNS_X))
        return turns_x, flat_stencil(stencil, interp_weight), points, rows

    columns, halo, (flat, points, eta_rows) = wave_surface(
        surface_eta,
        surface_potential,
        velocity,
        place,
        lists,
        (surface_eta, place, send_point, send_count, stencil, interp_weight),
    )
    outgoing, vertical = run(
        pick_vertical, [(3 * LANES, LANES), square], columns, points, eta_rows
    )
    arrived = swap(outgoing.reshape(32, 3, 4, LANES), "slab").reshape(3 * LANES, LANES)
    sent = (62, 2, LANES)
    here, upward, downward = run(
        sample, [(8, 256), sent, sent], arrived, place, flat, halo, velocity
    )
    from_low, from_high = shifted(upward, "pencil", 1), shifted(downward, "pencil", -1)
    (velocity,) = run(
        both_substeps,
        [(3, CX, CY, CZ)],
        velocity,
        halo,
        from_low,
        from_high,
        here,
        place,
        jnp.asarray(DECAY[None]),
        scratch=[(3, 20, 32, CZ)],
    )
    return (vertical, velocity)


def solution(mesh):
    in_specs = (
        P("pencil", "slab"),
        P("pencil", "slab"),
        P(None, "slab", "pencil", None),
        P("slab", "pencil", None, None),
        P("slab", "pencil", None),
        P(None, "slab", "pencil"),
        P(None, "slab", "pencil"),
    )
    out_specs = (P("pencil", "slab"), P(None, "slab", "pencil", None))
    return jax.shard_map(
        on_device, mesh=mesh, in_specs=in_specs, out_specs=out_specs, check_vma=False
    )
```

```python
import math

import jax
import jax.numpy as jnp
import ml_dtypes
import numpy as np
from jax import lax
from jax.experimental import pallas as pl
from jax.experimental.pallas import tpu as pltpu
from jax.sharding import PartitionSpec as P

NXW = 4096
NYW = 2048
LANES = 128
CX = 16
CY = 16
CZ = 128
NX = 512
NY = 256
ZONE = 2

TIME_STEP = 0.2
VISCOSITY = 0.6
DEPTH_RATE = 3.0


def stage_tables(peers):
    copies = LANES // peers
    length = peers * LANES
    outer = np.arange(peers)
    inner = np.arange(LANES)
    eye = np.eye(copies)
    angle_a = 2.0 * np.pi / peers * (outer[:, None] * outer[None, :] % peers)
    angle_t = 2.0 * np.pi / length * (outer[:, None] * inner[None, :] % length)
    angle_b = 2.0 * np.pi / LANES * (inner[:, None] * inner[None, :] % LANES)
    cos_a, sin_a = np.kron(np.cos(angle_a), eye), np.kron(np.sin(angle_a), eye)
    cos_b, sin_b = np.cos(angle_b), np.sin(angle_b)
    tables = {
        "fa": np.concatenate([cos_a, -sin_a], axis=0),
        "cos_t": np.repeat(np.cos(angle_t), copies, axis=0),
        "sin_t": np.repeat(np.sin(angle_t), copies, axis=0),
        "fb": np.concatenate([cos_b + sin_b, sin_b - cos_b], axis=0),
        "ib": np.concatenate([cos_b, -sin_b], axis=1),
        "ia": np.concatenate([cos_a + sin_a, sin_a - cos_a], axis=1),
    }
    return tables


TAB_Y = stage_tables(16)
TAB_X = stage_tables(32)


def pair_inverse_b(ib):
    rows = ib.reshape(32, 4, 2 * LANES)
    big = np.zeros((32, 2, 4, 2, 2 * LANES))
    for field in range(2):
        big[:, field, :, field, :] = rows
    return big.reshape(2 * LANES, 4 * LANES)


def pair_inverse_a(ia):
    rows = ia.reshape(32, 4, 2 * LANES)
    big = np.zeros((32, 2, 4, 2, 2 * LANES))
    for field in range(2):
        big[:, field, :, field, :] = rows
    return big.reshape(2 * LANES, 4 * LANES)


def twice_a(fa):
    return np.repeat(fa.reshape(2 * LANES, 32, 1, 4), 2, axis=2).reshape(2 * LANES, 2 * LANES)


X_FA_TWICE = twice_a(TAB_X["fa"])
Y_IB_PAIR = pair_inverse_b(TAB_Y["ib"])
X_IA_PAIR = pair_inverse_a(TAB_X["ia"])


def f32(array):
    return jnp.asarray(np.asarray(array, np.float32))


def halves_of(table):
    high = table.astype(ml_dtypes.bfloat16)
    return high, (table - high.astype(np.float64)).astype(ml_dtypes.bfloat16)


def left_table(table):
    high, low = halves_of(table)
    return jnp.asarray(np.concatenate([high, high, low], axis=1))


def right_table(table):
    high, low = halves_of(table)
    return jnp.asarray(np.concatenate([high, low, high], axis=0))


def halves(values):
    high = values.astype(jnp.bfloat16)
    return high, (values - high.astype(jnp.float32)).astype(jnp.bfloat16)


def from_left(table, values):
    high, low = halves(values)
    stacked = jnp.concatenate([high, low, high], axis=0)
    return jnp.dot(table, stacked, preferred_element_type=jnp.float32)


def from_right(values, table):
    high, low = halves(values)
    joined = jnp.concatenate([high, high, low], axis=1)
    return jnp.dot(joined, table, preferred_element_type=jnp.float32)


INDEX_X = np.arange(LANES)[:, None] // 4 + 32 * np.arange(LANES)[None, :]
WAVE_X = np.float32(2.0 * math.pi / NXW) * np.minimum(INDEX_X, NXW - INDEX_X).astype(np.float32)
TURNS_X = np.concatenate([TAB_X["cos_t"], TAB_X["sin_t"], WAVE_X, np.zeros((8, LANES))])


def twiddle(real, imag, cos_t, sin_t):
    return real * cos_t + imag * sin_t, imag * cos_t - real * sin_t


def forward(block, fa, cos_t, sin_t, fb):
    outer = from_left(fa, block)
    real, imag = twiddle(outer[:LANES], outer[LANES:], cos_t, sin_t)
    return from_right(jnp.concatenate([real, imag], axis=1), fb)


def run(body, outs, *args, room=8, scratch=()):
    shapes = [jax.ShapeDtypeStruct(shape, jnp.float32) for shape in outs]

    def kernel(*refs):
        inputs, rest = refs[: len(args)], refs[len(args) :]
        results = body(*inputs, *rest[len(outs) :])
        for ref, result in zip(rest[: len(outs)], results, strict=True):
            for index, piece in result if isinstance(result, list) else [(..., result)]:
                ref[index] = piece.reshape(ref.shape) if index is ... else piece

    params = pltpu.CompilerParams(vmem_limit_bytes=room << 20) if room else None
    call = pl.pallas_call(
        kernel,
        out_shape=shapes,
        scratch_shapes=[pltpu.VMEM(shape, jnp.float32) for shape in scratch],
        compiler_params=params,
    )
    return call(*args)


def loaded(body):
    return lambda *refs: body(*[ref[...] for ref in refs])


def turn_inputs(eta, potential):
    eta_t = eta.T.reshape(16, 8, LANES)
    potential_t = potential.T.reshape(16, 8, LANES)
    return (jnp.concatenate([eta_t, potential_t], axis=1),)


def turn(block):
    return (block.reshape(-1, LANES).T,)


def turn_twice(block):
    turned = block[...].reshape(LANES, LANES).T
    tiles = [turned[8 * tile : 8 * tile + 8] for tile in range(16)]
    return ([(peer, tiles[peer // 2]) for peer in range(32)],)


def turn_fields(block):
    return (block[:, 0:8].reshape(-1, LANES).T,)


def first_y(both, fa, turns, fb):
    eta = both[:, :8].reshape(LANES, LANES)
    potential = both[:, 8:].reshape(LANES, LANES)
    return forward(potential, fa, turns[:LANES], turns[LANES:], fb), eta


def magnitude(place, wave_x):
    line = lax.broadcasted_iota(jnp.int32, (LANES, LANES), 0) & 3
    wave_y = wavenumber(place[1:2, :] + 64 * place[0:1, :] + 16 * line, NYW)
    return jnp.sqrt(wave_x * wave_x + wave_y * wave_y)


def x_stage(powers, extra=None):
    def multiply(spec, kappa, power):
        factor = kappa
        for _ in range(power - 1):
            factor = factor * kappa
        return spec * (factor * (1.0 / (NXW * NYW)))

    def body(block, turns, fa, fb, ib, ia_pair, *more):
        cos_t, sin_t, kappa = [turns[i * LANES : (i + 1) * LANES] for i in range(3)]
        older, inputs = (more[:-2], more[-2:]) if extra else (more, ())
        lines = (block * turns[3 * LANES :]).reshape(2 * LANES, LANES)
        spec = forward(lines, fa, cos_t, sin_t, fb)
        other = older[0] if older else spec
        pair = jnp.concatenate(
            [multiply(spec, kappa, powers[0]), multiply(other, kappa, powers[1])], axis=0
        )
        inner = from_right(pair, ib)
        parts = []
        for field in range(2):
            rows = inner[field * LANES : (field + 1) * LANES]
            parts += twiddle(rows[:, :LANES], rows[:, LANES:], cos_t, sin_t)
        back = from_left(ia_pair, jnp.concatenate(parts, axis=0))
        if not extra:
            return (back,)
        every = slice(None)
        pieces = [((every, slice(0, 8)), back.reshape(32, 8, LANES))]
        pieces += [((peer, slice(8, 16)), tile) for peer, tile in extra(*inputs)]
        return pieces, spec

    return body


def halo_tiles(velocity, flat):
    edges = roll(flat, CY, 1)[:, :LANES]
    side = lax.shift_right_logical(lax.broadcasted_iota(jnp.int32, edges.shape, 1), 4)
    for start, first in ((0, CX - 2), (1, 0)):
        for tile in range(12):
            c, layer, half = tile // 4, tile // 2 % 2, tile % 2
            yield 16 * start + tile, velocity[c, first + layer, 8 * half : 8 * half + 8]
        yield 16 * start + 12, jnp.where(side == start, edges, 0.0)
        for tile in range(13, 16):
            yield 16 * start + tile, jnp.zeros((8, LANES), jnp.float32)


def forward_tiles(relay, place):
    nothing = jnp.zeros((8, LANES), jnp.float32)
    for slab in range(32):
        below = relay[slab - 1, 8:16] if slab > 0 else nothing
        above = relay[slab + 1, 8:16] if slab < 31 else nothing
        yield slab, jnp.where(place[0:1, :] < 16, below, above)


def back_y(block, cos_t, sin_t, ib_pair, ia):
    inner = from_right(block.reshape(LANES, 2 * LANES), ib_pair)
    reals, imags = [], []
    for field in range(2):
        part = inner[:, 2 * field * LANES : 2 * (field + 1) * LANES]
        real, imag = twiddle(part[:, :LANES], part[:, LANES:], cos_t, sin_t)
        reals.append(real)
        imags.append(imag)
    stacked = jnp.concatenate(
        [jnp.concatenate(reals, axis=1), jnp.concatenate(imags, axis=1)], axis=0
    )
    fields = from_left(ia, stacked)
    return fields[:, :LANES], fields[:, LANES:]


def second_y(block, eta, fa, turns, fb, ib_pair, ia):
    cos_t, sin_t = turns[:LANES], turns[LANES:]
    slope_one, cubic_one = back_y(block, cos_t, sin_t, ib_pair, ia)
    spectrum = forward(-eta * slope_one, fa, cos_t, sin_t, fb)
    return spectrum, slope_one, cubic_one


def third_y(block, eta, fa, turns, fb, ib_pair, ia):
    cos_t, sin_t = turns[:LANES], turns[LANES:]
    slope_two, curve_one = back_y(block, cos_t, sin_t, ib_pair, ia)
    potential_three = -eta * slope_two - 0.5 * eta * eta * curve_one
    return forward(potential_three, fa, cos_t, sin_t, fb), slope_two, curve_one


def last_y(block, eta, slope_one, cubic_one, slope_two, curve_one, turns, ib_pair, ia):
    cos_t, sin_t = turns[:LANES], turns[LANES:]
    slope_three, curve_two = back_y(block, cos_t, sin_t, ib_pair, ia)
    vertical = (
        slope_one
        + slope_two
        + eta * curve_one
        + slope_three
        + eta * curve_two
        + 0.5 * eta * eta * cubic_one
    )
    return (vertical,)


def swap(values, axis):
    return lax.all_to_all(values, axis, 0, 0, tiled=True)


def beside(values, axis, work, *inputs):
    values, inputs = lax.optimization_barrier((values, inputs))
    moved = swap(values, axis)
    return lax.optimization_barrier((moved, work(*inputs)))


def wave_surface(surface_eta, surface_potential, velocity, place, work, inputs):
    square = (LANES, LANES)
    turns_y = [f32(np.concatenate([TAB_Y["cos_t"], TAB_Y["sin_t"]]))]
    fwd_y = [left_table(TAB_Y["fa"]), *turns_y, right_table(TAB_Y["fb"])]
    inv_y = [right_table(Y_IB_PAIR), left_table(TAB_Y["ia"])]

    pair, wide = (32, 8, LANES), (32, 16, LANES)

    def to_slab(block):
        return run(turn_twice, [pair], swap(block.reshape(16, 8, LANES), "pencil"))[0]

    def to_pencil(block):
        (turned,) = run(turn_fields, [(LANES, 2 * LANES)], block)
        return swap(turned.reshape(16, 8, 2 * LANES), "pencil")

    (turned,) = run(
        loaded(turn_inputs), [(16, 16, LANES)], surface_eta, surface_potential, room=None
    )
    both, (turns_x, *given) = beside(turned, "pencil", work, *inputs)
    spectrum, eta = run(loaded(first_y), [square, square], both, *fwd_y)
    tab_x = [
        turns_x,
        left_table(X_FA_TWICE),
        right_table(TAB_X["fb"]),
        right_table(TAB_X["ib"]),
        left_table(X_IA_PAIR),
    ]
    block = swap(to_slab(spectrum), "slab")
    stage = x_stage((1, 3), halo_tiles)
    block, spec_one = run(
        loaded(stage), [wide, square], block, *tab_x, velocity, given[0]
    )
    relay = swap(block, "slab")
    spectrum, slope_one, cubic_one = run(
        loaded(second_y), [square] * 3, to_pencil(relay), eta, *fwd_y, *inv_y
    )
    block = swap(to_slab(spectrum), "slab")
    stage = x_stage((1, 2), forward_tiles)
    block, spec_two = run(loaded(stage), [wide, square], block, *tab_x, spec_one, relay, place)
    halo = swap(block, "slab")
    spectrum, slope_two, curve_one = run(
        loaded(third_y), [square] * 3, to_pencil(halo), eta, *fwd_y, *inv_y
    )
    block = swap(to_slab(spectrum), "slab")
    (block,) = run(loaded(x_stage((1, 2))), [pair], block, *tab_x, spec_two)
    (vertical,) = run(
        loaded(last_y),
        [(16, 8, LANES)],
        to_pencil(swap(block, "slab")),
        eta,
        slope_one,
        cubic_one,
        slope_two,
        curve_one,
        *turns_y,
        *inv_y,
    )
    return swap(vertical, "pencil").reshape(square), halo, given


def wavenumber(index, length):
    folded = jnp.minimum(index, length - index)
    return 2.0 * math.pi / length * folded.astype(jnp.float32)


def ramp_weight(distance, reach_len):
    ratio = jnp.clip(1.0 - distance / reach_len, 0.0, 1.0)
    return ratio * ratio


def relax_of(cell_x, cell_y):
    pos_x, pos_y = cell_x.astype(jnp.float32), cell_y.astype(jnp.float32)
    reach_x = float(ZONE * CX)
    reach_y = float(CY)
    along_x = jnp.maximum(ramp_weight(pos_x, reach_x), ramp_weight(NX - 1.0 - pos_x, reach_x))
    across = jnp.maximum(ramp_weight(pos_y, reach_y), ramp_weight(NY - 1.0 - pos_y, reach_y))
    in_x = jnp.where((cell_x >= 0) & (cell_x < NX), 1.0, 0.0)
    in_y = jnp.where((cell_y >= 0) & (cell_y < NY), 1.0, 0.0)
    return jnp.maximum(along_x, across), in_x * in_y


def thirds(values):
    terms = []
    for _ in range(3):
        term = values.astype(jnp.bfloat16)
        terms.append(term)
        values = values - term.astype(jnp.float32)
    return jnp.concatenate(terms, axis=1)


def chosen(terms, lanes):
    count, parts = lanes.shape[1], terms.shape[1] // LANES
    iota = lax.broadcasted_iota(jnp.int32, (LANES, count), 0)
    hot = jnp.where(iota == lanes, 1.0, 0.0).astype(jnp.bfloat16)
    picked = jnp.dot(
        terms, jnp.concatenate([hot] * parts, axis=0), preferred_element_type=jnp.float32
    )
    return picked, lax.broadcasted_iota(jnp.int32, picked.shape, 0)


def listed(columns, points, row_count):
    terms = thirds(columns)
    rows = []
    for i in range(row_count):
        point = points[i : i + 1, :]
        picked, iota = chosen(terms, lax.shift_right_arithmetic(point, 7))
        found = jnp.where(iota == (point & (LANES - 1)), picked, 0.0)
        rows.append(jnp.sum(found, axis=0, keepdims=True))
    return rows


POINT_ROWS = 11


def pick_elevation(eta, points, place, turns):
    rows = listed(eta[...].T, points, POINT_ROWS)
    pieces = [(slice(i, i + 1), row) for i, row in enumerate(rows)]
    first = slice(0, 2 * LANES)
    kappa = magnitude(place, turns[2 * LANES : 3 * LANES])
    half = lax.shift_right_logical(lax.broadcasted_iota(jnp.int32, (8, LANES), 0), 2)
    mine = jnp.where(half == (place[0:1, :] & 1), 1.0, 0.0)
    second, third = slice(2 * LANES, 3 * LANES), slice(3 * LANES, 3 * LANES + 8)
    return pieces, [(first, turns[first]), (second, kappa), (third, mine)]


def pick_vertical(columns, points, eta_rows):
    columns = columns[...]
    rows = listed(columns, points, POINT_ROWS)
    pieces = [((slice(None), slice(None)), jnp.zeros((3 * LANES, LANES), jnp.float32))]

    def put(slab, place, row, half):
        at = slice(half * LANES, (half + 1) * LANES)
        for field, value in enumerate((eta_rows[row : row + 1, at], rows[row][:, at])):
            for block in range(3):
                line = 12 * (slab + 1 - block) + 4 * block + 2 * place + field
                if 0 <= line < 3 * LANES:
                    pieces.append(((slice(line, line + 1), slice(None)), value))

    for row, slab in enumerate((0, 1, 30, 31)):
        for half in range(2):
            put(slab, half, row, half)
    for slab in range(2, 30):
        put(slab, 0, 4 + (slab - 2) // 4, (slab - 2) % 4 // 2)
    return pieces, columns.T


def slots_of(stencil, slab, block):
    source, slot = lax.shift_right_logical(stencil, 8), stencil & 255
    in_zone = jnp.where((slab < ZONE) | (slab >= 32 - ZONE), 1, 0)
    lines = 12 * source + 4 * block + 2 * in_zone * lax.shift_right_logical(slot, 7)
    lanes = in_zone * (slot & 127) + (1 - in_zone) * ((slot & 63) + 64 * (slab & 1))
    return lines, lanes


def both_fields(terms, lines, lanes, shares):
    picked, iota = chosen(terms, lanes)
    picked = picked * shares
    return [jnp.where(iota == lines + field, picked, 0.0) for field in range(2)]


def summed(values):
    return jnp.sum(values, axis=0, keepdims=True)


def over_q(values):
    values = values + roll(values, 64, 1)
    return values + roll(values, 32, 1)


def sample(arrived, place, flat, halo, velocity):
    slab = jnp.concatenate([place[0:1, :]] * 2, axis=1)
    terms = thirds(arrived[...])[:, : 2 * LANES]
    flat = flat[...]
    lines, lanes = slots_of(flat[0:4].astype(jnp.int32), slab, 1)
    weights = flat[4:8]
    shares = weights / jnp.sum(weights, axis=0, keepdims=True)
    totals = [0.0, 0.0]
    for q in range(4):
        at = slice(q, q + 1)
        found = both_fields(terms, lines[at], lanes[at], shares[at])
        totals = [total + part for total, part in zip(totals, found, strict=True)]
    rows = [summed(total) for total in totals]

    lane = lax.broadcasted_iota(jnp.int32, (8, LANES), 1)
    side = lax.shift_right_logical(lane, 4) & 1
    beside_x = halo[12, 8:16] + halo[28, 8:16]
    points, weight = in_lanes(beside_x, lane, 0), in_lanes(beside_x, lane, 4)
    lines, lanes = slots_of(points.astype(jnp.int32), place[0:1, :] - 1 + 2 * side, 2 * side)
    total = over_q(weight)
    shares = weight / jnp.where(total > 0.0, total, 1.0)
    for part in both_fields(terms, lines[0:1], lanes[0:1], shares[0:1]):
        value = over_q(jnp.broadcast_to(summed(part), (8, LANES)))[0:1]
        rows.append(jnp.concatenate([value, value], axis=1))

    sent = []
    for y_at in (CY - 2, 0):
        pieces = []
        for c in range(3):
            line = 20 * c
            for x in range(2):
                tile = 4 * c + 2 * x + y_at // 8
                at = slice(8 + y_at % 8, 10 + y_at % 8)
                pieces.append((line + x, halo[tile, at]))
                pieces.append((line + 18 + x, halo[16 + tile, at]))
            pieces.append((slice(line + 2, line + 18), velocity[c, :, y_at : y_at + 2]))
        for field in range(2):
            for half in range(2):
                at = (60 + field, slice(half, half + 1))
                pieces.append((at, rows[field][:, half * LANES : (half + 1) * LANES]))
        sent.append(pieces)
    here = jnp.concatenate(rows + [jnp.zeros((4, 256), jnp.float32)], axis=0)
    return here, *sent


def in_lanes(values, lane, first):
    result = jnp.zeros(values.shape, jnp.float32)
    for q in range(4):
        moved = jnp.broadcast_to(values[first + q : first + q + 1], values.shape)
        if q:
            moved = roll(moved, 32 * q, 1)
        result = jnp.where(lax.shift_right_logical(lane, 5) == q, moved, result)
    return result


def roll(values, shift, axis):
    return pltpu.roll(values, shift, axis)


def predicted_of(centers, neighbours):
    lane = lax.broadcasted_iota(jnp.int32, centers[0].shape, centers[0].ndim - 1)
    last = centers[0].ndim - 1
    results = []
    for center, (plus_x, minus_x, plus_y, minus_y) in zip(centers, neighbours, strict=True):
        plus_z = jnp.where(lane == CZ - 1, 0.0, roll(center, CZ - 1, last))
        minus_z = jnp.where(lane == 0, 0.0, roll(center, 1, last))
        laplace = plus_x + minus_x + (plus_y + minus_y) + (plus_z + minus_z) - 6.0 * center
        advect = (
            centers[0] * (plus_x - minus_x)
            + centers[1] * (plus_y - minus_y)
            + centers[2] * (plus_z - minus_z)
        )
        results.append(center + TIME_STEP * (VISCOSITY * laplace - 0.5 * advect))
    return results


def surface_columns(here, from_low, from_high):
    def lines_of(sent):
        lines = [
            jnp.concatenate([sent[60 + field, half : half + 1] for half in range(2)], axis=1)
            for field in range(2)
        ]
        return jnp.concatenate(lines + [jnp.zeros((6, 256), jnp.float32)], axis=0)

    lane = lax.broadcasted_iota(jnp.int32, (8, 256), 1)
    below, above = roll(lines_of(from_low), 241, 1), roll(lines_of(from_high), 15, 1)
    across_y = jnp.where(lane % CY == 0, below, above)
    surface = jnp.concatenate([here[...], across_y], axis=0).T
    return lambda index: surface[:, index : index + 1].reshape(CX, CY, 1)


def both_substeps(velocity, halo, from_low, from_high, here, place, decay, padded):
    for c in range(3):
        padded[c, 2:18, 8:24] = velocity[c]
        for tile in range(4):
            layer, half = tile // 2, tile % 2
            at = slice(8 + 8 * half, 16 + 8 * half)
            padded[c, layer, at] = halo[4 * c + tile, 8:16]
            padded[c, 18 + layer, at] = halo[16 + 4 * c + tile, 8:16]
        padded[c, :, 6:8] = from_low[20 * c : 20 * c + 20]
        padded[c, :, 24:26] = from_high[20 * c : 20 * c + 20]
    column = surface_columns(here, from_low, from_high)
    (keep, keep_x, keep_y), (pull, pull_x, pull_y) = relax_fields(place, decay[...])

    def region(x_at, x_to, y_at, y_to):
        def part(c, shift_x, shift_y):
            return padded[c, x_at + shift_x : x_to + shift_x, y_at + shift_y : y_to + shift_y]

        steps = ((1, 0), (-1, 0), (0, 1), (0, -1))
        centers = [part(c, 0, 0) for c in range(3)]
        return predicted_of(centers, [[part(c, *step) for step in steps] for c in range(3)])

    own = region(2, 18, 8, 24)
    sides_x = [region(1, 2, 8, 24), region(18, 19, 8, 24)]
    sides_y = [region(2, 18, 7, 8), region(2, 18, 24, 25)]

    shape = (CX, CY, CZ)
    row = lax.broadcasted_iota(jnp.int32, shape, 1)
    centers, neighbours, targets = [], [], []
    for c in range(3):
        center = own[c] * keep
        outer_x = [sides_x[side][c] * keep_x[side : side + 1] for side in range(2)]
        low, high = [jnp.broadcast_to(side[c], shape) for side in sides_y]
        outer_y = jnp.where(row == 0, low, high) * keep_y
        target = None
        if c != 1:
            field = c // 2
            target = pull * column(field)
            center = center + target
            line = column(2 + field)
            outer_x = [
                outer_x[0] + pull_x[0:1] * line[0:1],
                outer_x[1] + pull_x[1:2] * line[CX - 1 : CX],
            ]
            outer_y = outer_y + pull_y * column(8 + field)
        plus_x = jnp.concatenate([center[1:], outer_x[1]], axis=0)
        minus_x = jnp.concatenate([outer_x[0], center[:-1]], axis=0)
        plus_y = jnp.where(row == CY - 1, outer_y, roll(center, CY - 1, 1))
        minus_y = jnp.where(row == 0, outer_y, roll(center, 1, 1))
        centers.append(center)
        neighbours.append((plus_x, minus_x, plus_y, minus_y))
        targets.append(target)
    pieces = []
    for c, value in enumerate(predicted_of(centers, neighbours)):
        value = value * keep
        pieces.append((c, value if targets[c] is None else value + targets[c]))
    return (pieces,)


def shifted(values, axis, step):
    size = lax.axis_size(axis)
    pairs = [(i, i + step) for i in range(size) if 0 <= i + step < size]
    return lax.ppermute(values, axis, pairs)


def list_points(send_point, send_count):
    slot = lax.broadcasted_iota(jnp.int32, (32, 256), 1)
    points = jnp.where(slot < send_count[0, 0][:, None], send_point[0, 0], -1)
    inner = points[2:30, :64].reshape(7, 256)
    return jnp.concatenate([points[:2], points[30:], inner], axis=0)


DECAY = np.exp(-DEPTH_RATE * (CZ - 1.0 - np.arange(CZ)) / CZ).astype(np.float32)


def relax_fields(place, decay):
    def fields(cell_x, cell_y):
        relax, inside = relax_of(cell_x, cell_y)
        return (1.0 - relax) * inside, relax * inside * decay.reshape(1, 1, CZ)

    side = lax.broadcasted_iota(jnp.int32, (2, 1, CZ), 0)
    row = lax.broadcasted_iota(jnp.int32, (1, CY, CZ), 1)
    slab, pencil = place[0:1, :].reshape(1, 1, CZ), place[1:2, :].reshape(1, 1, CZ)
    cell_x = slab * CX + lax.broadcasted_iota(jnp.int32, (CX, 1, CZ), 0)
    cell_y = pencil * CY + row
    out_x = slab * CX - 1 + (CX + 1) * side
    out_y = cell_y + jnp.where(row == 0, -1, jnp.where(row == CY - 1, 1, 0))
    own, across_x, across_y = fields(cell_x, cell_y), fields(out_x, cell_y), fields(cell_x, out_y)
    return (own[0], across_x[0], across_y[0]), (own[1], across_x[1], across_y[1])


def flat_stencil(stencil, interp_weight):
    rows = [stencil.astype(jnp.float32), interp_weight]
    return jnp.concatenate(rows, axis=0).reshape(8, CX * CY)


def on_device(
    surface_eta, surface_potential, velocity, send_point, send_count, stencil, interp_weight
):
    line = lax.broadcasted_iota(jnp.int32, (8, LANES), 0)
    place = jnp.where(line == 0, lax.axis_index("slab"), lax.axis_index("pencil"))
    surface_eta, place = lax.optimization_barrier((surface_eta, place))
    square = (LANES, LANES)

    def lists(eta, place, send_point, send_count, stencil, interp_weight):
        points = list_points(send_point, send_count)
        shapes = [(POINT_ROWS, 256), TURNS_X.shape]
        rows, turns_x = run(pick_elevation, shapes, eta, points, place, f32(TURNS_X))
        return turns_x, flat_stencil(stencil, interp_weight), points, rows

    columns, halo, (flat, points, eta_rows) = wave_surface(
        surface_eta,
        surface_potential,
        velocity,
        place,
        lists,
        (surface_eta, place, send_point, send_count, stencil, interp_weight),
    )
    outgoing, vertical = run(
        pick_vertical, [(3 * LANES, LANES), square], columns, points, eta_rows
    )
    arrived = swap(outgoing.reshape(32, 3, 4, LANES), "slab").reshape(3 * LANES, LANES)
    sent = (62, 2, LANES)
    here, upward, downward = run(
        sample, [(8, 256), sent, sent], arrived, place, flat, halo, velocity
    )
    from_low, from_high = shifted(upward, "pencil", 1), shifted(downward, "pencil", -1)
    (velocity,) = run(
        both_substeps,
        [(3, CX, CY, CZ)],
        velocity,
        halo,
        from_low,
        from_high,
        here,
        place,
        jnp.asarray(DECAY[None]),
        scratch=[(3, 20, 32, CZ)],
    )
    return (vertical, velocity)


def solution(mesh):
    in_specs = (
        P("pencil", "slab"),
        P("pencil", "slab"),
        P(None, "slab", "pencil", None),
        P("slab", "pencil", None, None),
        P("slab", "pencil", None),
        P(None, "slab", "pencil"),
        P(None, "slab", "pencil"),
    )
    out_specs = (P("pencil", "slab"), P(None, "slab", "pencil", None))
    return jax.shard_map(
        on_device, mesh=mesh, in_specs=in_specs, out_specs=out_specs, check_vma=False
    )
```

```python
import math

import jax
import jax.numpy as jnp
import ml_dtypes
import numpy as np
from jax import lax
from jax.experimental import pallas as pl
from jax.experimental.pallas import tpu as pltpu
from jax.sharding import PartitionSpec as P

NXW = 4096
NYW = 2048
LANES = 128
CX = 16
CY = 16
CZ = 128
NX = 512
NY = 256
ZONE = 2

TIME_STEP = 0.2
VISCOSITY = 0.6
DEPTH_RATE = 3.0


def stage_tables(peers):
    copies = LANES // peers
    length = peers * LANES
    outer = np.arange(peers)
    inner = np.arange(LANES)
    eye = np.eye(copies)
    angle_a = 2.0 * np.pi / peers * (outer[:, None] * outer[None, :] % peers)
    angle_t = 2.0 * np.pi / length * (outer[:, None] * inner[None, :] % length)
    angle_b = 2.0 * np.pi / LANES * (inner[:, None] * inner[None, :] % LANES)
    cos_a, sin_a = np.kron(np.cos(angle_a), eye), np.kron(np.sin(angle_a), eye)
    cos_b, sin_b = np.cos(angle_b), np.sin(angle_b)
    tables = {
        "fa": np.concatenate([cos_a, -sin_a], axis=0),
        "cos_t": np.repeat(np.cos(angle_t), copies, axis=0),
        "sin_t": np.repeat(np.sin(angle_t), copies, axis=0),
        "fb": np.concatenate([cos_b + sin_b, sin_b - cos_b], axis=0),
        "ib": np.concatenate([cos_b, -sin_b], axis=1),
        "ia": np.concatenate([cos_a + sin_a, sin_a - cos_a], axis=1),
    }
    return tables


TAB_Y = stage_tables(16)
TAB_X = stage_tables(32)


def pair_inverse_b(ib):
    rows = ib.reshape(32, 4, 2 * LANES)
    big = np.zeros((32, 2, 4, 2, 2 * LANES))
    for field in range(2):
        big[:, field, :, field, :] = rows
    return big.reshape(2 * LANES, 4 * LANES)


def pair_inverse_a(ia):
    rows = ia.reshape(32, 4, 2 * LANES)
    big = np.zeros((32, 2, 4, 2, 2 * LANES))
    for field in range(2):
        big[:, field, :, field, :] = rows
    return big.reshape(2 * LANES, 4 * LANES)


Y_IB_PAIR = pair_inverse_b(TAB_Y["ib"])
X_IA_PAIR = pair_inverse_a(TAB_X["ia"])


def f32(array):
    return jnp.asarray(np.asarray(array, np.float32))


def halves_of(table):
    high = table.astype(ml_dtypes.bfloat16)
    return high, (table - high.astype(np.float64)).astype(ml_dtypes.bfloat16)


def left_table(table):
    high, low = halves_of(table)
    return jnp.asarray(np.concatenate([high, high, low], axis=1))


def right_table(table):
    high, low = halves_of(table)
    return jnp.asarray(np.concatenate([high, low, high], axis=0))


def halves(values):
    high = values.astype(jnp.bfloat16)
    return high, (values - high.astype(jnp.float32)).astype(jnp.bfloat16)


def from_left(table, values):
    high, low = halves(values)
    stacked = jnp.concatenate([high, low, high], axis=0)
    return jnp.dot(table, stacked, preferred_element_type=jnp.float32)


def from_right(values, table):
    high, low = halves(values)
    joined = jnp.concatenate([high, high, low], axis=1)
    return jnp.dot(joined, table, preferred_element_type=jnp.float32)


INDEX_X = np.arange(LANES)[:, None] // 4 + 32 * np.arange(LANES)[None, :]
WAVE_X = np.float32(2.0 * math.pi / NXW) * np.minimum(INDEX_X, NXW - INDEX_X).astype(np.float32)
TURNS_X = np.concatenate([TAB_X["cos_t"], TAB_X["sin_t"], WAVE_X])


def twiddle(real, imag, cos_t, sin_t):
    return real * cos_t + imag * sin_t, imag * cos_t - real * sin_t


def forward(block, fa, cos_t, sin_t, fb):
    outer = from_left(fa, block)
    real, imag = twiddle(outer[:LANES], outer[LANES:], cos_t, sin_t)
    return from_right(jnp.concatenate([real, imag], axis=1), fb)


def run(body, outs, *args, room=8, scratch=()):
    shapes = [jax.ShapeDtypeStruct(shape, jnp.float32) for shape in outs]

    def kernel(*refs):
        inputs, rest = refs[: len(args)], refs[len(args) :]
        results = body(*inputs, *rest[len(outs) :])
        for ref, result in zip(rest[: len(outs)], results, strict=True):
            for index, piece in result if isinstance(result, list) else [(..., result)]:
                ref[index] = piece.reshape(ref.shape) if index is ... else piece

    params = pltpu.CompilerParams(vmem_limit_bytes=room << 20) if room else None
    call = pl.pallas_call(
        kernel,
        out_shape=shapes,
        scratch_shapes=[pltpu.VMEM(shape, jnp.float32) for shape in scratch],
        compiler_params=params,
    )
    return call(*args)


def loaded(body):
    return lambda *refs: body(*[ref[...] for ref in refs])


def turn_inputs(eta, potential):
    eta_t = eta.T.reshape(16, 8, LANES)
    potential_t = potential.T.reshape(16, 8, LANES)
    return (jnp.concatenate([eta_t, potential_t], axis=1),)


def turn(block):
    return (block.reshape(-1, LANES).T,)


def turn_fields(block):
    return (block[:, 0:8].reshape(-1, LANES).T,)


def first_y(both, fa, turns, fb):
    eta = both[:, :8].reshape(LANES, LANES)
    potential = both[:, 8:].reshape(LANES, LANES)
    return forward(potential, fa, turns[:LANES], turns[LANES:], fb), eta


def magnitude(place, wave_x):
    line = lax.broadcasted_iota(jnp.int32, (LANES, LANES), 0) & 3
    wave_y = wavenumber(place[1:2, :] + 64 * place[0:1, :] + 16 * line, NYW)
    return jnp.sqrt(wave_x * wave_x + wave_y * wave_y)


def x_stage(powers, extra=None):
    def multiply(spec, kappa, power):
        factor = kappa
        for _ in range(power - 1):
            factor = factor * kappa
        return spec * (factor * (1.0 / (NXW * NYW)))

    def body(block, turns, fa, fb, ib, ia_pair, *more):
        cos_t, sin_t, kappa = [turns[i * LANES : (i + 1) * LANES] for i in range(3)]
        older, inputs = (more[:-2], more[-2:]) if extra else (more, ())
        spec = forward(block.reshape(LANES, LANES), fa, cos_t, sin_t, fb)
        other = older[0] if older else spec
        pair = jnp.concatenate(
            [multiply(spec, kappa, powers[0]), multiply(other, kappa, powers[1])], axis=0
        )
        inner = from_right(pair, ib)
        parts = []
        for field in range(2):
            rows = inner[field * LANES : (field + 1) * LANES]
            parts += twiddle(rows[:, :LANES], rows[:, LANES:], cos_t, sin_t)
        back = from_left(ia_pair, jnp.concatenate(parts, axis=0))
        if not extra:
            return (back,)
        every = slice(None)
        pieces = [((every, slice(0, 8)), back.reshape(32, 8, LANES))]
        pieces += [((peer, slice(8, 16)), tile) for peer, tile in extra(*inputs)]
        return pieces, spec

    return body


def halo_tiles(velocity, flat):
    edges = roll(flat, CY, 1)[:, :LANES]
    side = lax.shift_right_logical(lax.broadcasted_iota(jnp.int32, edges.shape, 1), 4)
    for start, first in ((0, CX - 2), (1, 0)):
        for tile in range(12):
            c, layer, half = tile // 4, tile // 2 % 2, tile % 2
            yield 16 * start + tile, velocity[c, first + layer, 8 * half : 8 * half + 8]
        yield 16 * start + 12, jnp.where(side == start, edges, 0.0)
        for tile in range(13, 16):
            yield 16 * start + tile, jnp.zeros((8, LANES), jnp.float32)


def forward_tiles(relay, place):
    nothing = jnp.zeros((8, LANES), jnp.float32)
    for slab in range(32):
        below = relay[slab - 1, 8:16] if slab > 0 else nothing
        above = relay[slab + 1, 8:16] if slab < 31 else nothing
        yield slab, jnp.where(place[0:1, :] < 16, below, above)


def back_y(block, cos_t, sin_t, ib_pair, ia):
    inner = from_right(block.reshape(LANES, 2 * LANES), ib_pair)
    reals, imags = [], []
    for field in range(2):
        part = inner[:, 2 * field * LANES : 2 * (field + 1) * LANES]
        real, imag = twiddle(part[:, :LANES], part[:, LANES:], cos_t, sin_t)
        reals.append(real)
        imags.append(imag)
    stacked = jnp.concatenate(
        [jnp.concatenate(reals, axis=1), jnp.concatenate(imags, axis=1)], axis=0
    )
    fields = from_left(ia, stacked)
    return fields[:, :LANES], fields[:, LANES:]


def second_y(block, eta, fa, turns, fb, ib_pair, ia):
    cos_t, sin_t = turns[:LANES], turns[LANES:]
    slope_one, cubic_one = back_y(block, cos_t, sin_t, ib_pair, ia)
    spectrum = forward(-eta * slope_one, fa, cos_t, sin_t, fb)
    return spectrum, slope_one, cubic_one


def third_y(block, eta, fa, turns, fb, ib_pair, ia):
    cos_t, sin_t = turns[:LANES], turns[LANES:]
    slope_two, curve_one = back_y(block, cos_t, sin_t, ib_pair, ia)
    potential_three = -eta * slope_two - 0.5 * eta * eta * curve_one
    return forward(potential_three, fa, cos_t, sin_t, fb), slope_two, curve_one


def last_y(block, eta, slope_one, cubic_one, slope_two, curve_one, turns, ib_pair, ia):
    cos_t, sin_t = turns[:LANES], turns[LANES:]
    slope_three, curve_two = back_y(block, cos_t, sin_t, ib_pair, ia)
    vertical = (
        slope_one
        + slope_two
        + eta * curve_one
        + slope_three
        + eta * curve_two
        + 0.5 * eta * eta * cubic_one
    )
    return (vertical,)


def swap(values, axis):
    return lax.all_to_all(values, axis, 0, 0, tiled=True)


def beside(values, axis, work, *inputs):
    values, inputs = lax.optimization_barrier((values, inputs))
    moved = swap(values, axis)
    return lax.optimization_barrier((moved, work(*inputs)))


def wave_surface(surface_eta, surface_potential, velocity, place, work, inputs):
    square = (LANES, LANES)
    turns_y = [f32(np.concatenate([TAB_Y["cos_t"], TAB_Y["sin_t"]]))]
    fwd_y = [left_table(TAB_Y["fa"]), *turns_y, right_table(TAB_Y["fb"])]
    inv_y = [right_table(Y_IB_PAIR), left_table(TAB_Y["ia"])]

    def to_slab(block):
        (turned,) = run(loaded(turn), [square], swap(block.reshape(16, 8, LANES), "pencil"))
        return turned.reshape(32, 4, LANES)

    def to_pencil(block):
        (turned,) = run(turn_fields, [(LANES, 2 * LANES)], block)
        return swap(turned.reshape(16, 8, 2 * LANES), "pencil")

    pair, wide = (32, 8, LANES), (32, 16, LANES)
    (turned,) = run(
        loaded(turn_inputs), [(16, 16, LANES)], surface_eta, surface_potential, room=None
    )
    both, (turns_x, *given) = beside(turned, "pencil", work, *inputs)
    spectrum, eta = run(loaded(first_y), [square, square], both, *fwd_y)
    tab_x = [
        turns_x,
        left_table(TAB_X["fa"]),
        right_table(TAB_X["fb"]),
        right_table(TAB_X["ib"]),
        left_table(X_IA_PAIR),
    ]
    block = swap(to_slab(spectrum), "slab")
    stage = x_stage((1, 3), halo_tiles)
    block, spec_one = run(
        loaded(stage), [wide, square], block.reshape(square), *tab_x, velocity, given[0]
    )
    relay = swap(block, "slab")
    spectrum, slope_one, cubic_one = run(
        loaded(second_y), [square] * 3, to_pencil(relay), eta, *fwd_y, *inv_y
    )
    block = swap(to_slab(spectrum), "slab").reshape(square)
    stage = x_stage((1, 2), forward_tiles)
    block, spec_two = run(loaded(stage), [wide, square], block, *tab_x, spec_one, relay, place)
    halo = swap(block, "slab")
    spectrum, slope_two, curve_one = run(
        loaded(third_y), [square] * 3, to_pencil(halo), eta, *fwd_y, *inv_y
    )
    block = swap(to_slab(spectrum), "slab").reshape(square)
    (block,) = run(loaded(x_stage((1, 2))), [pair], block, *tab_x, spec_two)
    (vertical,) = run(
        loaded(last_y),
        [(16, 8, LANES)],
        to_pencil(swap(block, "slab")),
        eta,
        slope_one,
        cubic_one,
        slope_two,
        curve_one,
        *turns_y,
        *inv_y,
    )
    return swap(vertical, "pencil").reshape(square), halo, given


def wavenumber(index, length):
    folded = jnp.minimum(index, length - index)
    return 2.0 * math.pi / length * folded.astype(jnp.float32)


def ramp_weight(distance, reach_len):
    ratio = jnp.clip(1.0 - distance / reach_len, 0.0, 1.0)
    return ratio * ratio


def relax_of(cell_x, cell_y):
    pos_x, pos_y = cell_x.astype(jnp.float32), cell_y.astype(jnp.float32)
    reach_x = float(ZONE * CX)
    reach_y = float(CY)
    along_x = jnp.maximum(ramp_weight(pos_x, reach_x), ramp_weight(NX - 1.0 - pos_x, reach_x))
    across = jnp.maximum(ramp_weight(pos_y, reach_y), ramp_weight(NY - 1.0 - pos_y, reach_y))
    in_x = jnp.where((cell_x >= 0) & (cell_x < NX), 1.0, 0.0)
    in_y = jnp.where((cell_y >= 0) & (cell_y < NY), 1.0, 0.0)
    return jnp.maximum(along_x, across), in_x * in_y


def thirds(values):
    terms = []
    for _ in range(3):
        term = values.astype(jnp.bfloat16)
        terms.append(term)
        values = values - term.astype(jnp.float32)
    return jnp.concatenate(terms, axis=1)


def chosen(terms, lanes):
    count, parts = lanes.shape[1], terms.shape[1] // LANES
    iota = lax.broadcasted_iota(jnp.int32, (LANES, count), 0)
    hot = jnp.where(iota == lanes, 1.0, 0.0).astype(jnp.bfloat16)
    picked = jnp.dot(
        terms, jnp.concatenate([hot] * parts, axis=0), preferred_element_type=jnp.float32
    )
    return picked, lax.broadcasted_iota(jnp.int32, picked.shape, 0)


def listed(columns, points, row_count):
    terms = thirds(columns)
    rows = []
    for i in range(row_count):
        point = points[i : i + 1, :]
        picked, iota = chosen(terms, lax.shift_right_arithmetic(point, 7))
        found = jnp.where(iota == (point & (LANES - 1)), picked, 0.0)
        rows.append(jnp.sum(found, axis=0, keepdims=True))
    return rows


POINT_ROWS = 11


def pick_elevation(eta, points, place, turns):
    rows = listed(eta[...].T, points, POINT_ROWS)
    pieces = [(slice(i, i + 1), row) for i, row in enumerate(rows)]
    first = slice(0, 2 * LANES)
    kappa = magnitude(place, turns[2 * LANES : 3 * LANES])
    return pieces, [(first, turns[first]), (slice(2 * LANES, 3 * LANES), kappa)]


def pick_vertical(columns, points, eta_rows):
    columns = columns[...]
    rows = listed(columns, points, POINT_ROWS)
    pieces = [((slice(None), slice(None)), jnp.zeros((3 * LANES, LANES), jnp.float32))]

    def put(slab, place, row, half):
        at = slice(half * LANES, (half + 1) * LANES)
        for field, value in enumerate((eta_rows[row : row + 1, at], rows[row][:, at])):
            for block in range(3):
                line = 12 * (slab + 1 - block) + 4 * block + 2 * place + field
                if 0 <= line < 3 * LANES:
                    pieces.append(((slice(line, line + 1), slice(None)), value))

    for row, slab in enumerate((0, 1, 30, 31)):
        for half in range(2):
            put(slab, half, row, half)
    for slab in range(2, 30):
        put(slab, 0, 4 + (slab - 2) // 4, (slab - 2) % 4 // 2)
    return pieces, columns.T


def slots_of(stencil, slab, block):
    source, slot = lax.shift_right_logical(stencil, 8), stencil & 255
    in_zone = jnp.where((slab < ZONE) | (slab >= 32 - ZONE), 1, 0)
    lines = 12 * source + 4 * block + 2 * in_zone * lax.shift_right_logical(slot, 7)
    lanes = in_zone * (slot & 127) + (1 - in_zone) * ((slot & 63) + 64 * (slab & 1))
    return lines, lanes


def both_fields(terms, lines, lanes, shares):
    picked, iota = chosen(terms, lanes)
    picked = picked * shares
    return [jnp.where(iota == lines + field, picked, 0.0) for field in range(2)]


def summed(values):
    return jnp.sum(values, axis=0, keepdims=True)


def over_q(values):
    values = values + roll(values, 64, 1)
    return values + roll(values, 32, 1)


def sample(arrived, place, flat, halo, velocity):
    slab = jnp.concatenate([place[0:1, :]] * 2, axis=1)
    terms = thirds(arrived[...])[:, : 2 * LANES]
    flat = flat[...]
    lines, lanes = slots_of(flat[0:4].astype(jnp.int32), slab, 1)
    weights = flat[4:8]
    shares = weights / jnp.sum(weights, axis=0, keepdims=True)
    totals = [0.0, 0.0]
    for q in range(4):
        at = slice(q, q + 1)
        found = both_fields(terms, lines[at], lanes[at], shares[at])
        totals = [total + part for total, part in zip(totals, found, strict=True)]
    rows = [summed(total) for total in totals]

    lane = lax.broadcasted_iota(jnp.int32, (8, LANES), 1)
    side = lax.shift_right_logical(lane, 4) & 1
    beside_x = halo[12, 8:16] + halo[28, 8:16]
    points, weight = in_lanes(beside_x, lane, 0), in_lanes(beside_x, lane, 4)
    lines, lanes = slots_of(points.astype(jnp.int32), place[0:1, :] - 1 + 2 * side, 2 * side)
    total = over_q(weight)
    shares = weight / jnp.where(total > 0.0, total, 1.0)
    for part in both_fields(terms, lines[0:1], lanes[0:1], shares[0:1]):
        value = over_q(jnp.broadcast_to(summed(part), (8, LANES)))[0:1]
        rows.append(jnp.concatenate([value, value], axis=1))

    sent = []
    for y_at in (CY - 2, 0):
        pieces = []
        for c in range(3):
            line = 20 * c
            for x in range(2):
                tile = 4 * c + 2 * x + y_at // 8
                at = slice(8 + y_at % 8, 10 + y_at % 8)
                pieces.append((line + x, halo[tile, at]))
                pieces.append((line + 18 + x, halo[16 + tile, at]))
            pieces.append((slice(line + 2, line + 18), velocity[c, :, y_at : y_at + 2]))
        for field in range(2):
            for half in range(2):
                at = (60 + field, slice(half, half + 1))
                pieces.append((at, rows[field][:, half * LANES : (half + 1) * LANES]))
        sent.append(pieces)
    here = jnp.concatenate(rows + [jnp.zeros((4, 256), jnp.float32)], axis=0)
    even = (place[1:2, :] & 1) == 0
    swaps = [[], []]
    for (at, up), (_, down) in zip(*sent, strict=True):
        swaps[0].append((at, jnp.where(even, up, down)))
        swaps[1].append((at, jnp.where(even, down, up)))
    return here, *swaps


def in_lanes(values, lane, first):
    result = jnp.zeros(values.shape, jnp.float32)
    for q in range(4):
        moved = jnp.broadcast_to(values[first + q : first + q + 1], values.shape)
        if q:
            moved = roll(moved, 32 * q, 1)
        result = jnp.where(lax.shift_right_logical(lane, 5) == q, moved, result)
    return result


def roll(values, shift, axis):
    return pltpu.roll(values, shift, axis)


def predicted_of(centers, neighbours):
    lane = lax.broadcasted_iota(jnp.int32, centers[0].shape, centers[0].ndim - 1)
    last = centers[0].ndim - 1
    results = []
    for center, (plus_x, minus_x, plus_y, minus_y) in zip(centers, neighbours, strict=True):
        plus_z = jnp.where(lane == CZ - 1, 0.0, roll(center, CZ - 1, last))
        minus_z = jnp.where(lane == 0, 0.0, roll(center, 1, last))
        laplace = plus_x + minus_x + (plus_y + minus_y) + (plus_z + minus_z) - 6.0 * center
        advect = (
            centers[0] * (plus_x - minus_x)
            + centers[1] * (plus_y - minus_y)
            + centers[2] * (plus_z - minus_z)
        )
        results.append(center + TIME_STEP * (VISCOSITY * laplace - 0.5 * advect))
    return results


def surface_columns(here, low, high):
    def lines_of(values):
        lines = [
            jnp.concatenate([values[field, half : half + 1] for half in range(2)], axis=1)
            for field in range(2)
        ]
        return jnp.concatenate(lines + [jnp.zeros((6, 256), jnp.float32)], axis=0)

    lane = lax.broadcasted_iota(jnp.int32, (8, 256), 1)
    below, above = roll(lines_of(low), 241, 1), roll(lines_of(high), 15, 1)
    across_y = jnp.where(lane % CY == 0, below, above)
    surface = jnp.concatenate([here[...], across_y], axis=0).T
    return lambda index: surface[:, index : index + 1].reshape(CX, CY, 1)


def both_substeps(velocity, halo, near, far, here, place, decay, padded):
    even = (place[1:2, :] & 1) == 0

    def from_low(at):
        return jnp.where(even, far[at], near[at])

    def from_high(at):
        return jnp.where(even, near[at], far[at])

    for c in range(3):
        padded[c, 2:18, 8:24] = velocity[c]
        for tile in range(4):
            layer, half = tile // 2, tile % 2
            at = slice(8 + 8 * half, 16 + 8 * half)
            padded[c, layer, at] = halo[4 * c + tile, 8:16]
            padded[c, 18 + layer, at] = halo[16 + 4 * c + tile, 8:16]
        lines = slice(20 * c, 20 * c + 20)
        padded[c, :, 6:8] = from_low(lines)
        padded[c, :, 24:26] = from_high(lines)
    lines = slice(60, 62)
    column = surface_columns(here, from_low(lines), from_high(lines))
    (keep, keep_x, keep_y), (pull, pull_x, pull_y) = relax_fields(place, decay[...])

    def region(x_at, x_to, y_at, y_to):
        def part(c, shift_x, shift_y):
            return padded[c, x_at + shift_x : x_to + shift_x, y_at + shift_y : y_to + shift_y]

        steps = ((1, 0), (-1, 0), (0, 1), (0, -1))
        centers = [part(c, 0, 0) for c in range(3)]
        return predicted_of(centers, [[part(c, *step) for step in steps] for c in range(3)])

    own = region(2, 18, 8, 24)
    sides_x = [region(1, 2, 8, 24), region(18, 19, 8, 24)]
    sides_y = [region(2, 18, 7, 8), region(2, 18, 24, 25)]

    shape = (CX, CY, CZ)
    row = lax.broadcasted_iota(jnp.int32, shape, 1)
    centers, neighbours, targets = [], [], []
    for c in range(3):
        center = own[c] * keep
        outer_x = [sides_x[side][c] * keep_x[side : side + 1] for side in range(2)]
        low, high = [jnp.broadcast_to(side[c], shape) for side in sides_y]
        outer_y = jnp.where(row == 0, low, high) * keep_y
        target = None
        if c != 1:
            field = c // 2
            target = pull * column(field)
            center = center + target
            line = column(2 + field)
            outer_x = [
                outer_x[0] + pull_x[0:1] * line[0:1],
                outer_x[1] + pull_x[1:2] * line[CX - 1 : CX],
            ]
            outer_y = outer_y + pull_y * column(8 + field)
        plus_x = jnp.concatenate([center[1:], outer_x[1]], axis=0)
        minus_x = jnp.concatenate([outer_x[0], center[:-1]], axis=0)
        plus_y = jnp.where(row == CY - 1, outer_y, roll(center, CY - 1, 1))
        minus_y = jnp.where(row == 0, outer_y, roll(center, 1, 1))
        centers.append(center)
        neighbours.append((plus_x, minus_x, plus_y, minus_y))
        targets.append(target)
    pieces = []
    for c, value in enumerate(predicted_of(centers, neighbours)):
        value = value * keep
        pieces.append((c, value if targets[c] is None else value + targets[c]))
    return (pieces,)


def swapped(values, axis, first):
    pairs = [(i, i + 1) for i in range(first, lax.axis_size(axis) - 1, 2)]
    return lax.ppermute(values, axis, pairs + [(j, i) for i, j in pairs])


def list_points(send_point, send_count):
    slot = lax.broadcasted_iota(jnp.int32, (32, 256), 1)
    points = jnp.where(slot < send_count[0, 0][:, None], send_point[0, 0], -1)
    inner = points[2:30, :64].reshape(7, 256)
    return jnp.concatenate([points[:2], points[30:], inner], axis=0)


DECAY = np.exp(-DEPTH_RATE * (CZ - 1.0 - np.arange(CZ)) / CZ).astype(np.float32)


def relax_fields(place, decay):
    def fields(cell_x, cell_y):
        relax, inside = relax_of(cell_x, cell_y)
        return (1.0 - relax) * inside, relax * inside * decay.reshape(1, 1, CZ)

    side = lax.broadcasted_iota(jnp.int32, (2, 1, CZ), 0)
    row = lax.broadcasted_iota(jnp.int32, (1, CY, CZ), 1)
    slab, pencil = place[0:1, :].reshape(1, 1, CZ), place[1:2, :].reshape(1, 1, CZ)
    cell_x = slab * CX + lax.broadcasted_iota(jnp.int32, (CX, 1, CZ), 0)
    cell_y = pencil * CY + row
    out_x = slab * CX - 1 + (CX + 1) * side
    out_y = cell_y + jnp.where(row == 0, -1, jnp.where(row == CY - 1, 1, 0))
    own, across_x, across_y = fields(cell_x, cell_y), fields(out_x, cell_y), fields(cell_x, out_y)
    return (own[0], across_x[0], across_y[0]), (own[1], across_x[1], across_y[1])


def flat_stencil(stencil, interp_weight):
    rows = [stencil.astype(jnp.float32), interp_weight]
    return jnp.concatenate(rows, axis=0).reshape(8, CX * CY)


def on_device(
    surface_eta, surface_potential, velocity, send_point, send_count, stencil, interp_weight
):
    line = lax.broadcasted_iota(jnp.int32, (8, LANES), 0)
    place = jnp.where(line == 0, lax.axis_index("slab"), lax.axis_index("pencil"))
    surface_eta, place = lax.optimization_barrier((surface_eta, place))
    square = (LANES, LANES)

    def lists(eta, place, send_point, send_count, stencil, interp_weight):
        points = list_points(send_point, send_count)
        shapes = [(POINT_ROWS, 256), TURNS_X.shape]
        rows, turns_x = run(pick_elevation, shapes, eta, points, place, f32(TURNS_X))
        return turns_x, flat_stencil(stencil, interp_weight), points, rows

    columns, halo, (flat, points, eta_rows) = wave_surface(
        surface_eta,
        surface_potential,
        velocity,
        place,
        lists,
        (surface_eta, place, send_point, send_count, stencil, interp_weight),
    )
    outgoing, vertical = run(
        pick_vertical, [(3 * LANES, LANES), square], columns, points, eta_rows
    )
    arrived = swap(outgoing.reshape(32, 3, 4, LANES), "slab").reshape(3 * LANES, LANES)
    sent = (62, 2, LANES)
    here, near, far = run(
        sample, [(8, 256), sent, sent], arrived, place, flat, halo, velocity
    )
    near, far = swapped(near, "pencil", 0), swapped(far, "pencil", 1)
    (velocity,) = run(
        both_substeps,
        [(3, CX, CY, CZ)],
        velocity,
        halo,
        near,
        far,
        here,
        place,
        jnp.asarray(DECAY[None]),
        scratch=[(3, 20, 32, CZ)],
    )
    return (vertical, velocity)


def solution(mesh):
    in_specs = (
        P("pencil", "slab"),
        P("pencil", "slab"),
        P(None, "slab", "pencil", None),
        P("slab", "pencil", None, None),
        P("slab", "pencil", None),
        P(None, "slab", "pencil"),
        P(None, "slab", "pencil"),
    )
    out_specs = (P("pencil", "slab"), P(None, "slab", "pencil", None))
    return jax.shard_map(
        on_device, mesh=mesh, in_specs=in_specs, out_specs=out_specs, check_vma=False
    )
```

```python
import math

import jax
import jax.numpy as jnp
import ml_dtypes
import numpy as np
from jax import lax
from jax.experimental import pallas as pl
from jax.experimental.pallas import tpu as pltpu
from jax.sharding import PartitionSpec as P

NXW = 4096
NYW = 2048
LANES = 128
CX = 16
CY = 16
CZ = 128
NX = 512
NY = 256
ZONE = 2

TIME_STEP = 0.2
VISCOSITY = 0.6
DEPTH_RATE = 3.0


def stage_tables(peers):
    copies = LANES // peers
    length = peers * LANES
    outer = np.arange(peers)
    inner = np.arange(LANES)
    eye = np.eye(copies)
    angle_a = 2.0 * np.pi / peers * (outer[:, None] * outer[None, :] % peers)
    angle_t = 2.0 * np.pi / length * (outer[:, None] * inner[None, :] % length)
    angle_b = 2.0 * np.pi / LANES * (inner[:, None] * inner[None, :] % LANES)
    cos_a, sin_a = np.kron(np.cos(angle_a), eye), np.kron(np.sin(angle_a), eye)
    cos_b, sin_b = np.cos(angle_b), np.sin(angle_b)
    tables = {
        "fa": np.concatenate([cos_a, -sin_a], axis=0),
        "cos_t": np.repeat(np.cos(angle_t), copies, axis=0),
        "sin_t": np.repeat(np.sin(angle_t), copies, axis=0),
        "fb": np.concatenate([cos_b + sin_b, sin_b - cos_b], axis=0),
        "ib": np.concatenate([cos_b, -sin_b], axis=1),
        "ia": np.concatenate([cos_a + sin_a, sin_a - cos_a], axis=1),
    }
    return tables


TAB_Y = stage_tables(16)
TAB_X = stage_tables(32)


def pair_inverse_b(ib):
    rows = ib.reshape(32, 4, 2 * LANES)
    big = np.zeros((32, 2, 4, 2, 2 * LANES))
    for field in range(2):
        big[:, field, :, field, :] = rows
    return big.reshape(2 * LANES, 4 * LANES)


def pair_inverse_a(ia):
    rows = ia.reshape(32, 4, 2 * LANES)
    big = np.zeros((32, 2, 4, 2, 2 * LANES))
    for field in range(2):
        big[:, field, :, field, :] = rows
    return big.reshape(2 * LANES, 4 * LANES)


Y_IB_PAIR = pair_inverse_b(TAB_Y["ib"])
X_IA_PAIR = pair_inverse_a(TAB_X["ia"])


def f32(array):
    return jnp.asarray(np.asarray(array, np.float32))


def halves_of(table):
    high = table.astype(ml_dtypes.bfloat16)
    return high, (table - high.astype(np.float64)).astype(ml_dtypes.bfloat16)


def left_table(table):
    high, low = halves_of(table)
    return jnp.asarray(np.concatenate([high, high, low], axis=1))


def right_table(table):
    high, low = halves_of(table)
    return jnp.asarray(np.concatenate([high, low, high], axis=0))


def halves(values):
    high = values.astype(jnp.bfloat16)
    return high, (values - high.astype(jnp.float32)).astype(jnp.bfloat16)


def from_left(table, values):
    high, low = halves(values)
    stacked = jnp.concatenate([high, low, high], axis=0)
    return jnp.dot(table, stacked, preferred_element_type=jnp.float32)


def from_right(values, table):
    high, low = halves(values)
    joined = jnp.concatenate([high, high, low], axis=1)
    return jnp.dot(joined, table, preferred_element_type=jnp.float32)


INDEX_X = np.arange(LANES)[:, None] // 4 + 32 * np.arange(LANES)[None, :]
WAVE_X = np.float32(2.0 * math.pi / NXW) * np.minimum(INDEX_X, NXW - INDEX_X).astype(np.float32)
TURNS_X = np.concatenate([TAB_X["cos_t"], TAB_X["sin_t"], WAVE_X])


def twiddle(real, imag, cos_t, sin_t):
    return real * cos_t + imag * sin_t, imag * cos_t - real * sin_t


def forward(block, fa, cos_t, sin_t, fb):
    outer = from_left(fa, block)
    real, imag = twiddle(outer[:LANES], outer[LANES:], cos_t, sin_t)
    return from_right(jnp.concatenate([real, imag], axis=1), fb)


def run(body, outs, *args, room=8, scratch=()):
    shapes = [jax.ShapeDtypeStruct(shape, jnp.float32) for shape in outs]

    def kernel(*refs):
        inputs, rest = refs[: len(args)], refs[len(args) :]
        results = body(*inputs, *rest[len(outs) :])
        for ref, result in zip(rest[: len(outs)], results, strict=True):
            for index, piece in result if isinstance(result, list) else [(..., result)]:
                ref[index] = piece.reshape(ref.shape) if index is ... else piece

    params = pltpu.CompilerParams(vmem_limit_bytes=room << 20) if room else None
    call = pl.pallas_call(
        kernel,
        out_shape=shapes,
        scratch_shapes=[pltpu.VMEM(shape, jnp.float32) for shape in scratch],
        compiler_params=params,
    )
    return call(*args)


def loaded(body):
    return lambda *refs: body(*[ref[...] for ref in refs])


def turn_inputs(eta, potential):
    eta_t = eta.T.reshape(16, 8, LANES)
    potential_t = potential.T.reshape(16, 8, LANES)
    return (jnp.concatenate([eta_t, potential_t], axis=1),)


def turn(block):
    return (block.reshape(-1, LANES).T,)


def turn_fields(block):
    return (block[:, 0:8].reshape(-1, LANES).T,)


def first_y(both, fa, turns, fb):
    eta = both[:, :8].reshape(LANES, LANES)
    potential = both[:, 8:].reshape(LANES, LANES)
    return forward(potential, fa, turns[:LANES], turns[LANES:], fb), eta


def magnitude(place, wave_x):
    line = lax.broadcasted_iota(jnp.int32, (LANES, LANES), 0) & 3
    wave_y = wavenumber(place[1:2, :] + 64 * place[0:1, :] + 16 * line, NYW)
    return jnp.sqrt(wave_x * wave_x + wave_y * wave_y)


def x_stage(powers, extra=None):
    def multiply(spec, kappa, power):
        factor = kappa
        for _ in range(power - 1):
            factor = factor * kappa
        return spec * (factor * (1.0 / (NXW * NYW)))

    def body(block, turns, fa, fb, ib, ia_pair, *more):
        cos_t, sin_t, kappa = [turns[i * LANES : (i + 1) * LANES] for i in range(3)]
        older, inputs = (more[:-2], more[-2:]) if extra else (more, ())
        spec = forward(block.reshape(LANES, LANES), fa, cos_t, sin_t, fb)
        other = older[0] if older else spec
        pair = jnp.concatenate(
            [multiply(spec, kappa, powers[0]), multiply(other, kappa, powers[1])], axis=0
        )
        inner = from_right(pair, ib)
        parts = []
        for field in range(2):
            rows = inner[field * LANES : (field + 1) * LANES]
            parts += twiddle(rows[:, :LANES], rows[:, LANES:], cos_t, sin_t)
        back = from_left(ia_pair, jnp.concatenate(parts, axis=0))
        if not extra:
            return (back,)
        every = slice(None)
        pieces = [((every, slice(0, 8)), back.reshape(32, 8, LANES))]
        pieces += [((peer, slice(8, 16)), tile) for peer, tile in extra(*inputs)]
        return pieces, spec

    return body


def halo_tiles(velocity, flat):
    edges = roll(flat, CY, 1)[:, :LANES]
    side = lax.shift_right_logical(lax.broadcasted_iota(jnp.int32, edges.shape, 1), 4)
    for start, first in ((0, CX - 2), (1, 0)):
        for tile in range(12):
            c, layer, half = tile // 4, tile // 2 % 2, tile % 2
            yield 16 * start + tile, velocity[c, first + layer, 8 * half : 8 * half + 8]
        yield 16 * start + 12, jnp.where(side == start, edges, 0.0)
        for tile in range(13, 16):
            yield 16 * start + tile, jnp.zeros((8, LANES), jnp.float32)


def forward_tiles(relay, place):
    nothing = jnp.zeros((8, LANES), jnp.float32)
    for slab in range(32):
        below = relay[slab - 1, 8:16] if slab > 0 else nothing
        above = relay[slab + 1, 8:16] if slab < 31 else nothing
        yield slab, jnp.where(place[0:1, :] < 16, below, above)


def back_y(block, cos_t, sin_t, ib_pair, ia):
    inner = from_right(block.reshape(LANES, 2 * LANES), ib_pair)
    reals, imags = [], []
    for field in range(2):
        part = inner[:, 2 * field * LANES : 2 * (field + 1) * LANES]
        real, imag = twiddle(part[:, :LANES], part[:, LANES:], cos_t, sin_t)
        reals.append(real)
        imags.append(imag)
    stacked = jnp.concatenate(
        [jnp.concatenate(reals, axis=1), jnp.concatenate(imags, axis=1)], axis=0
    )
    fields = from_left(ia, stacked)
    return fields[:, :LANES], fields[:, LANES:]


def second_y(block, eta, fa, turns, fb, ib_pair, ia):
    cos_t, sin_t = turns[:LANES], turns[LANES:]
    slope_one, cubic_one = back_y(block, cos_t, sin_t, ib_pair, ia)
    spectrum = forward(-eta * slope_one, fa, cos_t, sin_t, fb)
    return spectrum, slope_one, cubic_one


def third_y(block, eta, fa, turns, fb, ib_pair, ia):
    cos_t, sin_t = turns[:LANES], turns[LANES:]
    slope_two, curve_one = back_y(block, cos_t, sin_t, ib_pair, ia)
    potential_three = -eta * slope_two - 0.5 * eta * eta * curve_one
    return forward(potential_three, fa, cos_t, sin_t, fb), slope_two, curve_one


def last_y(block, eta, slope_one, cubic_one, slope_two, curve_one, turns, ib_pair, ia):
    cos_t, sin_t = turns[:LANES], turns[LANES:]
    slope_three, curve_two = back_y(block, cos_t, sin_t, ib_pair, ia)
    vertical = (
        slope_one
        + slope_two
        + eta * curve_one
        + slope_three
        + eta * curve_two
        + 0.5 * eta * eta * cubic_one
    )
    return (vertical,)


def swap(values, axis):
    return lax.all_to_all(values, axis, 0, 0, tiled=True)


def beside(values, axis, work, *inputs):
    values, inputs = lax.optimization_barrier((values, inputs))
    moved = swap(values, axis)
    return lax.optimization_barrier((moved, work(*inputs)))


def wave_surface(surface_eta, surface_potential, velocity, place, work, inputs):
    square = (LANES, LANES)
    turns_y = [f32(np.concatenate([TAB_Y["cos_t"], TAB_Y["sin_t"]]))]
    fwd_y = [left_table(TAB_Y["fa"]), *turns_y, right_table(TAB_Y["fb"])]
    inv_y = [right_table(Y_IB_PAIR), left_table(TAB_Y["ia"])]

    def to_slab(block):
        (turned,) = run(loaded(turn), [square], swap(block.reshape(16, 8, LANES), "pencil"))
        return turned.reshape(32, 4, LANES)

    def to_pencil(block):
        (turned,) = run(turn_fields, [(LANES, 2 * LANES)], block)
        return swap(turned.reshape(16, 8, 2 * LANES), "pencil")

    pair, wide = (32, 8, LANES), (32, 16, LANES)
    (turned,) = run(
        loaded(turn_inputs), [(16, 16, LANES)], surface_eta, surface_potential, room=None
    )
    both, (turns_x, *given) = beside(turned, "pencil", work, *inputs)
    spectrum, eta = run(loaded(first_y), [square, square], both, *fwd_y)
    tab_x = [
        turns_x,
        left_table(TAB_X["fa"]),
        right_table(TAB_X["fb"]),
        right_table(TAB_X["ib"]),
        left_table(X_IA_PAIR),
    ]
    block = swap(to_slab(spectrum), "slab")
    stage = x_stage((1, 3), halo_tiles)
    block, spec_one = run(
        loaded(stage), [wide, square], block.reshape(square), *tab_x, velocity, given[0]
    )
    relay = swap(block, "slab")
    spectrum, slope_one, cubic_one = run(
        loaded(second_y), [square] * 3, to_pencil(relay), eta, *fwd_y, *inv_y
    )
    block = swap(to_slab(spectrum), "slab").reshape(square)
    stage = x_stage((1, 2), forward_tiles)
    block, spec_two = run(loaded(stage), [wide, square], block, *tab_x, spec_one, relay, place)
    halo = swap(block, "slab")
    spectrum, slope_two, curve_one = run(
        loaded(third_y), [square] * 3, to_pencil(halo), eta, *fwd_y, *inv_y
    )
    block = swap(to_slab(spectrum), "slab").reshape(square)
    (block,) = run(loaded(x_stage((1, 2))), [pair], block, *tab_x, spec_two)
    (vertical,) = run(
        loaded(last_y),
        [(16, 8, LANES)],
        to_pencil(swap(block, "slab")),
        eta,
        slope_one,
        cubic_one,
        slope_two,
        curve_one,
        *turns_y,
        *inv_y,
    )
    return swap(vertical, "pencil").reshape(square), halo, given


def wavenumber(index, length):
    folded = jnp.minimum(index, length - index)
    return 2.0 * math.pi / length * folded.astype(jnp.float32)


def ramp_weight(distance, reach_len):
    ratio = jnp.clip(1.0 - distance / reach_len, 0.0, 1.0)
    return ratio * ratio


def relax_of(cell_x, cell_y):
    pos_x, pos_y = cell_x.astype(jnp.float32), cell_y.astype(jnp.float32)
    reach_x = float(ZONE * CX)
    reach_y = float(CY)
    along_x = jnp.maximum(ramp_weight(pos_x, reach_x), ramp_weight(NX - 1.0 - pos_x, reach_x))
    across = jnp.maximum(ramp_weight(pos_y, reach_y), ramp_weight(NY - 1.0 - pos_y, reach_y))
    in_x = jnp.where((cell_x >= 0) & (cell_x < NX), 1.0, 0.0)
    in_y = jnp.where((cell_y >= 0) & (cell_y < NY), 1.0, 0.0)
    return jnp.maximum(along_x, across), in_x * in_y


def parts_of(values):
    terms = []
    for _ in range(2):
        term = values.astype(jnp.bfloat16)
        terms.append(term)
        values = values - term.astype(jnp.float32)
    return jnp.concatenate(terms, axis=1)


def chosen(terms, lanes):
    count, parts = lanes.shape[1], terms.shape[1] // LANES
    iota = lax.broadcasted_iota(jnp.int32, (LANES, count), 0)
    hot = jnp.where(iota == lanes, 1.0, 0.0).astype(jnp.bfloat16)
    picked = jnp.dot(
        terms, jnp.concatenate([hot] * parts, axis=0), preferred_element_type=jnp.float32
    )
    return picked, lax.broadcasted_iota(jnp.int32, picked.shape, 0)


def listed(columns, points, row_count):
    terms = parts_of(columns)
    rows = []
    for i in range(row_count):
        point = points[i : i + 1, :]
        picked, iota = chosen(terms, lax.shift_right_arithmetic(point, 7))
        found = jnp.where(iota == (point & (LANES - 1)), picked, 0.0)
        rows.append(jnp.sum(found, axis=0, keepdims=True))
    return rows


POINT_ROWS = 11


def pick_elevation(eta, points, place, turns):
    rows = listed(eta[...].T, points, POINT_ROWS)
    pieces = [(slice(i, i + 1), row) for i, row in enumerate(rows)]
    first = slice(0, 2 * LANES)
    kappa = magnitude(place, turns[2 * LANES : 3 * LANES])
    return pieces, [(first, turns[first]), (slice(2 * LANES, 3 * LANES), kappa)]


def pick_vertical(columns, points, eta_rows):
    columns = columns[...]
    rows = listed(columns, points, POINT_ROWS)
    pieces = [((slice(None), slice(None)), jnp.zeros((3 * LANES, LANES), jnp.float32))]

    def put(slab, place, row, half):
        at = slice(half * LANES, (half + 1) * LANES)
        for field, value in enumerate((eta_rows[row : row + 1, at], rows[row][:, at])):
            for block in range(3):
                line = 12 * (slab + 1 - block) + 4 * block + 2 * place + field
                if 0 <= line < 3 * LANES:
                    pieces.append(((slice(line, line + 1), slice(None)), value))

    for row, slab in enumerate((0, 1, 30, 31)):
        for half in range(2):
            put(slab, half, row, half)
    for slab in range(2, 30):
        put(slab, 0, 4 + (slab - 2) // 4, (slab - 2) % 4 // 2)
    return pieces, columns.T


def slots_of(stencil, slab, block):
    source, slot = lax.shift_right_logical(stencil, 8), stencil & 255
    in_zone = jnp.where((slab < ZONE) | (slab >= 32 - ZONE), 1, 0)
    lines = 12 * source + 4 * block + 2 * in_zone * lax.shift_right_logical(slot, 7)
    lanes = in_zone * (slot & 127) + (1 - in_zone) * ((slot & 63) + 64 * (slab & 1))
    return lines, lanes


def both_fields(terms, lines, lanes, shares):
    picked, iota = chosen(terms, lanes)
    picked = picked * shares
    return [jnp.where(iota == lines + field, picked, 0.0) for field in range(2)]


def summed(values):
    return jnp.sum(values, axis=0, keepdims=True)


def over_q(values):
    values = values + roll(values, 64, 1)
    return values + roll(values, 32, 1)


def sample(arrived, place, flat, halo, velocity):
    slab = jnp.concatenate([place[0:1, :]] * 2, axis=1)
    terms = parts_of(arrived[...])
    flat = flat[...]
    lines, lanes = slots_of(flat[0:4].astype(jnp.int32), slab, 1)
    weights = flat[4:8]
    shares = weights / jnp.sum(weights, axis=0, keepdims=True)
    totals = [0.0, 0.0]
    for q in range(4):
        at = slice(q, q + 1)
        found = both_fields(terms, lines[at], lanes[at], shares[at])
        totals = [total + part for total, part in zip(totals, found, strict=True)]
    rows = [summed(total) for total in totals]

    lane = lax.broadcasted_iota(jnp.int32, (8, LANES), 1)
    side = lax.shift_right_logical(lane, 4) & 1
    beside_x = halo[12, 8:16] + halo[28, 8:16]
    points, weight = in_lanes(beside_x, lane, 0), in_lanes(beside_x, lane, 4)
    lines, lanes = slots_of(points.astype(jnp.int32), place[0:1, :] - 1 + 2 * side, 2 * side)
    total = over_q(weight)
    shares = weight / jnp.where(total > 0.0, total, 1.0)
    for part in both_fields(terms, lines[0:1], lanes[0:1], shares[0:1]):
        value = over_q(jnp.broadcast_to(summed(part), (8, LANES)))[0:1]
        rows.append(jnp.concatenate([value, value], axis=1))

    sent = []
    for y_at in (CY - 2, 0):
        pieces = []
        for c in range(3):
            line = 20 * c
            for x in range(2):
                tile = 4 * c + 2 * x + y_at // 8
                at = slice(8 + y_at % 8, 10 + y_at % 8)
                pieces.append((line + x, halo[tile, at]))
                pieces.append((line + 18 + x, halo[16 + tile, at]))
            pieces.append((slice(line + 2, line + 18), velocity[c, :, y_at : y_at + 2]))
        for field in range(2):
            for half in range(2):
                at = (60 + field, slice(half, half + 1))
                pieces.append((at, rows[field][:, half * LANES : (half + 1) * LANES]))
        sent.append(pieces)
    here = jnp.concatenate(rows + [jnp.zeros((4, 256), jnp.float32)], axis=0)
    even = (place[1:2, :] & 1) == 0
    swaps = [[], []]
    for (at, up), (_, down) in zip(*sent, strict=True):
        swaps[0].append((at, jnp.where(even, up, down)))
        swaps[1].append((at, jnp.where(even, down, up)))
    return here, *swaps


def in_lanes(values, lane, first):
    result = jnp.zeros(values.shape, jnp.float32)
    for q in range(4):
        moved = jnp.broadcast_to(values[first + q : first + q + 1], values.shape)
        if q:
            moved = roll(moved, 32 * q, 1)
        result = jnp.where(lax.shift_right_logical(lane, 5) == q, moved, result)
    return result


def roll(values, shift, axis):
    return pltpu.roll(values, shift, axis)


def predicted_of(centers, neighbours):
    lane = lax.broadcasted_iota(jnp.int32, centers[0].shape, centers[0].ndim - 1)
    last = centers[0].ndim - 1
    results = []
    for center, (plus_x, minus_x, plus_y, minus_y) in zip(centers, neighbours, strict=True):
        plus_z = jnp.where(lane == CZ - 1, 0.0, roll(center, CZ - 1, last))
        minus_z = jnp.where(lane == 0, 0.0, roll(center, 1, last))
        laplace = plus_x + minus_x + (plus_y + minus_y) + (plus_z + minus_z) - 6.0 * center
        advect = (
            centers[0] * (plus_x - minus_x)
            + centers[1] * (plus_y - minus_y)
            + centers[2] * (plus_z - minus_z)
        )
        results.append(center + TIME_STEP * (VISCOSITY * laplace - 0.5 * advect))
    return results


def surface_columns(here, low, high):
    def lines_of(values):
        lines = [
            jnp.concatenate([values[field, half : half + 1] for half in range(2)], axis=1)
            for field in range(2)
        ]
        return jnp.concatenate(lines + [jnp.zeros((6, 256), jnp.float32)], axis=0)

    lane = lax.broadcasted_iota(jnp.int32, (8, 256), 1)
    below, above = roll(lines_of(low), 241, 1), roll(lines_of(high), 15, 1)
    across_y = jnp.where(lane % CY == 0, below, above)
    surface = jnp.concatenate([here[...], across_y], axis=0).T
    return lambda index: surface[:, index : index + 1].reshape(CX, CY, 1)


def both_substeps(velocity, halo, near, far, here, place, decay, padded):
    even = (place[1:2, :] & 1) == 0

    def from_low(at):
        return jnp.where(even, far[at], near[at])

    def from_high(at):
        return jnp.where(even, near[at], far[at])

    for c in range(3):
        padded[c, 2:18, 8:24] = velocity[c]
        for tile in range(4):
            layer, half = tile // 2, tile % 2
            at = slice(8 + 8 * half, 16 + 8 * half)
            padded[c, layer, at] = halo[4 * c + tile, 8:16]
            padded[c, 18 + layer, at] = halo[16 + 4 * c + tile, 8:16]
        lines = slice(20 * c, 20 * c + 20)
        padded[c, :, 6:8] = from_low(lines)
        padded[c, :, 24:26] = from_high(lines)
    lines = slice(60, 62)
    column = surface_columns(here, from_low(lines), from_high(lines))
    (keep, keep_x, keep_y), (pull, pull_x, pull_y) = relax_fields(place, decay[...])

    def region(x_at, x_to, y_at, y_to):
        def part(c, shift_x, shift_y):
            return padded[c, x_at + shift_x : x_to + shift_x, y_at + shift_y : y_to + shift_y]

        steps = ((1, 0), (-1, 0), (0, 1), (0, -1))
        centers = [part(c, 0, 0) for c in range(3)]
        return predicted_of(centers, [[part(c, *step) for step in steps] for c in range(3)])

    own = region(2, 18, 8, 24)
    sides_x = [region(1, 2, 8, 24), region(18, 19, 8, 24)]
    sides_y = [region(2, 18, 7, 8), region(2, 18, 24, 25)]

    shape = (CX, CY, CZ)
    row = lax.broadcasted_iota(jnp.int32, shape, 1)
    centers, neighbours, targets = [], [], []
    for c in range(3):
        center = own[c] * keep
        outer_x = [sides_x[side][c] * keep_x[side : side + 1] for side in range(2)]
        low, high = [jnp.broadcast_to(side[c], shape) for side in sides_y]
        outer_y = jnp.where(row == 0, low, high) * keep_y
        target = None
        if c != 1:
            field = c // 2
            target = pull * column(field)
            center = center + target
            line = column(2 + field)
            outer_x = [
                outer_x[0] + pull_x[0:1] * line[0:1],
                outer_x[1] + pull_x[1:2] * line[CX - 1 : CX],
            ]
            outer_y = outer_y + pull_y * column(8 + field)
        plus_x = jnp.concatenate([center[1:], outer_x[1]], axis=0)
        minus_x = jnp.concatenate([outer_x[0], center[:-1]], axis=0)
        plus_y = jnp.where(row == CY - 1, outer_y, roll(center, CY - 1, 1))
        minus_y = jnp.where(row == 0, outer_y, roll(center, 1, 1))
        centers.append(center)
        neighbours.append((plus_x, minus_x, plus_y, minus_y))
        targets.append(target)
    pieces = []
    for c, value in enumerate(predicted_of(centers, neighbours)):
        value = value * keep
        pieces.append((c, value if targets[c] is None else value + targets[c]))
    return (pieces,)


def swapped(values, axis, first):
    pairs = [(i, i + 1) for i in range(first, lax.axis_size(axis) - 1, 2)]
    return lax.ppermute(values, axis, pairs + [(j, i) for i, j in pairs])


def list_points(send_point, send_count):
    slot = lax.broadcasted_iota(jnp.int32, (32, 256), 1)
    points = jnp.where(slot < send_count[0, 0][:, None], send_point[0, 0], -1)
    inner = points[2:30, :64].reshape(7, 256)
    return jnp.concatenate([points[:2], points[30:], inner], axis=0)


DECAY = np.exp(-DEPTH_RATE * (CZ - 1.0 - np.arange(CZ)) / CZ).astype(np.float32)


def relax_fields(place, decay):
    def fields(cell_x, cell_y):
        relax, inside = relax_of(cell_x, cell_y)
        return (1.0 - relax) * inside, relax * inside * decay.reshape(1, 1, CZ)

    side = lax.broadcasted_iota(jnp.int32, (2, 1, CZ), 0)
    row = lax.broadcasted_iota(jnp.int32, (1, CY, CZ), 1)
    slab, pencil = place[0:1, :].reshape(1, 1, CZ), place[1:2, :].reshape(1, 1, CZ)
    cell_x = slab * CX + lax.broadcasted_iota(jnp.int32, (CX, 1, CZ), 0)
    cell_y = pencil * CY + row
    out_x = slab * CX - 1 + (CX + 1) * side
    out_y = cell_y + jnp.where(row == 0, -1, jnp.where(row == CY - 1, 1, 0))
    own, across_x, across_y = fields(cell_x, cell_y), fields(out_x, cell_y), fields(cell_x, out_y)
    return (own[0], across_x[0], across_y[0]), (own[1], across_x[1], across_y[1])


def flat_stencil(stencil, interp_weight):
    rows = [stencil.astype(jnp.float32), interp_weight]
    return jnp.concatenate(rows, axis=0).reshape(8, CX * CY)


def on_device(
    surface_eta, surface_potential, velocity, send_point, send_count, stencil, interp_weight
):
    line = lax.broadcasted_iota(jnp.int32, (8, LANES), 0)
    place = jnp.where(line == 0, lax.axis_index("slab"), lax.axis_index("pencil"))
    surface_eta, place = lax.optimization_barrier((surface_eta, place))
    square = (LANES, LANES)

    def lists(eta, place, send_point, send_count, stencil, interp_weight):
        points = list_points(send_point, send_count)
        shapes = [(POINT_ROWS, 256), TURNS_X.shape]
        rows, turns_x = run(pick_elevation, shapes, eta, points, place, f32(TURNS_X))
        return turns_x, flat_stencil(stencil, interp_weight), points, rows

    columns, halo, (flat, points, eta_rows) = wave_surface(
        surface_eta,
        surface_potential,
        velocity,
        place,
        lists,
        (surface_eta, place, send_point, send_count, stencil, interp_weight),
    )
    outgoing, vertical = run(
        pick_vertical, [(3 * LANES, LANES), square], columns, points, eta_rows
    )
    arrived = swap(outgoing.reshape(32, 3, 4, LANES), "slab").reshape(3 * LANES, LANES)
    sent = (62, 2, LANES)
    here, near, far = run(
        sample, [(8, 256), sent, sent], arrived, place, flat, halo, velocity
    )
    far = swapped(far, "pencil", 1)
    near = swapped(near, "pencil", 0)
    (velocity,) = run(
        both_substeps,
        [(3, CX, CY, CZ)],
        velocity,
        halo,
        near,
        far,
        here,
        place,
        jnp.asarray(DECAY[None]),
        scratch=[(3, 20, 32, CZ)],
    )
    return (vertical, velocity)


def solution(mesh):
    in_specs = (
        P("pencil", "slab"),
        P("pencil", "slab"),
        P(None, "slab", "pencil", None),
        P("slab", "pencil", None, None),
        P("slab", "pencil", None),
        P(None, "slab", "pencil"),
        P(None, "slab", "pencil"),
    )
    out_specs = (P("pencil", "slab"), P(None, "slab", "pencil", None))
    return jax.shard_map(
        on_device, mesh=mesh, in_specs=in_specs, out_specs=out_specs, check_vma=False
    )
```
